128 devices in a mesh: gx: 8 (over y, core), gy: 16 (over z, x).
Axes of the slice: x: 4, y: 4, z: 4, core: 2. Of those that a mesh axis runs over, the one named last changes fastest.
Arguments:
- density: float32 [32, 2048, 4096], P(None, 'gx', 'gy'), may hold values from -6 to 6
- spacing_x: float32 [2048], replicated, may hold values from 0.5 to 2
- spacing_y: float32 [4096], replicated, may hold values from 0.5 to 2
Outputs:
- detail: float32 [32, 2048, 4096], P(None, 'gx', 'gy')
- coarse_new: float32 [32, 1024, 2048], P(None, 'gx', 'gy')
The draws below stay inside these ranges and needn't reach their ends.
All inputs are finite; a program needn't handle non-finite values.
Results may differ from the reference program's by a relative error of at most 0.0003.
Values sent between devices are 32-bit elements; how exact they have to be, the bound alone decides.
A program may use at most 192 MiB of HBM per device.

```python
import math
import jax
import jax.numpy as jnp
from jax import lax

Z = 32
NX = 2048
NY = 4096


def steps_of(own_key, shape, shards, least, high):
    loudness = 1.0
    for dim, blocks in shards:
        draws = jax.random.uniform(jax.random.fold_in(jax.random.fold_in(own_key, 6), dim), (blocks,), jnp.float32, least / len(shards), high / len(shards))
        loudness = loudness * jnp.repeat(jnp.exp(draws), shape[dim] // blocks).reshape((-1,) + (1,) * (len(shape) - 1 - dim))
    return loudness


def bell_draw(stream_key, dims, spread, most, shards=(), kind=jnp.bfloat16):
    result = spread * jax.random.normal(stream_key, dims, jnp.float32)
    if shards:
        result = result * steps_of(stream_key, dims, shards, -0.22, 0.18)
    return jnp.clip(result, -most, most).astype(kind)


def setup_inputs(seed: int = 0) -> dict:
    arg_keys = jax.random.split(jax.random.key(seed), 4)
    density = bell_draw(arg_keys[0], (Z, NX, NY), 1.0, 6.0, ((1, 8), (2, 16)), jnp.float32)
    spacing_x = jnp.clip(jnp.exp(jax.random.uniform(arg_keys[1], (NX,), jnp.float32, math.log(0.5), math.log(2.0))), 0.5, 2.0)
    spacing_y = jnp.clip(jnp.exp(jax.random.uniform(arg_keys[2], (NY,), jnp.float32, math.log(0.5), math.log(2.0))), 0.5, 2.0)
    return {"density": density, "spacing_x": spacing_x, "spacing_y": spacing_y}


stiffness_weight = 4096.0
operator_divisor = 32.0

def edge_tables(spacing, offset, cells):
    extent = spacing.shape[0]
    window = cells + 4
    ones_pad = jnp.ones((8,), spacing.dtype)
    zeros_pad = jnp.zeros((8,), spacing.dtype)
    interp_pad = jnp.concatenate([ones_pad, spacing, ones_pad])
    mass_pad = jnp.concatenate([zeros_pad, spacing, ones_pad])
    right_interp = lax.dynamic_slice_in_dim(interp_pad, offset + 6, window)
    left_interp = lax.dynamic_slice_in_dim(interp_pad, offset + 5, window)
    right_mass = lax.dynamic_slice_in_dim(mass_pad, offset + 6, window)
    left_mass = lax.dynamic_slice_in_dim(mass_pad, offset + 5, window)
    position = offset - 2 + jnp.arange(window, dtype=jnp.int32)
    odd_flag = (position % 2).astype(spacing.dtype)
    inside = ((position >= 0) & (position < extent)).astype(spacing.dtype)
    interval = left_interp + right_interp
    left_weight = right_interp / interval
    right_weight = left_interp / interval
    return (odd_flag, inside, left_weight, right_weight, left_mass / 6.0, (left_mass + right_mass) / 3.0, right_mass / 6.0)

def oriented(coef, dim_index, array_rank):
    if dim_index == array_rank - 2:
        return coef[:, None]
    return coef

def neighbours(values, dim_index):
    widths = [(0, 0)] * values.ndim
    widths[dim_index] = (1, 1)
    padded = jnp.pad(values, widths)
    length = values.shape[dim_index]
    return (lax.slice_in_dim(padded, 0, length, axis=dim_index), lax.slice_in_dim(padded, 2, length + 2, axis=dim_index))

def interpolate(values, tables, dim_index):
    array_rank = values.ndim
    below_cells, above_cells = neighbours(values, dim_index)
    odd_part = oriented(tables[0], dim_index, array_rank)
    guess = oriented(tables[2], dim_index, array_rank) * below_cells + oriented(tables[3], dim_index, array_rank) * above_cells
    return odd_part * guess + (1.0 - odd_part) * values

def apply_mass(values, tables, dim_index):
    array_rank = values.ndim
    below_cells, above_cells = neighbours(values, dim_index)
    return oriented(tables[4], dim_index, array_rank) * below_cells + oriented(tables[5], dim_index, array_rank) * values + oriented(tables[6], dim_index, array_rank) * above_cells

def restrict(values, tables, dim_index, cells):
    array_rank = values.ndim
    center = lax.slice_in_dim(values, 2, cells + 2, 2, dim_index)
    before = lax.slice_in_dim(values, 1, cells + 1, 2, dim_index)
    after_cells = lax.slice_in_dim(values, 3, cells + 3, 2, dim_index)
    from_before = lax.slice_in_dim(tables[3], 1, cells + 1, 2, 0)
    from_after = lax.slice_in_dim(tables[2], 3, cells + 3, 2, 0)
    return center + oriented(from_before, dim_index, array_rank) * before + oriented(from_after, dim_index, array_rank) * after_cells

def decompose(extended, tables_x, tables_y, count_x, count_y):
    array_rank = extended.ndim
    axis_x = array_rank - 2
    axis_y = array_rank - 1
    along_x = interpolate(extended, tables_x, axis_x)
    smooth = interpolate(along_x, tables_y, axis_y)
    detail_ext = (extended - smooth) * oriented(tables_x[1], axis_x, array_rank) * tables_y[1]
    load_x = restrict(apply_mass(detail_ext, tables_x, axis_x), tables_x, axis_x, count_x)
    load_term = restrict(apply_mass(load_x, tables_y, axis_y), tables_y, axis_y, count_y)
    coarse = extended[..., 2:count_x + 2:2, 2:count_y + 2:2]
    detail = detail_ext[..., 2:count_x + 2, 2:count_y + 2]
    return (detail, coarse, load_term)

def coarse_operator(spacing):
    coarse_span = spacing[0::2] + spacing[1::2]
    zeros_one = jnp.zeros((1,), spacing.dtype)
    previous = jnp.concatenate([zeros_one, coarse_span[:-1]])
    inverse_span = 1.0 / coarse_span
    previous_inverse = jnp.concatenate([zeros_one, inverse_span[:-1]])
    diagonal = ((previous + coarse_span) / 3.0 + stiffness_weight * (previous_inverse + inverse_span)) / operator_divisor
    coupling = (coarse_span[:-1] / 6.0 - stiffness_weight * inverse_span[:-1]) / operator_divisor
    return (diagonal, coupling)

def reference(density, spacing_x, spacing_y):
    count_x = spacing_x.shape[0]
    count_y = spacing_y.shape[0]
    tables_x = edge_tables(spacing_x, 0, count_x)
    tables_y = edge_tables(spacing_y, 0, count_y)
    diag_x, coup_x = coarse_operator(spacing_x)
    diag_y, coup_y = coarse_operator(spacing_y)
    zeros_one = jnp.zeros((1,), density.dtype)
    lower_x = jnp.concatenate([zeros_one, coup_x])
    upper_x = jnp.concatenate([coup_x, zeros_one])
    lower_y = jnp.concatenate([zeros_one, coup_y])
    upper_y = jnp.concatenate([coup_y, zeros_one])

    def one_plane(sheet):
        extended = jnp.pad(sheet, 2)
        detail, coarse, load_term = decompose(extended, tables_x, tables_y, count_x, count_y)
        corr_x = lax.linalg.tridiagonal_solve(lower_x, diag_x, upper_x, load_term)
        correction = lax.linalg.tridiagonal_solve(lower_y, diag_y, upper_y, corr_x.T).T
        return (detail, coarse + correction)
    detail, coarse_new = lax.map(one_plane, density)
    return (detail, coarse_new)
```

```python
import functools

import jax
import jax.numpy as jnp
from jax import lax
from jax.experimental import pallas as pl
from jax.experimental.pallas import tpu as pltpu
from jax.sharding import PartitionSpec as P

MESH = pl.DeviceIdType.MESH
F32 = jnp.float32
BF16 = jnp.bfloat16
HIGHEST = lax.Precision.HIGHEST
stiffness_weight = 4096.0
operator_divisor = 32.0
LANES = 128
FINE = 256
PLANES = 32
STEP = 4
MIB = 1 << 20
X_WL, X_WR, X_K1, X_K2, X_K3, X_K4, X_K5, X_U, X_PSI, X_W = range(10)
Y_K1, Y_K2, Y_K3, Y_K4, Y_K5, Y_U, Y_W = range(10, 17)
S_FX, S_BX, S_FY, S_BY, S_WRM, S_UY, S_PSIY = range(7)


def split(values):
    high = values.astype(BF16)
    return high, (values - high.astype(F32)).astype(BF16)


def mxu(a, b):
    return jnp.dot(a, b, preferred_element_type=F32)


def iota(shape, dim):
    return lax.broadcasted_iota(jnp.int32, shape, dim)


def column(table, index):
    return jnp.broadcast_to(table[:, index : index + 1], (LANES, LANES))


def shift_up(values, last):
    rolled = pltpu.roll(values, LANES - 1, 0)
    return jnp.where(iota(values.shape, 0) == LANES - 1, last, rolled)


def shift_down(values, first):
    return jnp.where(iota(values.shape, 0) == 0, first, pltpu.roll(values, 1, 0))


def chain_tables(blocks_x, blocks_y, sx, sy, tab, rows_in):
    count = blocks_x + blocks_y
    shape = (count, LANES)
    lane, row = iota(shape, 1), iota(shape, 0)
    first = (lane == 0) & ((row == 0) | (row == blocks_x))

    def prev(values, fill):
        rolled = pltpu.roll(values, 1, 1)
        return jnp.where(first, fill, jnp.where(lane == 0, pltpu.roll(rolled, 1, 0), rolled))

    def following(values):
        rolled = pltpu.roll(values, LANES - 1, 1)
        return jnp.where(lane == LANES - 1, pltpu.roll(rolled, count - 1, 0), rolled)

    def halves(start):
        return jnp.concatenate(
            [sx[pl.ds(start, blocks_x, stride=2), :], sy[pl.ds(start, blocks_y, stride=2), :]], axis=0
        )

    fine = jnp.concatenate([halves(0), halves(1)], axis=1)
    node, place = iota((FINE, FINE), 0), iota((FINE, FINE), 1)
    pick = jnp.where(place < LANES, 2 * place, 2 * (place - LANES) + 1)
    parts = jnp.dot((fine), (node == pick).astype(F32), precision=HIGHEST, preferred_element_type=F32)
    c, d = parts[:, :LANES], parts[:, LANES:]
    span = c + d
    a, b = prev(c, 0.0), prev(d, 0.0)
    span_before = prev(span, 1.0)
    inverse = 1.0 / span
    inverse_before = 1.0 / span_before
    tab[0] = d * inverse
    tab[1] = c * inverse
    tab[2] = a * a * inverse_before * (1.0 / 6.0)
    tab[3] = a * (1.0 / 3.0) + b * (1.0 / 6.0)
    tab[4] = (a * b * inverse_before + c * d * inverse) * (1.0 / 6.0) + (b + c) * (1.0 / 3.0)
    tab[5] = c * (1.0 / 6.0) + d * (1.0 / 3.0)
    tab[6] = d * d * inverse * (1.0 / 6.0)
    tab[9] = b * inverse_before
    tab[10] = a * inverse_before

    rho = 1.0 / (stiffness_weight * inverse - span * (1.0 / 6.0))
    rho_before = prev(rho, 0.0)
    mu = 0.5 * (a + b + span)
    mu_after = following(mu)
    one = jnp.ones(shape, F32)
    fwd = (one + mu * rho_before, mu, rho_before, one)
    bwd = (one, mu_after, rho, one + rho * mu_after)
    step = 1
    while step < LANES:
        def join(m, shift, outside):
            fill = (1.0, 0.0, 0.0, 1.0)
            a1, b1, c1, d1 = m
            a0, b0, c0, d0 = (
                jnp.where(outside, f, pltpu.roll(v, shift, 1)) for v, f in zip(m, fill)
            )
            return (a1 * a0 + b1 * c0, a1 * b0 + b1 * d0, c1 * a0 + d1 * c0, c1 * b0 + d1 * d0)

        fwd = join(fwd, step, lane < step)
        bwd = join(bwd, LANES - step, lane >= LANES - step)
        step *= 2
    ends = [jnp.broadcast_to(v[:, LANES - 1 : LANES], shape) for v in fwd]
    starts = [jnp.broadcast_to(v[:, 0:1], shape) for v in bwd]
    for low, size in ((0, blocks_x), (blocks_x, blocks_y)):
        y = jnp.zeros((1, LANES), F32)
        for q in range(low, low + size):
            rows_in[0, q : q + 1, :] = y
            at, bt, ct, dt = (v[q : q + 1, :] for v in ends)
            y = (at * y + bt) / (ct * y + dt)
        z = None
        for q in reversed(range(low, low + size)):
            at, bt, ct, dt = (v[q : q + 1, :] for v in starts)
            if z is None:
                rows_in[1, q : q + 1, :] = jnp.ones((1, LANES), F32)
                rows_in[2, q : q + 1, :] = jnp.zeros((1, LANES), F32)
                z = at / ct
            else:
                rows_in[1, q : q + 1, :] = z
                rows_in[2, q : q + 1, :] = jnp.ones((1, LANES), F32)
                z = (at * z + bt) / (ct * z + dt)
    y_in, z_num, z_den = rows_in[0], rows_in[1], rows_in[2]
    den = fwd[2] * y_in + fwd[3]
    left = (fwd[0] * y_in + fwd[1]) / den
    right = (bwd[0] * z_num + bwd[1] * z_den) / (bwd[2] * z_num + bwd[3] * z_den)
    green = operator_divisor / (left + right)
    tab[7] = green / den
    tab[8] = den
    tab[11] = 1.0 / jnp.broadcast_to(den[:, LANES - 1 : LANES], shape)
    tab[12] = 1.0 / jnp.broadcast_to(green[:, LANES - 1 : LANES], shape)
    tab[13] = 1.0 / jnp.broadcast_to(den[:, 0:1], shape)


def weights_between(gain, low, size, own, forward, backward):
    q = iota((size, LANES), 0)
    ahead = jnp.ones((size, LANES), F32)
    behind = jnp.ones((size, LANES), F32)
    for m in range(size):
        g = gain[low + m : low + m + 1, :]
        ahead = ahead * jnp.where((m > q) & (m < own), g, 1.0)
        behind = behind * jnp.where((m < q) & (m > own), g, 1.0)
    forward[low : low + size, :] = jnp.where(q < own, ahead, 0.0)
    backward[low : low + size, :] = jnp.where(q > own, behind, 0.0)


def green_block(u_col, w_col, u_row, w_row):
    i, j = iota((LANES, LANES), 0), iota((LANES, LANES), 1)
    return jnp.where(i >= j, u_col * w_row, w_col * u_row)


def prepare_kernel(
    nx, ny, dens, sx, sy,
    colx, ycoef, scal, cf, cb, wcat, gxh, gxl, rh, er, lch, lcl,
    box, rsend, csend, rrecv, cl, cr, tiles, tab, rows_in, stack, wfine, merged, load_sem, send_sem, recv_sem,
):
    p, r = lax.axis_index("gx"), lax.axis_index("gy")
    up, down = lax.rem(p + nx - 1, nx), lax.rem(p + 1, nx)
    left, right = lax.rem(r + ny - 1, ny), lax.rem(r + 1, ny)
    loads = []
    for k in range(PLANES // STEP):
        part = pl.ds(k * STEP, STEP)
        loads.append(pltpu.make_async_copy(dens.at[part], box.at[part], load_sem.at[k]))
        loads[-1].start()
    barrier = pltpu.get_barrier_semaphore()
    for i in (up, p, down):
        for j in (left, r, right):
            if i is p and j is r:
                continue
            pl.semaphore_signal(barrier, inc=1, device_id=(i, j), device_id_type=MESH)

    lane_f = iota((FINE, LANES), 1)
    csend[...] = jnp.zeros((FINE, LANES), F32)
    for k in range(PLANES // STEP):
        loads[k].wait()
        acc = csend[...]
        for zi in range(STEP):
            z = k * STEP + zi
            acc = jnp.where(lane_f == z, box[z, :, FINE - 2 : FINE - 1], acc)
            acc = jnp.where(lane_f == PLANES + z, box[z, :, FINE - 1 : FINE], acc)
            acc = jnp.where(lane_f == 2 * PLANES + z, box[z, :, 0:1], acc)
            rsend[0, z : z + 1, :] = box[z, FINE - 2 : FINE - 1, :]
            rsend[1, z : z + 1, :] = box[z, FINE - 1 : FINE, :]
            rsend[2, z : z + 1, :] = box[z, 0:1, :]
        csend[...] = acc

    pl.semaphore_wait(barrier, 8)
    top, bottom = pl.ds(0, 8), pl.ds(FINE - 8, 8)
    plan = (
        (rsend.at[pl.ds(0, 2)], rrecv.at[pl.ds(0, 2)], down, r),
        (rsend.at[pl.ds(2, 1)], rrecv.at[pl.ds(2, 1)], up, r),
        (csend, cl, p, right),
        (csend, cr, p, left),
        (csend.at[bottom], tiles.at[0], down, r),
        (csend.at[top], tiles.at[1], up, r),
        (csend.at[bottom], tiles.at[2], down, right),
        (csend.at[bottom], tiles.at[3], down, left),
        (csend.at[top], tiles.at[4], up, right),
        (csend.at[top], tiles.at[5], up, left),
    )
    copies = []
    for k, (src, dst, i, j) in enumerate(plan):
        copies.append(
            pltpu.make_async_remote_copy(
                src_ref=src, dst_ref=dst, send_sem=send_sem.at[k], recv_sem=recv_sem.at[k],
                device_id=(i, j), device_id_type=MESH,
            )
        )
        copies[-1].start()

    chain_tables(nx, ny, sx, sy, tab, rows_in)
    weights_between(tab[11], 0, nx, p, cf, cb)
    weights_between(tab[11], nx, ny, r, cf, cb)
    row_x, row_y = pl.ds(p, 1), pl.ds(nx + r, 1)
    ux, wx, uy, wy = tab[7, row_x, :], tab[8, row_x, :], tab[7, row_y, :], tab[8, row_y, :]
    stack[...] = jnp.zeros((LANES, LANES), F32)
    for k in range(7):
        stack[k : k + 1, :] = tab[k, row_x, :]
    stack[X_U : X_U + 1, :] = ux
    stack[X_PSI : X_PSI + 1, :] = wx * tab[11, row_x, :]
    stack[X_W : X_W + 1, :] = wx
    for k in range(5):
        stack[Y_K1 + k : Y_K1 + k + 1, :] = tab[2 + k, row_y, :]
    stack[Y_U : Y_U + 1, :] = uy
    stack[Y_W : Y_W + 1, :] = wy
    cols = stack[...].T
    colx[...] = cols
    scal[...] = jnp.zeros((8, LANES), F32)
    scal[S_FX : S_FX + 1, :] = tab[12, row_x, :]
    scal[S_BX : S_BX + 1, :] = tab[13, row_x, :]
    scal[S_FY : S_FY + 1, :] = tab[12, row_y, :]
    scal[S_BY : S_BY + 1, :] = tab[13, row_y, :]
    wl_x = tab[9, row_x, :][:, 0:1]
    wr_x = tab[10, row_x, :][:, 0:1]
    wl_y = tab[9, row_y, :][:, 0:1]
    wr_y = tab[10, row_y, :][:, 0:1]
    scal[S_WRM : S_WRM + 1, :] = jnp.broadcast_to(wr_x, (1, LANES))
    scal[S_UY : S_UY + 1, :] = uy
    scal[S_PSIY : S_PSIY + 1, :] = wy * tab[11, row_y, :]

    odd_row = (iota((1, LANES), 1) & 1) == 1
    ycoef[...] = jnp.zeros((8, FINE), F32)
    for t in range(2):
        h = sy[pl.ds(2 * r + t, 1), :]
        hp = pltpu.roll(h, 1, 1)
        inv = 1.0 / (h + hp)
        ycoef[0:1, t * LANES : (t + 1) * LANES] = jnp.where(odd_row, h * inv, 0.0)
        ycoef[1:2, t * LANES : (t + 1) * LANES] = jnp.where(odd_row, hp * inv, 0.0)

    hi, lo = split(green_block(column(cols, X_U), column(cols, X_W), ux, wx))
    gxh[...] = hi
    gxl[...] = lo
    gy = green_block(column(cols, Y_U), column(cols, Y_W), uy, wy)
    g1, g2, g3, g4, g5 = (column(cols, Y_K1 + k) * gy for k in range(5))
    wfine[pl.ds(0, LANES, stride=2), :] = g3 + shift_down(g5, 0.0) + shift_up(g1, 0.0)
    wfine[pl.ds(1, LANES, stride=2), :] = g4 + shift_up(g2, 0.0)
    i = iota((LANES, LANES), 0)
    outer = jnp.where(
        i < PLANES, g1[0:1, :],
        jnp.where(i < 2 * PLANES, g2[0:1, :], jnp.where(i < 3 * PLANES, g5[LANES - 1 : LANES, :], 0.0)),
    )
    hi, lo = split(wfine[...])
    wcat[0:FINE, 0:LANES] = hi
    wcat[0:FINE, LANES:FINE] = lo
    hi, lo = split(outer)
    wcat[FINE : FINE + LANES, 0:LANES] = hi
    wcat[FINE : FINE + LANES, LANES:FINE] = lo

    for copy in copies:
        copy.wait()

    has_up = (p > 0).astype(F32)
    has_down = (p < nx - 1).astype(F32)
    has_left = (r > 0).astype(F32)
    has_right = (r < ny - 1).astype(F32)
    lane_8 = iota((8, LANES), 1)
    lane = iota((LANES, LANES), 1)
    merged[...] = jnp.where(lane_f < 2 * PLANES, cl[...] * has_left, cr[...] * has_right)
    e_c, o_c = merged[pl.ds(0, LANES, stride=2), :], merged[pl.ds(1, LANES, stride=2), :]
    own = csend[pl.ds(0, LANES, stride=2), :]
    own_n, own_s = tiles[0] * has_up, tiles[1] * has_down
    north = jnp.where(lane_8 < 2 * PLANES, tiles[2] * has_left, tiles[3] * has_right) * has_up
    south = jnp.where(lane_8 < 2 * PLANES, tiles[4] * has_left, tiles[5] * has_right) * has_down

    def along_y(values, own_values):
        at = iota(values.shape, 1)
        guess = wl_y * pltpu.roll(values, PLANES, 1) + wr_y * pltpu.roll(own_values, LANES - PLANES, 1)
        return jnp.where((at >= PLANES) & (at < 2 * PLANES), guess, values)

    se = along_y(e_c, own)
    se_n = along_y(north, own_n)[6:7, :]
    se_s = along_y(south, own_s)[0:1, :]
    do = o_c - (column(cols, X_WL) * se + column(cols, X_WR) * shift_up(se, se_s))
    de = e_c - se
    de_n = north[6:7, :] - se_n
    do_n = north[7:8, :] - (wl_x * se_n + wr_x * se[0:1, :])
    de_s = south[0:1, :] - se_s
    loads_c = (
        column(cols, X_K1) * shift_down(de, de_n)
        + column(cols, X_K2) * shift_down(do, do_n)
        + column(cols, X_K3) * de
        + column(cols, X_K4) * do
        + column(cols, X_K5) * shift_up(de, de_s)
    )
    hi, lo = split(loads_c)
    lch[...] = hi
    lcl[...] = lo
    er[...] = e_c

    stack[0:8, :] = north
    stack[8:16, :] = south
    corner = stack[...].T
    corner_n = corner[2 * PLANES : 3 * PLANES, 6:7]
    corner_s = corner[2 * PLANES : 3 * PLANES, 8:9]
    lane_z = iota((PLANES, LANES), 1)
    odd = (lane_z & 1) == 1

    def row_along_y(layer, scale, corner_col):
        tiles_in = [layer[:, t * LANES : (t + 1) * LANES] * scale for t in range(2)]
        next_in = [pltpu.roll(v, LANES - 1, 1) for v in tiles_in]
        after = [
            jnp.where(lane_z < LANES - 1, next_in[0], next_in[1]),
            jnp.where(lane_z < LANES - 1, next_in[1], corner_col),
        ]
        result = []
        for t in range(2):
            part = slice(t * LANES, (t + 1) * LANES)
            guess = ycoef[0:1, part] * pltpu.roll(tiles_in[t], 1, 1) + ycoef[1:2, part] * after[t]
            result.append(jnp.where(odd, guess, tiles_in[t]))
        return tiles_in, result

    e_n, s_n = row_along_y(rrecv[0], has_up, corner_n)
    e_s, s_s = row_along_y(rrecv[2], has_down, corner_s)
    for t in range(2):
        part = slice(t * LANES, (t + 1) * LANES)
        rh[0, t] = e_n[t] - s_n[t]
        rh[1, t] = rrecv[1, :, part] * has_up - wl_x * s_n[t]
        rh[2, t] = s_s[t]
        rh[3, t] = e_s[t] - s_s[t]


def main_kernel(
    dens_l, dens_r, colx, ycoef, scal, rh, er, lch, lcl, wcat, gxh, gxl,
    detail, local, coarse, wide, se_buf, de_buf, do_buf, woven,
):
    g = pl.program_id(0)

    @pl.when(g == 0)
    def _():
        for k in range(7):
            wide[k] = column(colx[...], k)

    lane = iota((LANES, LANES), 1)
    odd = (lane & 1) == 1
    inner = lane < LANES - 1
    pick = (2 * lane) & (LANES - 1)
    wrm = scal[S_WRM : S_WRM + 1, :]
    body, before, after = pl.ds(8, LANES), pl.ds(7, LANES), pl.ds(9, LANES)

    def plane(zi, z):
        row = pl.ds(z, 1)
        parts = [slice(t * LANES, (t + 1) * LANES) for t in range(2)]
        e = [dens[zi, pl.ds(0, LANES, stride=2), :] for dens in (dens_l, dens_r)]
        o = [dens[zi, pl.ds(1, LANES, stride=2), :] for dens in (dens_l, dens_r)]
        nxt = [pltpu.roll(v, LANES - 1, 1) for v in e]
        beyond = pltpu.roll(er[...], lax.rem(3 * LANES - 1 - 2 * PLANES - z, LANES), 1)
        nxt = [jnp.where(inner, nxt[0], nxt[1]), jnp.where(inner, nxt[1], beyond)]
        high, low = [], []
        for t in range(2):
            part = parts[t]
            guess = ycoef[0:1, part] * pltpu.roll(e[t], 1, 1) + ycoef[1:2, part] * nxt[t]
            se = jnp.where(odd, guess, e[t])
            de = e[t] - se
            se_buf[t, body, :] = se
            se_buf[t, pl.ds(8 + LANES, 1), :] = rh[2, t, row, :]
            do = o[t] - (wide[X_WL] * se + wide[X_WR] * se_buf[t, after, :])
            woven[t, pl.ds(0, LANES, stride=2), :] = de
            woven[t, pl.ds(1, LANES, stride=2), :] = do
            detail[zi, :, part] = woven[t]
            de_buf[t, body, :] = de
            de_buf[t, pl.ds(7, 1), :] = rh[0, t, row, :]
            de_buf[t, pl.ds(8 + LANES, 1), :] = rh[3, t, row, :]
            do_buf[t, body, :] = do
            do_buf[t, pl.ds(7, 1), :] = rh[1, t, row, :] - wrm * se[0:1, :]
            load = (
                wide[X_K3] * de
                + wide[X_K4] * do
                + wide[X_K1] * de_buf[t, before, :]
                + wide[X_K2] * do_buf[t, before, :]
                + wide[X_K5] * de_buf[t, after, :]
            )
            hi, lo = split(load)
            high.append(hi)
            low.append(lo)
        coarse[zi] = jnp.where(
            lane < LANES // 2,
            jnp.take_along_axis(e[0], pick, axis=1, mode="promise_in_bounds"),
            jnp.take_along_axis(e[1], pick, axis=1, mode="promise_in_bounds"),
        )
        mine = (lane & (PLANES - 1)) == z
        high.append(jnp.where(mine, lch[...].astype(F32), 0.0).astype(BF16))
        low.append(jnp.where(mine, lcl[...].astype(F32), 0.0).astype(BF16))
        both = mxu(jnp.concatenate(high, axis=1), wcat[...])
        rest = mxu(jnp.concatenate(low, axis=1), wcat[:, 0:LANES])
        return both[:, :LANES] + both[:, LANES:] + rest

    for zi in range(0, STEP, 2):
        z = g * STEP + zi
        pair = jnp.concatenate([plane(zi, z), plane(zi + 1, z + 1)], axis=1)
        hi, lo = split(pair)
        solved = mxu(gxh[...], hi) + (mxu(gxh[...], lo) + mxu(gxl[...], hi))
        local[zi] = solved[:, :LANES]
        local[zi + 1] = solved[:, LANES:]


def exchange_kernel(
    nx, ny, local, colx, scal, cf, cb, out,
    xs, xr, ys, yr, sums, uwide, pwide, sx_sem, rx_sem, sy_sem, ry_sem,
):
    p, r = lax.axis_index("gx"), lax.axis_index("gy")
    barrier = pltpu.get_barrier_semaphore()
    for k in range(1, nx):
        pl.semaphore_signal(barrier, inc=1, device_id=(lax.rem(p + k, nx), r), device_id_type=MESH)
    for k in range(1, ny):
        pl.semaphore_signal(barrier, inc=1, device_id=(p, lax.rem(r + k, ny)), device_id_type=MESH)
    xs[0] = local[:, LANES - 1, :] * scal[S_FX : S_FX + 1, :]
    xs[1] = local[:, 0, :] * scal[S_BX : S_BX + 1, :]
    uwide[...] = column(colx[...], X_U)
    pwide[...] = column(colx[...], X_PSI)
    pl.semaphore_wait(barrier, nx + ny - 2)

    def start(sent, got, send_sem, recv_sem, own, count, target):
        copies = []
        for k in range(1, count):
            wraps = jnp.where(own + k >= count, 1, 0)
            copies.append(
                pltpu.make_async_remote_copy(
                    src_ref=sent.at[wraps], dst_ref=got.at[k - 1],
                    send_sem=send_sem.at[k - 1], recv_sem=recv_sem.at[k - 1],
                    device_id=target(lax.rem(own + k, count)), device_id_type=MESH,
                )
            )
            copies[-1].start()
        return copies

    def gather(copies, got, own, count, low):
        forward = jnp.zeros((PLANES, LANES), F32)
        backward = jnp.zeros((PLANES, LANES), F32)
        for k in range(1, count):
            copies[k - 1].wait()
            row = pl.ds(low + lax.rem(own + count - k, count), 1)
            values = got[k - 1]
            forward = forward + cf[row, :] * values
            backward = backward + cb[row, :] * values
        return forward, backward

    copies = start(xs, xr, sx_sem, rx_sem, p, nx, lambda i: (i, r))
    forward, backward = gather(copies, xr, p, nx, 0)
    sums[0] = forward
    sums[1] = backward
    lane = iota((PLANES, LANES), 1)
    blocks = LANES // PLANES

    def x_part(z, carry):
        last, head = carry
        row = pl.ds(z, 1)
        values = local[z] + uwide[...] * sums[0, row, :] + pwide[...] * sums[1, row, :]
        out[z] = values
        for m in range(blocks):
            block = values[m * PLANES : (m + 1) * PLANES, :]
            here = lane == m * PLANES + z
            last = jnp.where(here, block[:, LANES - 1 : LANES], last)
            head = jnp.where(here, block[:, 0:1], head)
        return last, head

    zero = jnp.zeros((PLANES, LANES), F32)
    last, head = lax.fori_loop(0, PLANES, x_part, (zero, zero), unroll=4)
    ys[0] = last * scal[S_FY : S_FY + 1, :]
    ys[1] = head * scal[S_BY : S_BY + 1, :]
    copies = start(ys, yr, sy_sem, ry_sem, r, ny, lambda j: (p, j))
    forward, backward = gather(copies, yr, r, ny, nx)
    sums[0] = forward
    sums[1] = backward
    u_y, psi_y = scal[S_UY : S_UY + 1, :], scal[S_PSIY : S_PSIY + 1, :]

    def y_part(z, carry):
        shift = lax.rem(LANES - z, LANES)
        f = pltpu.roll(sums[0], shift, 1)
        b = pltpu.roll(sums[1], shift, 1)
        for m in range(blocks):
            rows = pl.ds(m * PLANES, PLANES)
            at = m * PLANES
            out[z, rows, :] = out[z, rows, :] + (f[:, at : at + 1] * u_y + b[:, at : at + 1] * psi_y)
        return carry

    lax.fori_loop(0, PLANES, y_part, 0, unroll=4)


def per_device(nx, ny, density, spacing_x, spacing_y):
    blocks = nx + ny
    any_spec = pl.BlockSpec(memory_space=pl.ANY)
    vmem = pl.BlockSpec(memory_space=pltpu.VMEM)
    f32 = lambda *shape: jax.ShapeDtypeStruct(shape, F32)
    bf16 = lambda *shape: jax.ShapeDtypeStruct(shape, BF16)
    sx = spacing_x.reshape(2 * nx, LANES)
    sy = spacing_y.reshape(2 * ny, LANES)
    colx, ycoef, scal, cf, cb, wcat, gxh, gxl, rh, er, lch, lcl = pl.pallas_call(
        functools.partial(prepare_kernel, nx, ny),
        out_shape=(
            f32(LANES, LANES), f32(8, FINE), f32(8, LANES), f32(blocks, LANES), f32(blocks, LANES),
            bf16(FINE + LANES, FINE), bf16(LANES, LANES), bf16(LANES, LANES),
            f32(4, 2, PLANES, LANES), f32(LANES, LANES), bf16(LANES, LANES), bf16(LANES, LANES),
        ),
        in_specs=[any_spec, vmem, vmem],
        out_specs=(vmem,) * 12,
        scratch_shapes=[
            pltpu.VMEM((PLANES, FINE, FINE), F32),
            pltpu.VMEM((3, PLANES, FINE), F32),
            pltpu.VMEM((FINE, LANES), F32),
            pltpu.VMEM((3, PLANES, FINE), F32),
            pltpu.VMEM((FINE, LANES), F32),
            pltpu.VMEM((FINE, LANES), F32),
            pltpu.VMEM((6, 8, LANES), F32),
            pltpu.VMEM((14, blocks, LANES), F32),
            pltpu.VMEM((3, blocks, LANES), F32),
            pltpu.VMEM((LANES, LANES), F32),
            pltpu.VMEM((FINE, LANES), F32),
            pltpu.VMEM((FINE, LANES), F32),
            pltpu.SemaphoreType.DMA((PLANES // STEP,)),
            pltpu.SemaphoreType.DMA((10,)),
            pltpu.SemaphoreType.DMA((10,)),
        ],
        compiler_params=pltpu.CompilerParams(
            collective_id=0, has_side_effects=True, vmem_limit_bytes=32 * MIB
        ),
        name="prepare",
    )(density, sx, sy)
    whole = lambda array: pl.BlockSpec(array.shape, lambda g: (0,) * array.ndim, pipeline_mode=pl.Buffered(1))
    tables = (colx, ycoef, scal, rh, er, lch, lcl, wcat, gxh, gxl)
    detail, local, coarse = pl.pallas_call(
        main_kernel,
        grid=(PLANES // STEP,),
        out_shape=(f32(PLANES, FINE, FINE), f32(PLANES, LANES, LANES), f32(PLANES, LANES, LANES)),
        in_specs=[
            pl.BlockSpec((STEP, FINE, LANES), lambda g: (g, 0, 0)),
            pl.BlockSpec((STEP, FINE, LANES), lambda g: (g, 0, 1)),
        ]
        + [whole(t) for t in tables],
        out_specs=(
            pl.BlockSpec((STEP, FINE, FINE), lambda g: (g, 0, 0)),
            pl.BlockSpec((STEP, LANES, LANES), lambda g: (g, 0, 0)),
            pl.BlockSpec((STEP, LANES, LANES), lambda g: (g, 0, 0)),
        ),
        scratch_shapes=[
            pltpu.VMEM((7, LANES, LANES), F32),
            pltpu.VMEM((2, LANES + 16, LANES), F32),
            pltpu.VMEM((2, LANES + 16, LANES), F32),
            pltpu.VMEM((2, LANES + 16, LANES), F32),
            pltpu.VMEM((2, FINE, LANES), F32),
        ],
        compiler_params=pltpu.CompilerParams(vmem_limit_bytes=32 * MIB),
        name="main",
    )(density, density, *tables)
    correction = pl.pallas_call(
        functools.partial(exchange_kernel, nx, ny),
        out_shape=f32(PLANES, LANES, LANES),
        in_specs=[vmem] * 5,
        out_specs=vmem,
        scratch_shapes=[
            pltpu.VMEM((2, PLANES, LANES), F32),
            pltpu.VMEM((nx - 1, PLANES, LANES), F32),
            pltpu.VMEM((2, PLANES, LANES), F32),
            pltpu.VMEM((ny - 1, PLANES, LANES), F32),
            pltpu.VMEM((2, PLANES, LANES), F32),
            pltpu.VMEM((LANES, LANES), F32),
            pltpu.VMEM((LANES, LANES), F32),
            pltpu.SemaphoreType.DMA((nx - 1,)),
            pltpu.SemaphoreType.DMA((nx - 1,)),
            pltpu.SemaphoreType.DMA((ny - 1,)),
            pltpu.SemaphoreType.DMA((ny - 1,)),
        ],
        compiler_params=pltpu.CompilerParams(
            collective_id=1, has_side_effects=True, vmem_limit_bytes=32 * MIB
        ),
        name="exchange",
    )(local, colx, scal, cf, cb)
    return detail, coarse + correction


def solution(mesh):
    placed = P(None, "gx", "gy")
    return jax.shard_map(
        functools.partial(per_device, mesh.shape["gx"], mesh.shape["gy"]),
        mesh=mesh,
        in_specs=(placed, P(), P()),
        out_specs=(placed, placed),
        check_vma=False,
    )
```

```python
import functools

import jax
import jax.numpy as jnp
from jax import lax
from jax.experimental import pallas as pl
from jax.experimental.pallas import tpu as pltpu
from jax.sharding import PartitionSpec as P

MESH = pl.DeviceIdType.MESH
F32 = jnp.float32
BF16 = jnp.bfloat16
HIGHEST = lax.Precision.HIGHEST
stiffness_weight = 4096.0
operator_divisor = 32.0
LANES = 128
FINE = 256
PLANES = 32
STEP = 4
MIB = 1 << 20
X_WL, X_WR, X_K1, X_K2, X_K3, X_K4, X_K5, X_U, X_PSI, X_W = range(10)
Y_K1, Y_K2, Y_K3, Y_K4, Y_K5, Y_U, Y_W = range(10, 17)
S_FX, S_BX, S_FY, S_BY, S_WRM, S_UY, S_PSIY = range(7)


def split(values):
    high = values.astype(BF16)
    return high, (values - high.astype(F32)).astype(BF16)


def mxu(a, b):
    return jnp.dot(a, b, preferred_element_type=F32)


def iota(shape, dim):
    return lax.broadcasted_iota(jnp.int32, shape, dim)


def column(table, index):
    return jnp.broadcast_to(table[:, index : index + 1], (LANES, LANES))


def shift_up(values, last):
    rolled = pltpu.roll(values, LANES - 1, 0)
    return jnp.where(iota(values.shape, 0) == LANES - 1, last, rolled)


def shift_down(values, first):
    return jnp.where(iota(values.shape, 0) == 0, first, pltpu.roll(values, 1, 0))


def chain_tables(blocks_x, blocks_y, sx, sy, tab, rows_in):
    count = blocks_x + blocks_y
    shape = (count, LANES)
    lane, row = iota(shape, 1), iota(shape, 0)
    first = (lane == 0) & ((row == 0) | (row == blocks_x))

    def prev(values, fill):
        rolled = pltpu.roll(values, 1, 1)
        return jnp.where(first, fill, jnp.where(lane == 0, pltpu.roll(rolled, 1, 0), rolled))

    def following(values):
        rolled = pltpu.roll(values, LANES - 1, 1)
        return jnp.where(lane == LANES - 1, pltpu.roll(rolled, count - 1, 0), rolled)

    def halves(start):
        return jnp.concatenate(
            [sx[pl.ds(start, blocks_x, stride=2), :], sy[pl.ds(start, blocks_y, stride=2), :]], axis=0
        )

    fine = jnp.concatenate([halves(0), halves(1)], axis=1)
    node, place = iota((FINE, FINE), 0), iota((FINE, FINE), 1)
    pick = jnp.where(place < LANES, 2 * place, 2 * (place - LANES) + 1)
    parts = jnp.dot((fine), (node == pick).astype(F32), precision=HIGHEST, preferred_element_type=F32)
    c, d = parts[:, :LANES], parts[:, LANES:]
    span = c + d
    a, b = prev(c, 0.0), prev(d, 0.0)
    span_before = prev(span, 1.0)
    inverse = 1.0 / span
    inverse_before = 1.0 / span_before
    tab[0] = d * inverse
    tab[1] = c * inverse
    tab[2] = a * a * inverse_before * (1.0 / 6.0)
    tab[3] = a * (1.0 / 3.0) + b * (1.0 / 6.0)
    tab[4] = (a * b * inverse_before + c * d * inverse) * (1.0 / 6.0) + (b + c) * (1.0 / 3.0)
    tab[5] = c * (1.0 / 6.0) + d * (1.0 / 3.0)
    tab[6] = d * d * inverse * (1.0 / 6.0)
    tab[9] = b * inverse_before
    tab[10] = a * inverse_before

    rho = 1.0 / (stiffness_weight * inverse - span * (1.0 / 6.0))
    rho_before = prev(rho, 0.0)
    mu = 0.5 * (a + b + span)
    mu_after = following(mu)
    one = jnp.ones(shape, F32)
    fwd = (one + mu * rho_before, mu, rho_before, one)
    bwd = (one, mu_after, rho, one + rho * mu_after)
    step = 1
    while step < LANES:
        def join(m, shift, outside):
            fill = (1.0, 0.0, 0.0, 1.0)
            a1, b1, c1, d1 = m
            a0, b0, c0, d0 = (
                jnp.where(outside, f, pltpu.roll(v, shift, 1)) for v, f in zip(m, fill)
            )
            return (a1 * a0 + b1 * c0, a1 * b0 + b1 * d0, c1 * a0 + d1 * c0, c1 * b0 + d1 * d0)

        fwd = join(fwd, step, lane < step)
        bwd = join(bwd, LANES - step, lane >= LANES - step)
        step *= 2
    ends = [jnp.broadcast_to(v[:, LANES - 1 : LANES], shape) for v in fwd]
    starts = [jnp.broadcast_to(v[:, 0:1], shape) for v in bwd]
    for low, size in ((0, blocks_x), (blocks_x, blocks_y)):
        y = jnp.zeros((1, LANES), F32)
        for q in range(low, low + size):
            rows_in[0, q : q + 1, :] = y
            at, bt, ct, dt = (v[q : q + 1, :] for v in ends)
            y = (at * y + bt) / (ct * y + dt)
        z = None
        for q in reversed(range(low, low + size)):
            at, bt, ct, dt = (v[q : q + 1, :] for v in starts)
            if z is None:
                rows_in[1, q : q + 1, :] = jnp.ones((1, LANES), F32)
                rows_in[2, q : q + 1, :] = jnp.zeros((1, LANES), F32)
                z = at / ct
            else:
                rows_in[1, q : q + 1, :] = z
                rows_in[2, q : q + 1, :] = jnp.ones((1, LANES), F32)
                z = (at * z + bt) / (ct * z + dt)
    y_in, z_num, z_den = rows_in[0], rows_in[1], rows_in[2]
    den = fwd[2] * y_in + fwd[3]
    left = (fwd[0] * y_in + fwd[1]) / den
    right = (bwd[0] * z_num + bwd[1] * z_den) / (bwd[2] * z_num + bwd[3] * z_den)
    green = operator_divisor / (left + right)
    tab[7] = green / den
    tab[8] = den
    tab[11] = 1.0 / jnp.broadcast_to(den[:, LANES - 1 : LANES], shape)
    tab[12] = 1.0 / jnp.broadcast_to(green[:, LANES - 1 : LANES], shape)
    tab[13] = 1.0 / jnp.broadcast_to(den[:, 0:1], shape)


def weights_between(gain, low, size, own, forward, backward):
    q = iota((size, LANES), 0)
    ahead = jnp.ones((size, LANES), F32)
    behind = jnp.ones((size, LANES), F32)
    for m in range(size):
        g = gain[low + m : low + m + 1, :]
        ahead = ahead * jnp.where((m > q) & (m < own), g, 1.0)
        behind = behind * jnp.where((m < q) & (m > own), g, 1.0)
    forward[low : low + size, :] = jnp.where(q < own, ahead, 0.0)
    backward[low : low + size, :] = jnp.where(q > own, behind, 0.0)


def green_block(u_col, w_col, u_row, w_row):
    i, j = iota((LANES, LANES), 0), iota((LANES, LANES), 1)
    return jnp.where(i >= j, u_col * w_row, w_col * u_row)


def prepare_kernel(
    nx, ny, dens, sx_in, sy_in,
    colx, ycoef, scal, cf, cb, wcat, gxh, gxl, rh, er, lch, lcl, packed, box,
    sx, sy, rsend, to_right, to_left, rrecv, from_left, from_right, tiles,
    tab, rows_in, stack, wfine, load_sem, send_sem, recv_sem,
):
    p, r = lax.axis_index("gx"), lax.axis_index("gy")
    up, down = lax.rem(p + nx - 1, nx), lax.rem(p + 1, nx)
    left, right = lax.rem(r + ny - 1, ny), lax.rem(r + 1, ny)
    loads = []
    for k in range(PLANES // STEP):
        part = pl.ds(k * STEP, STEP)
        loads.append(pltpu.make_async_copy(dens.at[part], box.at[part], load_sem.at[k]))
        loads[-1].start()
    for k, (src, dst) in enumerate(((sx_in, sx), (sy_in, sy))):
        loads.append(pltpu.make_async_copy(src, dst, load_sem.at[PLANES // STEP + k]))
        loads[-1].start()
    barrier = pltpu.get_barrier_semaphore()
    for i in (up, p, down):
        for j in (left, r, right):
            if i is p and j is r:
                continue
            pl.semaphore_signal(barrier, inc=1, device_id=(i, j), device_id_type=MESH)

    right_rows, left_rows = FINE // 2, FINE // 4
    lane_r, lane_l = iota((right_rows, LANES), 1), iota((left_rows, LANES), 1)
    to_right[...] = jnp.zeros((right_rows, LANES), F32)
    to_left[...] = jnp.zeros((left_rows, LANES), F32)
    for k in range(PLANES // STEP):
        loads[k].wait()
        acc_r, acc_l = to_right[...], to_left[...]
        for zi in range(STEP):
            z = k * STEP + zi
            for m in range(2):
                rows = slice(m * right_rows, (m + 1) * right_rows)
                at = 2 * m * PLANES + z
                acc_r = jnp.where(lane_r == at, box[z, rows, FINE - 2 : FINE - 1], acc_r)
                acc_r = jnp.where(lane_r == at + PLANES, box[z, rows, FINE - 1 : FINE], acc_r)
            for m in range(4):
                rows = slice(m * left_rows, (m + 1) * left_rows)
                acc_l = jnp.where(lane_l == m * PLANES + z, box[z, rows, 0:1], acc_l)
            rsend[0, z : z + 1, :] = box[z, FINE - 2 : FINE - 1, :]
            rsend[1, z : z + 1, :] = box[z, FINE - 1 : FINE, :]
            rsend[2, z : z + 1, :] = box[z, 0:1, :]
        to_right[...] = acc_r
        to_left[...] = acc_l

    pl.semaphore_wait(barrier, 8)
    top = pl.ds(0, 8)
    end_r, end_l = pl.ds(right_rows - 8, 8), pl.ds(left_rows - 8, 8)
    plan = (
        (to_right, from_left, p, right),
        (to_left, from_right, p, left),
        (rsend.at[pl.ds(0, 2)], rrecv.at[pl.ds(0, 2)], down, r),
        (rsend.at[pl.ds(2, 1)], rrecv.at[pl.ds(2, 1)], up, r),
        (to_left.at[end_l], tiles.at[0], down, r),
        (to_left.at[top], tiles.at[1], up, r),
        (to_right.at[end_r], tiles.at[2], down, right),
        (to_left.at[end_l], tiles.at[3], down, left),
        (to_right.at[top], tiles.at[4], up, right),
        (to_left.at[top], tiles.at[5], up, left),
    )
    copies = []
    for k, (src, dst, i, j) in enumerate(plan):
        copies.append(
            pltpu.make_async_remote_copy(
                src_ref=src, dst_ref=dst, send_sem=send_sem.at[k], recv_sem=recv_sem.at[k],
                device_id=(i, j), device_id_type=MESH,
            )
        )
        copies[-1].start()

    for load in loads[PLANES // STEP :]:
        load.wait()
    chain_tables(nx, ny, sx, sy, tab, rows_in)
    weights_between(tab[11], 0, nx, p, cf, cb)
    weights_between(tab[11], nx, ny, r, cf, cb)
    row_x, row_y = pl.ds(p, 1), pl.ds(nx + r, 1)
    ux, wx, uy, wy = tab[7, row_x, :], tab[8, row_x, :], tab[7, row_y, :], tab[8, row_y, :]
    stack[...] = jnp.zeros((LANES, LANES), F32)
    for k in range(7):
        stack[k : k + 1, :] = tab[k, row_x, :]
    stack[X_U : X_U + 1, :] = ux
    stack[X_PSI : X_PSI + 1, :] = wx * tab[11, row_x, :]
    stack[X_W : X_W + 1, :] = wx
    for k in range(5):
        stack[Y_K1 + k : Y_K1 + k + 1, :] = tab[2 + k, row_y, :]
    stack[Y_U : Y_U + 1, :] = uy
    stack[Y_W : Y_W + 1, :] = wy
    cols = stack[...].T
    colx[...] = cols
    scal[...] = jnp.zeros((8, LANES), F32)
    scal[S_FX : S_FX + 1, :] = tab[12, row_x, :]
    scal[S_BX : S_BX + 1, :] = tab[13, row_x, :]
    scal[S_FY : S_FY + 1, :] = tab[12, row_y, :]
    scal[S_BY : S_BY + 1, :] = tab[13, row_y, :]
    wl_x = tab[9, row_x, :][:, 0:1]
    wr_x = tab[10, row_x, :][:, 0:1]
    wl_y = tab[9, row_y, :][:, 0:1]
    wr_y = tab[10, row_y, :][:, 0:1]
    scal[S_WRM : S_WRM + 1, :] = jnp.broadcast_to(wr_x, (1, LANES))
    scal[S_UY : S_UY + 1, :] = uy
    scal[S_PSIY : S_PSIY + 1, :] = wy * tab[11, row_y, :]

    lane_z = iota((PLANES, LANES), 1)
    for k, index in enumerate((X_U, X_PSI)):
        packed[k] = sum(
            jnp.where(lane_z // PLANES == m, cols[m * PLANES : (m + 1) * PLANES, index : index + 1], 0.0)
            for m in range(LANES // PLANES)
        )

    odd_row = (iota((1, LANES), 1) & 1) == 1
    ycoef[...] = jnp.zeros((8, FINE), F32)
    for t in range(2):
        h = sy[pl.ds(2 * r + t, 1), :]
        hp = pltpu.roll(h, 1, 1)
        inv = 1.0 / (h + hp)
        ycoef[0:1, t * LANES : (t + 1) * LANES] = jnp.where(odd_row, h * inv, 0.0)
        ycoef[1:2, t * LANES : (t + 1) * LANES] = jnp.where(odd_row, hp * inv, 0.0)

    hi, lo = split(green_block(column(cols, X_U), column(cols, X_W), ux, wx))
    gxh[...] = hi
    gxl[...] = lo
    gy = green_block(column(cols, Y_U), column(cols, Y_W), uy, wy)
    g1, g2, g3, g4, g5 = (column(cols, Y_K1 + k) * gy for k in range(5))
    wfine[pl.ds(0, LANES, stride=2), :] = g3 + shift_down(g5, 0.0) + shift_up(g1, 0.0)
    wfine[pl.ds(1, LANES, stride=2), :] = g4 + shift_up(g2, 0.0)
    i = iota((LANES, LANES), 0)
    outer = jnp.where(
        i < PLANES, g1[0:1, :],
        jnp.where(i < 2 * PLANES, g2[0:1, :], jnp.where(i < 3 * PLANES, g5[LANES - 1 : LANES, :], 0.0)),
    )
    hi, lo = split(wfine[...])
    wcat[0:FINE, 0:LANES] = hi
    wcat[0:FINE, LANES:FINE] = lo
    hi, lo = split(outer)
    wcat[FINE : FINE + LANES, 0:LANES] = hi
    wcat[FINE : FINE + LANES, LANES:FINE] = lo

    for copy in copies:
        copy.wait()

    has_up = (p > 0).astype(F32)
    has_down = (p < nx - 1).astype(F32)
    has_left = (r > 0).astype(F32)
    has_right = (r < ny - 1).astype(F32)
    lane_8 = iota((8, LANES), 1)
    lane = iota((LANES, LANES), 1)

    def unpack(ref, start, shifts):
        values = ref[pl.ds(start, LANES // len(shifts), stride=2), :]
        return jnp.concatenate([pltpu.roll(values, n, 1) if n else values for n in shifts], axis=0)

    e_c, o_c = (
        jnp.where(
            lane < 2 * PLANES,
            unpack(from_left, start, (0, 64)) * has_left,
            unpack(from_right, start, (64, 32, 0, 96)) * has_right,
        )
        for start in range(2)
    )
    own = unpack(to_left, 0, (32, 0, 96, 64))
    own_n = pltpu.roll(tiles[0], 64, 1) * has_up
    own_s = pltpu.roll(tiles[1], 32, 1) * has_down
    north = (
        jnp.where(
            lane_8 < 2 * PLANES,
            pltpu.roll(tiles[2], 64, 1) * has_left,
            pltpu.roll(tiles[3], 96, 1) * has_right,
        )
        * has_up
    )
    south = (
        jnp.where(lane_8 < 2 * PLANES, tiles[4] * has_left, pltpu.roll(tiles[5], 64, 1) * has_right)
        * has_down
    )

    def along_y(values, own_values):
        at = iota(values.shape, 1)
        guess = wl_y * pltpu.roll(values, PLANES, 1) + wr_y * own_values
        return jnp.where((at >= PLANES) & (at < 2 * PLANES), guess, values)

    se = along_y(e_c, own)
    se_n = along_y(north, own_n)[6:7, :]
    se_s = along_y(south, own_s)[0:1, :]
    do = o_c - (column(cols, X_WL) * se + column(cols, X_WR) * shift_up(se, se_s))
    de = e_c - se
    de_n = north[6:7, :] - se_n
    do_n = north[7:8, :] - (wl_x * se_n + wr_x * se[0:1, :])
    de_s = south[0:1, :] - se_s
    loads_c = (
        column(cols, X_K1) * shift_down(de, de_n)
        + column(cols, X_K2) * shift_down(do, do_n)
        + column(cols, X_K3) * de
        + column(cols, X_K4) * do
        + column(cols, X_K5) * shift_up(de, de_s)
    )
    hi, lo = split(loads_c)
    lch[...] = hi
    lcl[...] = lo
    er[...] = e_c

    stack[0:8, :] = north
    stack[8:16, :] = south
    corner = stack[...].T
    corner_n = corner[2 * PLANES : 3 * PLANES, 6:7]
    corner_s = corner[2 * PLANES : 3 * PLANES, 8:9]
    odd = (lane_z & 1) == 1

    def row_along_y(layer, scale, corner_col):
        tiles_in = [layer[:, t * LANES : (t + 1) * LANES] * scale for t in range(2)]
        next_in = [pltpu.roll(v, LANES - 1, 1) for v in tiles_in]
        after = [
            jnp.where(lane_z < LANES - 1, next_in[0], next_in[1]),
            jnp.where(lane_z < LANES - 1, next_in[1], corner_col),
        ]
        result = []
        for t in range(2):
            part = slice(t * LANES, (t + 1) * LANES)
            guess = ycoef[0:1, part] * pltpu.roll(tiles_in[t], 1, 1) + ycoef[1:2, part] * after[t]
            result.append(jnp.where(odd, guess, tiles_in[t]))
        return tiles_in, result

    e_n, s_n = row_along_y(rrecv[0], has_up, corner_n)
    e_s, s_s = row_along_y(rrecv[2], has_down, corner_s)
    for t in range(2):
        part = slice(t * LANES, (t + 1) * LANES)
        rh[0, t] = e_n[t] - s_n[t]
        rh[1, t] = rrecv[1, :, part] * has_up - wl_x * s_n[t]
        rh[2, t] = s_s[t]
        rh[3, t] = e_s[t] - s_s[t]


def main_kernel(
    dens_l, dens_r, colx, ycoef, scal, rh, er, lch, lcl, wcat, gxh, gxl,
    detail, local, coarse, wide, se_buf, de_buf, do_buf, woven,
):
    g = pl.program_id(0)

    @pl.when(g == 0)
    def _():
        for k in range(7):
            wide[k] = column(colx[...], k)

    lane = iota((LANES, LANES), 1)
    odd = (lane & 1) == 1
    inner = lane < LANES - 1
    pick = (2 * lane) & (LANES - 1)
    wrm = scal[S_WRM : S_WRM + 1, :]
    body, before, after = pl.ds(8, LANES), pl.ds(7, LANES), pl.ds(9, LANES)

    def plane(zi, z):
        row = pl.ds(z, 1)
        parts = [slice(t * LANES, (t + 1) * LANES) for t in range(2)]
        e = [dens[zi, pl.ds(0, LANES, stride=2), :] for dens in (dens_l, dens_r)]
        o = [dens[zi, pl.ds(1, LANES, stride=2), :] for dens in (dens_l, dens_r)]
        nxt = [pltpu.roll(v, LANES - 1, 1) for v in e]
        beyond = pltpu.roll(er[...], lax.rem(3 * LANES - 1 - 2 * PLANES - z, LANES), 1)
        nxt = [jnp.where(inner, nxt[0], nxt[1]), jnp.where(inner, nxt[1], beyond)]
        high, low = [], []
        for t in range(2):
            part = parts[t]
            guess = ycoef[0:1, part] * pltpu.roll(e[t], 1, 1) + ycoef[1:2, part] * nxt[t]
            se = jnp.where(odd, guess, e[t])
            de = e[t] - se
            se_buf[t, body, :] = se
            se_buf[t, pl.ds(8 + LANES, 1), :] = rh[2, t, row, :]
            do = o[t] - (wide[X_WL] * se + wide[X_WR] * se_buf[t, after, :])
            woven[t, pl.ds(0, LANES, stride=2), :] = de
            woven[t, pl.ds(1, LANES, stride=2), :] = do
            detail[zi, :, part] = woven[t]
            de_buf[t, body, :] = de
            de_buf[t, pl.ds(7, 1), :] = rh[0, t, row, :]
            de_buf[t, pl.ds(8 + LANES, 1), :] = rh[3, t, row, :]
            do_buf[t, body, :] = do
            do_buf[t, pl.ds(7, 1), :] = rh[1, t, row, :] - wrm * se[0:1, :]
            load = (
                wide[X_K3] * de
                + wide[X_K4] * do
                + wide[X_K1] * de_buf[t, before, :]
                + wide[X_K2] * do_buf[t, before, :]
                + wide[X_K5] * de_buf[t, after, :]
            )
            hi, lo = split(load)
            high.append(hi)
            low.append(lo)
        coarse[zi] = jnp.where(
            lane < LANES // 2,
            jnp.take_along_axis(e[0], pick, axis=1, mode="promise_in_bounds"),
            jnp.take_along_axis(e[1], pick, axis=1, mode="promise_in_bounds"),
        )
        mine = (lane & (PLANES - 1)) == z
        high.append(jnp.where(mine, lch[...].astype(F32), 0.0).astype(BF16))
        low.append(jnp.where(mine, lcl[...].astype(F32), 0.0).astype(BF16))
        both = mxu(jnp.concatenate(high, axis=1), wcat[...])
        rest = mxu(jnp.concatenate(low, axis=1), wcat[:, 0:LANES])
        return both[:, :LANES] + both[:, LANES:] + rest

    for zi in range(0, STEP, 2):
        z = g * STEP + zi
        pair = jnp.concatenate([plane(zi, z), plane(zi + 1, z + 1)], axis=1)
        hi, lo = split(pair)
        solved = mxu(gxh[...], hi) + (mxu(gxh[...], lo) + mxu(gxl[...], hi))
        local[zi] = solved[:, :LANES]
        local[zi + 1] = solved[:, LANES:]


def exchange_kernel(
    nx, ny, local, coarse, colx, scal, cf, cb, packed, mid, outer_l, outer_r,
    xs, xr, ys, yr, sums, uwide, pwide, sx_sem, rx_sem, sy_sem, ry_sem,
):
    p, r = lax.axis_index("gx"), lax.axis_index("gy")
    barrier = pltpu.get_barrier_semaphore()
    for k in range(1, nx):
        pl.semaphore_signal(barrier, inc=1, device_id=(lax.rem(p + k, nx), r), device_id_type=MESH)
    for k in range(1, ny):
        pl.semaphore_signal(barrier, inc=1, device_id=(p, lax.rem(r + k, ny)), device_id_type=MESH)
    xs[0] = local[:, LANES - 1, :] * scal[S_FX : S_FX + 1, :]
    xs[1] = local[:, 0, :] * scal[S_BX : S_BX + 1, :]
    uwide[...] = column(colx[...], X_U)
    pwide[...] = column(colx[...], X_PSI)
    pl.semaphore_wait(barrier, nx + ny - 2)

    def start(sent, got, send_sem, recv_sem, own, count, target):
        copies = []
        for k in range(1, count):
            wraps = jnp.where(own + k >= count, 1, 0)
            copies.append(
                pltpu.make_async_remote_copy(
                    src_ref=sent.at[wraps], dst_ref=got.at[k - 1],
                    send_sem=send_sem.at[k - 1], recv_sem=recv_sem.at[k - 1],
                    device_id=target(lax.rem(own + k, count)), device_id_type=MESH,
                )
            )
            copies[-1].start()
        return copies

    def gather(copies, got, own, count, low):
        forward = jnp.zeros((PLANES, LANES), F32)
        backward = jnp.zeros((PLANES, LANES), F32)
        for k in range(1, count):
            copies[k - 1].wait_recv()
            row = pl.ds(low + lax.rem(own + count - k, count), 1)
            values = got[k - 1]
            forward = forward + cf[row, :] * values
            backward = backward + cb[row, :] * values
        return forward, backward

    x_copies = start(xs, xr, sx_sem, rx_sem, p, nx, lambda i: (i, r))

    lane = iota((PLANES, LANES), 1)
    blocks = LANES // PLANES

    def edges(z, carry):
        last, head = carry
        for m in range(blocks):
            block = local[z, pl.ds(m * PLANES, PLANES), :]
            here = lane == m * PLANES + z
            last = jnp.where(here, block[:, LANES - 1 : LANES], last)
            head = jnp.where(here, block[:, 0:1], head)
        return last, head

    zero = jnp.zeros((PLANES, LANES), F32)
    last, head = lax.fori_loop(0, PLANES, edges, (zero, zero), unroll=4)
    forward, backward = gather(x_copies, xr, p, nx, 0)
    sums[0] = forward
    sums[1] = backward
    across_f = jnp.concatenate([forward] * blocks, axis=0).T
    across_b = jnp.concatenate([backward] * blocks, axis=0).T
    u_x, psi_x = packed[0], packed[1]
    end = slice(LANES - 1, LANES)
    ys[0] = (last + u_x * across_f[end, :] + psi_x * across_b[end, :]) * scal[S_FY : S_FY + 1, :]
    ys[1] = (head + u_x * across_f[0:1, :] + psi_x * across_b[0:1, :]) * scal[S_BY : S_BY + 1, :]
    y_copies = start(ys, yr, sy_sem, ry_sem, r, ny, lambda j: (p, j))

    edge = jnp.where(
        (iota((LANES, LANES), 0) // PLANES) % 2 == 0,
        scal[S_UY : S_UY + 1, :], scal[S_PSIY : S_PSIY + 1, :],
    )
    edge_h = edge.astype(BF16).astype(F32)
    edge_l = edge - edge_h
    plane_of = iota((LANES, LANES), 0) % PLANES

    def x_part(z, carry):
        row = pl.ds(z, 1)
        mid[z] = local[z] + coarse[z] + uwide[...] * sums[0, row, :] + pwide[...] * sums[1, row, :]
        outer_r[z, 0:LANES, :] = jnp.where(plane_of == z, edge_h, 0.0).astype(BF16)
        outer_r[z, LANES:, :] = jnp.where(plane_of == z, edge_l, 0.0).astype(BF16)
        return carry

    lax.fori_loop(0, PLANES, x_part, 0, unroll=2)
    forward, backward = gather(y_copies, yr, r, ny, nx)
    lane = iota((LANES, LANES), 1)

    def spread(values):
        return jnp.concatenate(
            [pltpu.roll(values, (LANES - m * PLANES) % LANES, 1) if m else values for m in range(blocks)],
            axis=0,
        )

    both = jnp.where(lane < PLANES, spread(forward), pltpu.roll(spread(backward), PLANES, 1))
    high = both.astype(BF16).astype(F32)
    both = jnp.where(lane < 2 * PLANES, high, pltpu.roll(both - high, 2 * PLANES, 1))
    outer_l[:, 0:LANES] = both.astype(BF16)
    outer_l[:, LANES:] = both.astype(BF16)
    for copy in x_copies + y_copies:
        copy.wait_send()


def final_kernel(mid, outer_l, outer_r, out):
    for z in range(0, mid.shape[0], 2):
        pair = jnp.concatenate([outer_r[z], outer_r[z + 1]], axis=1)
        update = mxu(outer_l[...], pair)
        out[z] = mid[z] + update[:, :LANES]
        out[z + 1] = mid[z + 1] + update[:, LANES:]


def per_device(nx, ny, density, spacing_x, spacing_y):
    blocks = nx + ny
    hbm = pl.BlockSpec(memory_space=pltpu.HBM)
    vmem = pl.BlockSpec(memory_space=pltpu.VMEM)
    f32 = lambda *shape: jax.ShapeDtypeStruct(shape, F32)
    bf16 = lambda *shape: jax.ShapeDtypeStruct(shape, BF16)
    sx = spacing_x.reshape(2 * nx, LANES)
    sy = spacing_y.reshape(2 * ny, LANES)
    colx, ycoef, scal, cf, cb, wcat, gxh, gxl, rh, er, lch, lcl, packed, box = pl.pallas_call(
        functools.partial(prepare_kernel, nx, ny),
        out_shape=(
            f32(LANES, LANES), f32(8, FINE), f32(8, LANES), f32(blocks, LANES), f32(blocks, LANES),
            bf16(FINE + LANES, FINE), bf16(LANES, LANES), bf16(LANES, LANES),
            f32(4, 2, PLANES, LANES), f32(LANES, LANES), bf16(LANES, LANES), bf16(LANES, LANES),
            f32(2, PLANES, LANES), f32(PLANES, FINE, FINE),
        ),
        in_specs=[hbm] * 3,
        out_specs=(vmem,) * 14,
        scratch_shapes=[
            pltpu.VMEM((2 * nx, LANES), F32),
            pltpu.VMEM((2 * ny, LANES), F32),
            pltpu.VMEM((3, PLANES, FINE), F32),
            pltpu.VMEM((FINE // 2, LANES), F32),
            pltpu.VMEM((FINE // 4, LANES), F32),
            pltpu.VMEM((3, PLANES, FINE), F32),
            pltpu.VMEM((FINE // 2, LANES), F32),
            pltpu.VMEM((FINE // 4, LANES), F32),
            pltpu.VMEM((6, 8, LANES), F32),
            pltpu.VMEM((14, blocks, LANES), F32),
            pltpu.VMEM((3, blocks, LANES), F32),
            pltpu.VMEM((LANES, LANES), F32),
            pltpu.VMEM((FINE, LANES), F32),
            pltpu.SemaphoreType.DMA((PLANES // STEP + 2,)),
            pltpu.SemaphoreType.DMA((10,)),
            pltpu.SemaphoreType.DMA((10,)),
        ],
        compiler_params=pltpu.CompilerParams(
            collective_id=0, has_side_effects=True, vmem_limit_bytes=32 * MIB
        ),
        name="prepare",
    )(*(pltpu.with_memory_space_constraint(v, pltpu.HBM) for v in (density, sx, sy)))
    whole = lambda array: pl.BlockSpec(array.shape, lambda g: (0,) * array.ndim, pipeline_mode=pl.Buffered(1))
    tables = (colx, ycoef, scal, rh, er, lch, lcl, wcat, gxh, gxl)
    detail, local, coarse = pl.pallas_call(
        main_kernel,
        grid=(PLANES // STEP,),
        out_shape=(f32(PLANES, FINE, FINE), f32(PLANES, LANES, LANES), f32(PLANES, LANES, LANES)),
        in_specs=[
            pl.BlockSpec((STEP, FINE, LANES), lambda g: (g, 0, 0)),
            pl.BlockSpec((STEP, FINE, LANES), lambda g: (g, 0, 1)),
        ]
        + [whole(t) for t in tables],
        out_specs=(
            pl.BlockSpec((STEP, FINE, FINE), lambda g: (g, 0, 0)),
            pl.BlockSpec((STEP, LANES, LANES), lambda g: (g, 0, 0)),
            pl.BlockSpec((STEP, LANES, LANES), lambda g: (g, 0, 0)),
        ),
        scratch_shapes=[
            pltpu.VMEM((7, LANES, LANES), F32),
            pltpu.VMEM((2, LANES + 16, LANES), F32),
            pltpu.VMEM((2, LANES + 16, LANES), F32),
            pltpu.VMEM((2, LANES + 16, LANES), F32),
            pltpu.VMEM((2, FINE, LANES), F32),
        ],
        compiler_params=pltpu.CompilerParams(vmem_limit_bytes=32 * MIB),
        name="main",
    )(box, box, *tables)
    mid, outer_l, outer_r = pl.pallas_call(
        functools.partial(exchange_kernel, nx, ny),
        out_shape=(f32(PLANES, LANES, LANES), bf16(LANES, FINE), bf16(PLANES, FINE, LANES)),
        in_specs=[vmem] * 7,
        out_specs=(vmem,) * 3,
        scratch_shapes=[
            pltpu.VMEM((2, PLANES, LANES), F32),
            pltpu.VMEM((nx - 1, PLANES, LANES), F32),
            pltpu.VMEM((2, PLANES, LANES), F32),
            pltpu.VMEM((ny - 1, PLANES, LANES), F32),
            pltpu.VMEM((2, PLANES, LANES), F32),
            pltpu.VMEM((LANES, LANES), F32),
            pltpu.VMEM((LANES, LANES), F32),
            pltpu.SemaphoreType.DMA((nx - 1,)),
            pltpu.SemaphoreType.DMA((nx - 1,)),
            pltpu.SemaphoreType.DMA((ny - 1,)),
            pltpu.SemaphoreType.DMA((ny - 1,)),
        ],
        compiler_params=pltpu.CompilerParams(
            collective_id=1, has_side_effects=True, vmem_limit_bytes=32 * MIB
        ),
        name="exchange",
    )(local, coarse, colx, scal, cf, cb, packed)
    coarse_new = pl.pallas_call(
        final_kernel,
        grid=(PLANES // 8,),
        out_shape=f32(PLANES, LANES, LANES),
        in_specs=[
            pl.BlockSpec((8, LANES, LANES), lambda g: (g, 0, 0)),
            pl.BlockSpec((LANES, FINE), lambda g: (0, 0)),
            pl.BlockSpec((8, FINE, LANES), lambda g: (g, 0, 0)),
        ],
        out_specs=pl.BlockSpec((8, LANES, LANES), lambda g: (g, 0, 0)),
        compiler_params=pltpu.CompilerParams(vmem_limit_bytes=32 * MIB),
        name="final",
    )(mid, outer_l, outer_r)
    return detail, coarse_new


def solution(mesh):
    placed = P(None, "gx", "gy")
    return jax.shard_map(
        functools.partial(per_device, mesh.shape["gx"], mesh.shape["gy"]),
        mesh=mesh,
        in_specs=(placed, P(), P()),
        out_specs=(placed, placed),
        check_vma=False,
    )
```

```python
import functools

import jax
import jax.numpy as jnp
from jax import lax
from jax.experimental import pallas as pl
from jax.experimental.pallas import tpu as pltpu
from jax.sharding import PartitionSpec as P

MESH = pl.DeviceIdType.MESH
F32 = jnp.float32
BF16 = jnp.bfloat16
HIGHEST = lax.Precision.HIGHEST
stiffness_weight = 4096.0
operator_divisor = 32.0
LANES = 128
FINE = 256
PLANES = 32
PER = 8
STEP = 4
MIB = 1 << 20
X_WL, X_WR, X_K1, X_K2, X_K3, X_K4, X_K5, X_U, X_PSI, X_W = range(10)
Y_K1, Y_K2, Y_K3, Y_K4, Y_K5, Y_U, Y_W = range(10, 17)
S_FX, S_BX, S_FY, S_BY, S_WRM, S_UY, S_PSIY = range(7)


def split(values):
    high = values.astype(BF16)
    return high, (values - high.astype(F32)).astype(BF16)


def mxu(a, b):
    return jnp.dot(a, b, preferred_element_type=F32)


def iota(shape, dim):
    return lax.broadcasted_iota(jnp.int32, shape, dim)


def column(table, index):
    return jnp.broadcast_to(table[:, index : index + 1], (LANES, LANES))


def shift_up(values, last):
    rolled = pltpu.roll(values, LANES - 1, 0)
    return jnp.where(iota(values.shape, 0) == LANES - 1, last, rolled)


def shift_down(values, first):
    return jnp.where(iota(values.shape, 0) == 0, first, pltpu.roll(values, 1, 0))


def chain_tables(blocks_x, blocks_y, sx, sy, tab, rows_in):
    count = blocks_x + blocks_y
    shape = (count, LANES)
    lane, row = iota(shape, 1), iota(shape, 0)
    first = (lane == 0) & ((row == 0) | (row == blocks_x))

    def prev(values, fill):
        rolled = pltpu.roll(values, 1, 1)
        return jnp.where(first, fill, jnp.where(lane == 0, pltpu.roll(rolled, 1, 0), rolled))

    def following(values):
        rolled = pltpu.roll(values, LANES - 1, 1)
        return jnp.where(lane == LANES - 1, pltpu.roll(rolled, count - 1, 0), rolled)

    def halves(start):
        return jnp.concatenate(
            [sx[pl.ds(start, blocks_x, stride=2), :], sy[pl.ds(start, blocks_y, stride=2), :]], axis=0
        )

    fine = jnp.concatenate([halves(0), halves(1)], axis=1)
    node, place = iota((FINE, FINE), 0), iota((FINE, FINE), 1)
    pick = jnp.where(place < LANES, 2 * place, 2 * (place - LANES) + 1)
    parts = jnp.dot((fine), (node == pick).astype(F32), precision=HIGHEST, preferred_element_type=F32)
    c, d = parts[:, :LANES], parts[:, LANES:]
    span = c + d
    a, b = prev(c, 0.0), prev(d, 0.0)
    span_before = prev(span, 1.0)
    inverse = 1.0 / span
    inverse_before = 1.0 / span_before
    tab[0] = d * inverse
    tab[1] = c * inverse
    tab[2] = a * a * inverse_before * (1.0 / 6.0)
    tab[3] = a * (1.0 / 3.0) + b * (1.0 / 6.0)
    tab[4] = (a * b * inverse_before + c * d * inverse) * (1.0 / 6.0) + (b + c) * (1.0 / 3.0)
    tab[5] = c * (1.0 / 6.0) + d * (1.0 / 3.0)
    tab[6] = d * d * inverse * (1.0 / 6.0)
    tab[9] = b * inverse_before
    tab[10] = a * inverse_before

    rho = 1.0 / (stiffness_weight * inverse - span * (1.0 / 6.0))
    rho_before = prev(rho, 0.0)
    mu = 0.5 * (a + b + span)
    mu_after = following(mu)
    one = jnp.ones(shape, F32)
    fwd = (one + mu * rho_before, mu, rho_before, one)
    bwd = (one, mu_after, rho, one + rho * mu_after)
    step = 1
    while step < LANES:
        def join(m, shift, outside):
            fill = (1.0, 0.0, 0.0, 1.0)
            a1, b1, c1, d1 = m
            a0, b0, c0, d0 = (
                jnp.where(outside, f, pltpu.roll(v, shift, 1)) for v, f in zip(m, fill)
            )
            return (a1 * a0 + b1 * c0, a1 * b0 + b1 * d0, c1 * a0 + d1 * c0, c1 * b0 + d1 * d0)

        fwd = join(fwd, step, lane < step)
        bwd = join(bwd, LANES - step, lane >= LANES - step)
        step *= 2
    ends = [jnp.broadcast_to(v[:, LANES - 1 : LANES], shape) for v in fwd]
    starts = [jnp.broadcast_to(v[:, 0:1], shape) for v in bwd]
    for low, size in ((0, blocks_x), (blocks_x, blocks_y)):
        y = jnp.zeros((1, LANES), F32)
        for q in range(low, low + size):
            rows_in[0, q : q + 1, :] = y
            at, bt, ct, dt = (v[q : q + 1, :] for v in ends)
            y = (at * y + bt) / (ct * y + dt)
        z = None
        for q in reversed(range(low, low + size)):
            at, bt, ct, dt = (v[q : q + 1, :] for v in starts)
            if z is None:
                rows_in[1, q : q + 1, :] = jnp.ones((1, LANES), F32)
                rows_in[2, q : q + 1, :] = jnp.zeros((1, LANES), F32)
                z = at / ct
            else:
                rows_in[1, q : q + 1, :] = z
                rows_in[2, q : q + 1, :] = jnp.ones((1, LANES), F32)
                z = (at * z + bt) / (ct * z + dt)
    y_in, z_num, z_den = rows_in[0], rows_in[1], rows_in[2]
    den = fwd[2] * y_in + fwd[3]
    left = (fwd[0] * y_in + fwd[1]) / den
    right = (bwd[0] * z_num + bwd[1] * z_den) / (bwd[2] * z_num + bwd[3] * z_den)
    green = operator_divisor / (left + right)
    tab[7] = green / den
    tab[8] = den
    tab[11] = 1.0 / jnp.broadcast_to(den[:, LANES - 1 : LANES], shape)
    tab[12] = 1.0 / jnp.broadcast_to(green[:, LANES - 1 : LANES], shape)
    tab[13] = 1.0 / jnp.broadcast_to(den[:, 0:1], shape)


def weights_between(gain, low, size, own, forward, backward):
    q = iota((size, LANES), 0)
    ahead = jnp.ones((size, LANES), F32)
    behind = jnp.ones((size, LANES), F32)
    for m in range(size):
        g = gain[low + m : low + m + 1, :]
        ahead = ahead * jnp.where((m > q) & (m < own), g, 1.0)
        behind = behind * jnp.where((m < q) & (m > own), g, 1.0)
    forward[low : low + size, :] = jnp.where(q < own, ahead, 0.0)
    backward[low : low + size, :] = jnp.where(q > own, behind, 0.0)


def green_block(u_col, w_col, u_row, w_row):
    i, j = iota((LANES, LANES), 0), iota((LANES, LANES), 1)
    return jnp.where(i >= j, u_col * w_row, w_col * u_row)


def prepare_kernel(
    nx, ny, dens, sx_in, sy_in,
    colx, ycoef, scal, cf, cb, wcat, gxh, gxl, rh, er, lch, lcl, packed, box,
    sx, sy, rsend, to_right, to_left, rrecv, from_left, from_right, tiles,
    tab, rows_in, stack, wfine, load_sem, send_sem, recv_sem,
):
    p, r = lax.axis_index("gx"), lax.axis_index("gy")
    up, down = lax.rem(p + nx - 1, nx), lax.rem(p + 1, nx)
    left, right = lax.rem(r + ny - 1, ny), lax.rem(r + 1, ny)
    loads = []
    for k in range(PLANES // STEP):
        part = pl.ds(k * STEP, STEP)
        for t in range(2):
            loads.append(
                pltpu.make_async_copy(
                    dens.at[part, :, pl.ds(t * LANES, LANES)], box.at[t, part], load_sem.at[2 * k + t]
                )
            )
            loads[-1].start()
    for k, (src, dst) in enumerate(((sx_in, sx), (sy_in, sy))):
        loads.append(pltpu.make_async_copy(src, dst, load_sem.at[2 * PLANES // STEP + k]))
        loads[-1].start()
    barrier = pltpu.get_barrier_semaphore()
    for i in (up, p, down):
        for j in (left, r, right):
            if i is p and j is r:
                continue
            pl.semaphore_signal(barrier, inc=1, device_id=(i, j), device_id_type=MESH)

    right_rows, left_rows = FINE // 2, FINE // 4
    lane_r, lane_l = iota((right_rows, LANES), 1), iota((left_rows, LANES), 1)
    to_right[...] = jnp.zeros((right_rows, LANES), F32)
    to_left[...] = jnp.zeros((left_rows, LANES), F32)
    for k in range(PLANES // STEP):
        loads[2 * k].wait()
        loads[2 * k + 1].wait()
        acc_r, acc_l = to_right[...], to_left[...]
        for zi in range(STEP):
            z = k * STEP + zi
            for m in range(2):
                rows = slice(m * right_rows, (m + 1) * right_rows)
                at = 2 * m * PLANES + z
                acc_r = jnp.where(lane_r == at, box[1, z, rows, LANES - 2 : LANES - 1], acc_r)
                acc_r = jnp.where(lane_r == at + PLANES, box[1, z, rows, LANES - 1 : LANES], acc_r)
            for m in range(4):
                rows = slice(m * left_rows, (m + 1) * left_rows)
                acc_l = jnp.where(lane_l == m * PLANES + z, box[0, z, rows, 0:1], acc_l)
            for t in range(2):
                rsend[0, t, z : z + 1, :] = box[t, z, FINE - 2 : FINE - 1, :]
                rsend[1, t, z : z + 1, :] = box[t, z, FINE - 1 : FINE, :]
                rsend[2, t, z : z + 1, :] = box[t, z, 0:1, :]
        to_right[...] = acc_r
        to_left[...] = acc_l

    pl.semaphore_wait(barrier, 8)
    top = pl.ds(0, 8)
    end_r, end_l = pl.ds(right_rows - 8, 8), pl.ds(left_rows - 8, 8)
    plan = (
        (to_right, from_left, p, right),
        (to_left, from_right, p, left),
        (rsend.at[pl.ds(0, 2)], rrecv.at[pl.ds(0, 2)], down, r),
        (rsend.at[pl.ds(2, 1)], rrecv.at[pl.ds(2, 1)], up, r),
        (to_left.at[end_l], tiles.at[0], down, r),
        (to_left.at[top], tiles.at[1], up, r),
        (to_right.at[end_r], tiles.at[2], down, right),
        (to_left.at[end_l], tiles.at[3], down, left),
        (to_right.at[top], tiles.at[4], up, right),
        (to_left.at[top], tiles.at[5], up, left),
    )
    copies = []
    for k, (src, dst, i, j) in enumerate(plan):
        copies.append(
            pltpu.make_async_remote_copy(
                src_ref=src, dst_ref=dst, send_sem=send_sem.at[k], recv_sem=recv_sem.at[k],
                device_id=(i, j), device_id_type=MESH,
            )
        )
        copies[-1].start()

    for load in loads[2 * PLANES // STEP :]:
        load.wait()
    chain_tables(nx, ny, sx, sy, tab, rows_in)
    weights_between(tab[11], 0, nx, p, cf, cb)
    weights_between(tab[11], nx, ny, r, cf, cb)
    row_x, row_y = pl.ds(p, 1), pl.ds(nx + r, 1)
    ux, wx, uy, wy = tab[7, row_x, :], tab[8, row_x, :], tab[7, row_y, :], tab[8, row_y, :]
    stack[...] = jnp.zeros((LANES, LANES), F32)
    for k in range(7):
        stack[k : k + 1, :] = tab[k, row_x, :]
    stack[X_U : X_U + 1, :] = ux
    stack[X_PSI : X_PSI + 1, :] = wx * tab[11, row_x, :]
    stack[X_W : X_W + 1, :] = wx
    for k in range(5):
        stack[Y_K1 + k : Y_K1 + k + 1, :] = tab[2 + k, row_y, :]
    stack[Y_U : Y_U + 1, :] = uy
    stack[Y_W : Y_W + 1, :] = wy
    cols = stack[...].T
    colx[...] = cols
    scal[...] = jnp.zeros((8, LANES), F32)
    scal[S_FX : S_FX + 1, :] = tab[12, row_x, :]
    scal[S_BX : S_BX + 1, :] = tab[13, row_x, :]
    scal[S_FY : S_FY + 1, :] = tab[12, row_y, :]
    scal[S_BY : S_BY + 1, :] = tab[13, row_y, :]
    wl_x = tab[9, row_x, :][:, 0:1]
    wr_x = tab[10, row_x, :][:, 0:1]
    wl_y = tab[9, row_y, :][:, 0:1]
    wr_y = tab[10, row_y, :][:, 0:1]
    scal[S_WRM : S_WRM + 1, :] = jnp.broadcast_to(wr_x, (1, LANES))
    scal[S_UY : S_UY + 1, :] = uy
    scal[S_PSIY : S_PSIY + 1, :] = wy * tab[11, row_y, :]

    lane_z = iota((PLANES, LANES), 1)
    for k, index in enumerate((X_U, X_PSI)):
        packed[k] = sum(
            jnp.where(lane_z // PLANES == m, cols[m * PLANES : (m + 1) * PLANES, index : index + 1], 0.0)
            for m in range(LANES // PLANES)
        )

    odd_row = (iota((1, LANES), 1) & 1) == 1
    ycoef[...] = jnp.zeros((8, FINE), F32)
    for t in range(2):
        h = sy[pl.ds(2 * r + t, 1), :]
        hp = pltpu.roll(h, 1, 1)
        inv = 1.0 / (h + hp)
        ycoef[0:1, t * LANES : (t + 1) * LANES] = jnp.where(odd_row, h * inv, 0.0)
        ycoef[1:2, t * LANES : (t + 1) * LANES] = jnp.where(odd_row, hp * inv, 0.0)

    hi, lo = split(green_block(column(cols, X_U), column(cols, X_W), ux, wx))
    gxh[...] = hi
    gxl[...] = lo
    gy = green_block(column(cols, Y_U), column(cols, Y_W), uy, wy)
    g1, g2, g3, g4, g5 = (column(cols, Y_K1 + k) * gy for k in range(5))
    wfine[pl.ds(0, LANES, stride=2), :] = g3 + shift_down(g5, 0.0) + shift_up(g1, 0.0)
    wfine[pl.ds(1, LANES, stride=2), :] = g4 + shift_up(g2, 0.0)
    i = iota((LANES, LANES), 0)
    outer = jnp.where(
        i < PLANES, g1[0:1, :],
        jnp.where(i < 2 * PLANES, g2[0:1, :], jnp.where(i < 3 * PLANES, g5[LANES - 1 : LANES, :], 0.0)),
    )
    hi, lo = split(wfine[...])
    wcat[0:FINE, 0:LANES] = hi
    wcat[0:FINE, LANES:FINE] = lo
    hi, lo = split(outer)
    wcat[FINE : FINE + LANES, 0:LANES] = hi
    wcat[FINE : FINE + LANES, LANES:FINE] = lo

    for copy in copies:
        copy.wait()

    has_up = (p > 0).astype(F32)
    has_down = (p < nx - 1).astype(F32)
    has_left = (r > 0).astype(F32)
    has_right = (r < ny - 1).astype(F32)
    lane_8 = iota((8, LANES), 1)
    lane = iota((LANES, LANES), 1)

    def unpack(ref, start, shifts):
        values = ref[pl.ds(start, LANES // len(shifts), stride=2), :]
        return jnp.concatenate([pltpu.roll(values, n, 1) if n else values for n in shifts], axis=0)

    e_c, o_c = (
        jnp.where(
            lane < 2 * PLANES,
            unpack(from_left, start, (0, 64)) * has_left,
            unpack(from_right, start, (64, 32, 0, 96)) * has_right,
        )
        for start in range(2)
    )
    own = unpack(to_left, 0, (32, 0, 96, 64))
    own_n = pltpu.roll(tiles[0], 64, 1) * has_up
    own_s = pltpu.roll(tiles[1], 32, 1) * has_down
    north = (
        jnp.where(
            lane_8 < 2 * PLANES,
            pltpu.roll(tiles[2], 64, 1) * has_left,
            pltpu.roll(tiles[3], 96, 1) * has_right,
        )
        * has_up
    )
    south = (
        jnp.where(lane_8 < 2 * PLANES, tiles[4] * has_left, pltpu.roll(tiles[5], 64, 1) * has_right)
        * has_down
    )

    def along_y(values, own_values):
        at = iota(values.shape, 1)
        guess = wl_y * pltpu.roll(values, PLANES, 1) + wr_y * own_values
        return jnp.where((at >= PLANES) & (at < 2 * PLANES), guess, values)

    se = along_y(e_c, own)
    se_n = along_y(north, own_n)[6:7, :]
    se_s = along_y(south, own_s)[0:1, :]
    do = o_c - (column(cols, X_WL) * se + column(cols, X_WR) * shift_up(se, se_s))
    de = e_c - se
    de_n = north[6:7, :] - se_n
    do_n = north[7:8, :] - (wl_x * se_n + wr_x * se[0:1, :])
    de_s = south[0:1, :] - se_s
    loads_c = (
        column(cols, X_K1) * shift_down(de, de_n)
        + column(cols, X_K2) * shift_down(do, do_n)
        + column(cols, X_K3) * de
        + column(cols, X_K4) * do
        + column(cols, X_K5) * shift_up(de, de_s)
    )
    hi, lo = split(loads_c)
    lch[...] = hi
    lcl[...] = lo
    er[...] = e_c

    stack[0:8, :] = north
    stack[8:16, :] = south
    corner = stack[...].T
    corner_n = corner[2 * PLANES : 3 * PLANES, 6:7]
    corner_s = corner[2 * PLANES : 3 * PLANES, 8:9]
    odd = (lane_z & 1) == 1

    def row_along_y(layer, scale, corner_col):
        tiles_in = [layer[t] * scale for t in range(2)]
        next_in = [pltpu.roll(v, LANES - 1, 1) for v in tiles_in]
        after = [
            jnp.where(lane_z < LANES - 1, next_in[0], next_in[1]),
            jnp.where(lane_z < LANES - 1, next_in[1], corner_col),
        ]
        result = []
        for t in range(2):
            part = slice(t * LANES, (t + 1) * LANES)
            guess = ycoef[0:1, part] * pltpu.roll(tiles_in[t], 1, 1) + ycoef[1:2, part] * after[t]
            result.append(jnp.where(odd, guess, tiles_in[t]))
        return tiles_in, result

    e_n, s_n = row_along_y(rrecv[0], has_up, corner_n)
    e_s, s_s = row_along_y(rrecv[2], has_down, corner_s)
    for t in range(2):
        rh[0, t] = e_n[t] - s_n[t]
        rh[1, t] = rrecv[1, t] * has_up - wl_x * s_n[t]
        rh[2, t] = s_s[t]
        rh[3, t] = e_s[t] - s_s[t]


def main_kernel(
    box, colx, ycoef, scal, rh, er, lch, lcl, wcat, gxh, gxl,
    detail, local, coarse, wide, se_buf, de_buf, do_buf, woven, high, low, sem,
):
    for k in range(7):
        wide[k] = column(colx[...], k)
    lane = iota((LANES, LANES), 1)
    odd = (lane & 1) == 1
    inner = lane < LANES - 1
    pick = (2 * lane) & (LANES - 1)
    wrm = scal[S_WRM : S_WRM + 1, :]
    body, before, after = pl.ds(8, LANES), pl.ds(7, LANES), pl.ds(9, LANES)
    turns = PLANES // PER

    def stencil(z, k, slot):
        row = pl.ds(z, 1)
        e = [box[t, z, pl.ds(0, LANES, stride=2), :] for t in range(2)]
        o = [box[t, z, pl.ds(1, LANES, stride=2), :] for t in range(2)]
        nxt = [pltpu.roll(v, LANES - 1, 1) for v in e]
        beyond = pltpu.roll(er[...], lax.rem(3 * LANES - 1 - 2 * PLANES - z, LANES), 1)
        nxt = [jnp.where(inner, nxt[0], nxt[1]), jnp.where(inner, nxt[1], beyond)]
        for t in range(2):
            part = slice(t * LANES, (t + 1) * LANES)
            guess = ycoef[0:1, part] * pltpu.roll(e[t], 1, 1) + ycoef[1:2, part] * nxt[t]
            se = jnp.where(odd, guess, e[t])
            de = e[t] - se
            se_buf[k, t, body, :] = se
            se_buf[k, t, pl.ds(8 + LANES, 1), :] = rh[2, t, row, :]
            do = o[t] - (wide[X_WL] * se + wide[X_WR] * se_buf[k, t, after, :])
            woven[slot, k, t, pl.ds(0, LANES, stride=2), :] = de
            woven[slot, k, t, pl.ds(1, LANES, stride=2), :] = do
            de_buf[k, t, body, :] = de
            de_buf[k, t, pl.ds(7, 1), :] = rh[0, t, row, :]
            de_buf[k, t, pl.ds(8 + LANES, 1), :] = rh[3, t, row, :]
            do_buf[k, t, body, :] = do
            do_buf[k, t, pl.ds(7, 1), :] = rh[1, t, row, :] - wrm * se[0:1, :]
            load = (
                wide[X_K3] * de
                + wide[X_K4] * do
                + wide[X_K1] * de_buf[k, t, before, :]
                + wide[X_K2] * do_buf[k, t, before, :]
                + wide[X_K5] * de_buf[k, t, after, :]
            )
            hi, lo = split(load)
            high[slot, k, :, part] = hi
            low[slot, k, :, part] = lo
        coarse[z] = jnp.where(
            lane < LANES // 2,
            jnp.take_along_axis(e[0], pick, axis=1, mode="promise_in_bounds"),
            jnp.take_along_axis(e[1], pick, axis=1, mode="promise_in_bounds"),
        )
        mine = (lane & (PLANES - 1)) == z
        high[slot, k, :, FINE:] = jnp.where(mine, lch[...].astype(F32), 0.0).astype(BF16)
        low[slot, k, :, FINE:] = jnp.where(mine, lcl[...].astype(F32), 0.0).astype(BF16)

    def solve(z, slot):
        pairs = []
        for k in range(0, PER, 2):
            pair = []
            for n in (k, k + 1):
                both = mxu(high[slot, n], wcat[...])
                rest = mxu(low[slot, n], wcat[:, 0:LANES])
                pair.append(both[:, :LANES] + both[:, LANES:] + rest)
            pairs.append(jnp.concatenate(pair, axis=1))
        for k in range(0, PER, 2):
            hi, lo = split(pairs[k // 2])
            solved = mxu(gxh[...], hi) + (mxu(gxh[...], lo) + mxu(gxl[...], hi))
            local[z + k] = solved[:, :LANES]
            local[z + k + 1] = solved[:, LANES:]

    def writes(it, slot):
        return [
            pltpu.make_async_copy(
                woven.at[slot, :, t],
                detail.at[pl.ds(PER * it, PER), :, pl.ds(t * LANES, LANES)],
                sem.at[slot, t],
            )
            for t in range(2)
        ]

    def step(it, carry):
        slot = lax.rem(it, 2)

        @pl.when(it >= 2)
        def _():
            for write in writes(it - 2, slot):
                write.wait()

        solve(PER * it - PER, 1 - slot)
        for k in range(PER):
            stencil(PER * it + k, k, slot)
        for write in writes(it, slot):
            write.start()
        return carry

    for k in range(PER):
        stencil(k, k, 0)
    for write in writes(0, 0):
        write.start()
    lax.fori_loop(1, turns, step, 0)
    solve(PLANES - PER, (turns - 1) % 2)
    for it in (turns - 2, turns - 1):
        for write in writes(it, it % 2):
            write.wait()


def exchange_kernel(
    nx, ny, local, coarse, colx, scal, cf, cb, packed, mid, outer_l, outer_r,
    xs, xr, ys, yr, cs, cr, sums, uwide, pwide, sx_sem, rx_sem, sy_sem, ry_sem, sc_sem, rc_sem,
):
    p, r = lax.axis_index("gx"), lax.axis_index("gy")
    barrier = pltpu.get_barrier_semaphore()
    for k in range(1, nx):
        pl.semaphore_signal(barrier, inc=1, device_id=(lax.rem(p + k, nx), r), device_id_type=MESH)
    for k in range(1, ny):
        pl.semaphore_signal(barrier, inc=1, device_id=(p, lax.rem(r + k, ny)), device_id_type=MESH)
    xs[0] = local[:, LANES - 1, :] * scal[S_FX : S_FX + 1, :]
    xs[1] = local[:, 0, :] * scal[S_BX : S_BX + 1, :]
    uwide[...] = column(colx[...], X_U)
    pwide[...] = column(colx[...], X_PSI)

    def start(sent, got, send_sem, recv_sem, own, count, target):
        copies = []
        for k in range(1, count):
            wraps = jnp.where(own + k >= count, 1, 0)
            copies.append(
                pltpu.make_async_remote_copy(
                    src_ref=sent.at[wraps], dst_ref=got.at[k - 1],
                    send_sem=send_sem.at[k - 1], recv_sem=recv_sem.at[k - 1],
                    device_id=target(lax.rem(own + k, count)), device_id_type=MESH,
                )
            )
            copies[-1].start()
        return copies

    def gather(copies, got, own, count, low):
        forward = backward = 0.0
        for k in range(1, count):
            copies[k - 1].wait_recv()
            row = pl.ds(low + lax.rem(own + count - k, count), 1)
            values = got[k - 1]
            forward = forward + cf[row, :] * values
            backward = backward + cb[row, :] * values
        return forward, backward

    lane = iota((PLANES, LANES), 1)
    blocks = LANES // PLANES

    def edges(z, carry):
        last, head = carry
        for m in range(blocks):
            block = local[z, pl.ds(m * PLANES, PLANES), :]
            here = lane == m * PLANES + z
            last = jnp.where(here, block[:, LANES - 1 : LANES], last)
            head = jnp.where(here, block[:, 0:1], head)
        return last, head

    zero = jnp.zeros((PLANES, LANES), F32)
    last, head = lax.fori_loop(0, PLANES, edges, (zero, zero), unroll=4)
    scale_f, scale_b = scal[S_FY : S_FY + 1, :], scal[S_BY : S_BY + 1, :]
    ys[0] = last * scale_f
    ys[1] = head * scale_b
    pl.semaphore_wait(barrier, nx + ny - 2)
    x_copies = start(xs, xr, sx_sem, rx_sem, p, nx, lambda i: (i, r))
    y_copies = start(ys, yr, sy_sem, ry_sem, r, ny, lambda j: (p, j))

    forward, backward = gather(x_copies, xr, p, nx, 0)
    sums[0] = forward
    sums[1] = backward
    across_f = jnp.concatenate([forward] * blocks, axis=0).T
    across_b = jnp.concatenate([backward] * blocks, axis=0).T
    end = slice(LANES - 1, LANES)
    cs[...] = jnp.zeros((2, 8, LANES), F32)
    cs[0, 0:1, :] = across_f[end, :] * scale_f
    cs[0, 1:2, :] = across_b[end, :] * scale_f
    cs[1, 0:1, :] = across_f[0:1, :] * scale_b
    cs[1, 1:2, :] = across_b[0:1, :] * scale_b
    c_copies = start(cs, cr, sc_sem, rc_sem, r, ny, lambda j: (p, j))

    edge = jnp.where(
        (iota((LANES, LANES), 0) // PLANES) % 2 == 0,
        scal[S_UY : S_UY + 1, :], scal[S_PSIY : S_PSIY + 1, :],
    )
    edge_h = edge.astype(BF16).astype(F32)
    edge_l = edge - edge_h
    plane_of = iota((LANES, LANES), 0) % PLANES

    def x_part(z, carry):
        row = pl.ds(z, 1)
        mid[z] = local[z] + coarse[z] + uwide[...] * sums[0, row, :] + pwide[...] * sums[1, row, :]
        outer_r[z, 0:LANES, :] = jnp.where(plane_of == z, edge_h, 0.0).astype(BF16)
        outer_r[z, LANES:, :] = jnp.where(plane_of == z, edge_l, 0.0).astype(BF16)
        return carry

    lax.fori_loop(0, PLANES, x_part, 0, unroll=2)
    u_x, psi_x = packed[0], packed[1]
    forward, backward = gather(y_copies, yr, r, ny, nx)
    extra_f, extra_b = gather(c_copies, cr, r, ny, nx)
    forward = forward + u_x * extra_f[0:1, :] + psi_x * extra_f[1:2, :]
    backward = backward + u_x * extra_b[0:1, :] + psi_x * extra_b[1:2, :]
    lane = iota((LANES, LANES), 1)

    def spread(values):
        return jnp.concatenate(
            [pltpu.roll(values, (LANES - m * PLANES) % LANES, 1) if m else values for m in range(blocks)],
            axis=0,
        )

    both = jnp.where(lane < PLANES, spread(forward), pltpu.roll(spread(backward), PLANES, 1))
    high = both.astype(BF16).astype(F32)
    both = jnp.where(lane < 2 * PLANES, high, pltpu.roll(both - high, 2 * PLANES, 1))
    outer_l[:, 0:LANES] = both.astype(BF16)
    outer_l[:, LANES:] = both.astype(BF16)
    for copy in x_copies + y_copies + c_copies:
        copy.wait_send()


def final_kernel(mid, outer_l, outer_r, out):
    for z in range(0, mid.shape[0], 2):
        pair = jnp.concatenate([outer_r[z], outer_r[z + 1]], axis=1)
        update = mxu(outer_l[...], pair)
        out[z] = mid[z] + update[:, :LANES]
        out[z + 1] = mid[z + 1] + update[:, LANES:]


def per_device(nx, ny, density, spacing_x, spacing_y):
    blocks = nx + ny
    hbm = pl.BlockSpec(memory_space=pltpu.HBM)
    vmem = pl.BlockSpec(memory_space=pltpu.VMEM)
    f32 = lambda *shape: jax.ShapeDtypeStruct(shape, F32)
    bf16 = lambda *shape: jax.ShapeDtypeStruct(shape, BF16)
    sx = spacing_x.reshape(2 * nx, LANES)
    sy = spacing_y.reshape(2 * ny, LANES)
    colx, ycoef, scal, cf, cb, wcat, gxh, gxl, rh, er, lch, lcl, packed, box = pl.pallas_call(
        functools.partial(prepare_kernel, nx, ny),
        out_shape=(
            f32(LANES, LANES), f32(8, FINE), f32(8, LANES), f32(blocks, LANES), f32(blocks, LANES),
            bf16(FINE + LANES, FINE), bf16(LANES, LANES), bf16(LANES, LANES),
            f32(4, 2, PLANES, LANES), f32(LANES, LANES), bf16(LANES, LANES), bf16(LANES, LANES),
            f32(2, PLANES, LANES), f32(2, PLANES, FINE, LANES),
        ),
        in_specs=[hbm] * 3,
        out_specs=(vmem,) * 14,
        scratch_shapes=[
            pltpu.VMEM((2 * nx, LANES), F32),
            pltpu.VMEM((2 * ny, LANES), F32),
            pltpu.VMEM((3, 2, PLANES, LANES), F32),
            pltpu.VMEM((FINE // 2, LANES), F32),
            pltpu.VMEM((FINE // 4, LANES), F32),
            pltpu.VMEM((3, 2, PLANES, LANES), F32),
            pltpu.VMEM((FINE // 2, LANES), F32),
            pltpu.VMEM((FINE // 4, LANES), F32),
            pltpu.VMEM((6, 8, LANES), F32),
            pltpu.VMEM((14, blocks, LANES), F32),
            pltpu.VMEM((3, blocks, LANES), F32),
            pltpu.VMEM((LANES, LANES), F32),
            pltpu.VMEM((FINE, LANES), F32),
            pltpu.SemaphoreType.DMA((2 * PLANES // STEP + 2,)),
            pltpu.SemaphoreType.DMA((10,)),
            pltpu.SemaphoreType.DMA((10,)),
        ],
        compiler_params=pltpu.CompilerParams(
            collective_id=0, has_side_effects=True, vmem_limit_bytes=32 * MIB
        ),
        name="prepare",
    )(*(pltpu.with_memory_space_constraint(v, pltpu.HBM) for v in (density, sx, sy)))
    tables = (colx, ycoef, scal, rh, er, lch, lcl, wcat, gxh, gxl)
    detail, local, coarse = pl.pallas_call(
        main_kernel,
        out_shape=(f32(PLANES, FINE, FINE), f32(PLANES, LANES, LANES), f32(PLANES, LANES, LANES)),
        in_specs=[vmem] * (1 + len(tables)),
        out_specs=(hbm, vmem, vmem),
        scratch_shapes=[
            pltpu.VMEM((7, LANES, LANES), F32),
            pltpu.VMEM((PER, 2, LANES + 16, LANES), F32),
            pltpu.VMEM((PER, 2, LANES + 16, LANES), F32),
            pltpu.VMEM((PER, 2, LANES + 16, LANES), F32),
            pltpu.VMEM((2, PER, 2, FINE, LANES), F32),
            pltpu.VMEM((2, PER, LANES, FINE + LANES), BF16),
            pltpu.VMEM((2, PER, LANES, FINE + LANES), BF16),
            pltpu.SemaphoreType.DMA((2, 2)),
        ],
        compiler_params=pltpu.CompilerParams(vmem_limit_bytes=32 * MIB),
        name="main",
    )(box, *tables)
    mid, outer_l, outer_r = pl.pallas_call(
        functools.partial(exchange_kernel, nx, ny),
        out_shape=(f32(PLANES, LANES, LANES), bf16(LANES, FINE), bf16(PLANES, FINE, LANES)),
        in_specs=[vmem] * 7,
        out_specs=(vmem,) * 3,
        scratch_shapes=[
            pltpu.VMEM((2, PLANES, LANES), F32),
            pltpu.VMEM((nx - 1, PLANES, LANES), F32),
            pltpu.VMEM((2, PLANES, LANES), F32),
            pltpu.VMEM((ny - 1, PLANES, LANES), F32),
            pltpu.VMEM((2, 8, LANES), F32),
            pltpu.VMEM((ny - 1, 8, LANES), F32),
            pltpu.VMEM((2, PLANES, LANES), F32),
            pltpu.VMEM((LANES, LANES), F32),
            pltpu.VMEM((LANES, LANES), F32),
            pltpu.SemaphoreType.DMA((nx - 1,)),
            pltpu.SemaphoreType.DMA((nx - 1,)),
            pltpu.SemaphoreType.DMA((ny - 1,)),
            pltpu.SemaphoreType.DMA((ny - 1,)),
            pltpu.SemaphoreType.DMA((ny - 1,)),
            pltpu.SemaphoreType.DMA((ny - 1,)),
        ],
        compiler_params=pltpu.CompilerParams(
            collective_id=1, has_side_effects=True, vmem_limit_bytes=32 * MIB
        ),
        name="exchange",
    )(local, coarse, colx, scal, cf, cb, packed)
    coarse_new = pl.pallas_call(
        final_kernel,
        grid=(PLANES // 8,),
        out_shape=f32(PLANES, LANES, LANES),
        in_specs=[
            pl.BlockSpec((8, LANES, LANES), lambda g: (g, 0, 0)),
            pl.BlockSpec((LANES, FINE), lambda g: (0, 0)),
            pl.BlockSpec((8, FINE, LANES), lambda g: (g, 0, 0)),
        ],
        out_specs=pl.BlockSpec((8, LANES, LANES), lambda g: (g, 0, 0)),
        compiler_params=pltpu.CompilerParams(vmem_limit_bytes=32 * MIB),
        name="final",
    )(mid, outer_l, outer_r)
    return detail, coarse_new


def solution(mesh):
    placed = P(None, "gx", "gy")
    return jax.shard_map(
        functools.partial(per_device, mesh.shape["gx"], mesh.shape["gy"]),
        mesh=mesh,
        in_specs=(placed, P(), P()),
        out_specs=(placed, placed),
        check_vma=False,
    )
```

```python
import functools

import jax
import jax.numpy as jnp
from jax import lax
from jax.experimental import pallas as pl
from jax.experimental.pallas import tpu as pltpu
from jax.sharding import PartitionSpec as P

MESH = pl.DeviceIdType.MESH
F32 = jnp.float32
BF16 = jnp.bfloat16
HIGHEST = lax.Precision.HIGHEST
stiffness_weight = 4096.0
operator_divisor = 32.0
LANES = 128
FINE = 256
PLANES = 32
PER = 8
STEP = 4
MIB = 1 << 20
X_WL, X_WR, X_K1, X_K2, X_K3, X_K4, X_K5, X_U, X_PSI, X_W = range(10)
Y_K1, Y_K2, Y_K3, Y_K4, Y_K5, Y_U, Y_W = range(10, 17)
S_FX, S_BX, S_FY, S_BY, S_WRM, S_UY, S_PSIY = range(7)


def split(values):
    high = values.astype(BF16)
    return high, (values - high.astype(F32)).astype(BF16)


def mxu(a, b):
    return jnp.dot(a, b, preferred_element_type=F32)


def iota(shape, dim):
    return lax.broadcasted_iota(jnp.int32, shape, dim)


def column(table, index):
    return jnp.broadcast_to(table[:, index : index + 1], (LANES, LANES))


def shift_up(values, last):
    rolled = pltpu.roll(values, LANES - 1, 0)
    return jnp.where(iota(values.shape, 0) == LANES - 1, last, rolled)


def shift_down(values, first):
    return jnp.where(iota(values.shape, 0) == 0, first, pltpu.roll(values, 1, 0))


def chain_tables(blocks_x, blocks_y, sx, sy, tab, rows_in):
    count = blocks_x + blocks_y
    shape = (count, LANES)
    lane, row = iota(shape, 1), iota(shape, 0)
    first = (lane == 0) & ((row == 0) | (row == blocks_x))

    def prev(values, fill):
        rolled = pltpu.roll(values, 1, 1)
        return jnp.where(first, fill, jnp.where(lane == 0, pltpu.roll(rolled, 1, 0), rolled))

    def following(values):
        rolled = pltpu.roll(values, LANES - 1, 1)
        return jnp.where(lane == LANES - 1, pltpu.roll(rolled, count - 1, 0), rolled)

    def halves(start):
        return jnp.concatenate(
            [sx[pl.ds(start, blocks_x, stride=2), :], sy[pl.ds(start, blocks_y, stride=2), :]], axis=0
        )

    fine = jnp.concatenate([halves(0), halves(1)], axis=1)
    node, place = iota((FINE, FINE), 0), iota((FINE, FINE), 1)
    pick = jnp.where(place < LANES, 2 * place, 2 * (place - LANES) + 1)
    parts = jnp.dot((fine), (node == pick).astype(F32), precision=HIGHEST, preferred_element_type=F32)
    c, d = parts[:, :LANES], parts[:, LANES:]
    span = c + d
    a, b = prev(c, 0.0), prev(d, 0.0)
    span_before = prev(span, 1.0)
    inverse = 1.0 / span
    inverse_before = 1.0 / span_before
    tab[0] = d * inverse
    tab[1] = c * inverse
    tab[2] = a * a * inverse_before * (1.0 / 6.0)
    tab[3] = a * (1.0 / 3.0) + b * (1.0 / 6.0)
    tab[4] = (a * b * inverse_before + c * d * inverse) * (1.0 / 6.0) + (b + c) * (1.0 / 3.0)
    tab[5] = c * (1.0 / 6.0) + d * (1.0 / 3.0)
    tab[6] = d * d * inverse * (1.0 / 6.0)
    tab[9] = b * inverse_before
    tab[10] = a * inverse_before

    rho = 1.0 / (stiffness_weight * inverse - span * (1.0 / 6.0))
    rho_before = prev(rho, 0.0)
    mu = 0.5 * (a + b + span)
    mu_after = following(mu)
    one = jnp.ones(shape, F32)
    fwd = (one + mu * rho_before, mu, rho_before, one)
    bwd = (one, mu_after, rho, one + rho * mu_after)
    step = 1
    while step < LANES:
        def join(m, shift, outside):
            fill = (1.0, 0.0, 0.0, 1.0)
            a1, b1, c1, d1 = m
            a0, b0, c0, d0 = (
                jnp.where(outside, f, pltpu.roll(v, shift, 1)) for v, f in zip(m, fill)
            )
            return (a1 * a0 + b1 * c0, a1 * b0 + b1 * d0, c1 * a0 + d1 * c0, c1 * b0 + d1 * d0)

        fwd = join(fwd, step, lane < step)
        bwd = join(bwd, LANES - step, lane >= LANES - step)
        step *= 2
    ends = [jnp.broadcast_to(v[:, LANES - 1 : LANES], shape) for v in fwd]
    starts = [jnp.broadcast_to(v[:, 0:1], shape) for v in bwd]
    for low, size in ((0, blocks_x), (blocks_x, blocks_y)):
        y = jnp.zeros((1, LANES), F32)
        for q in range(low, low + size):
            rows_in[0, q : q + 1, :] = y
            at, bt, ct, dt = (v[q : q + 1, :] for v in ends)
            y = (at * y + bt) / (ct * y + dt)
        z = None
        for q in reversed(range(low, low + size)):
            at, bt, ct, dt = (v[q : q + 1, :] for v in starts)
            if z is None:
                rows_in[1, q : q + 1, :] = jnp.ones((1, LANES), F32)
                rows_in[2, q : q + 1, :] = jnp.zeros((1, LANES), F32)
                z = at / ct
            else:
                rows_in[1, q : q + 1, :] = z
                rows_in[2, q : q + 1, :] = jnp.ones((1, LANES), F32)
                z = (at * z + bt) / (ct * z + dt)
    y_in, z_num, z_den = rows_in[0], rows_in[1], rows_in[2]
    den = fwd[2] * y_in + fwd[3]
    left = (fwd[0] * y_in + fwd[1]) / den
    right = (bwd[0] * z_num + bwd[1] * z_den) / (bwd[2] * z_num + bwd[3] * z_den)
    green = operator_divisor / (left + right)
    tab[7] = green / den
    tab[8] = den
    tab[11] = 1.0 / jnp.broadcast_to(den[:, LANES - 1 : LANES], shape)
    tab[12] = 1.0 / jnp.broadcast_to(green[:, LANES - 1 : LANES], shape)
    tab[13] = 1.0 / jnp.broadcast_to(den[:, 0:1], shape)


def weights_between(gain, low, size, own, forward, backward):
    q = iota((size, LANES), 0)
    ahead = jnp.ones((size, LANES), F32)
    behind = jnp.ones((size, LANES), F32)
    for m in range(size):
        g = gain[low + m : low + m + 1, :]
        ahead = ahead * jnp.where((m > q) & (m < own), g, 1.0)
        behind = behind * jnp.where((m < q) & (m > own), g, 1.0)
    forward[low : low + size, :] = jnp.where(q < own, ahead, 0.0)
    backward[low : low + size, :] = jnp.where(q > own, behind, 0.0)


def green_block(u_col, w_col, u_row, w_row):
    i, j = iota((LANES, LANES), 0), iota((LANES, LANES), 1)
    return jnp.where(i >= j, u_col * w_row, w_col * u_row)


def prepare_kernel(
    nx, ny, dens, sx_in, sy_in,
    colx, ycoef, scal, cf, cb, wcat, gxh, gxl, rh, er, lch, lcl, packed, box,
    sx, sy, rsend, to_right, to_left, rrecv, from_left, from_right, tiles,
    tab, rows_in, stack, wfine, load_sem, send_sem, recv_sem,
):
    p, r = lax.axis_index("gx"), lax.axis_index("gy")
    up, down = lax.rem(p + nx - 1, nx), lax.rem(p + 1, nx)
    left, right = lax.rem(r + ny - 1, ny), lax.rem(r + 1, ny)
    loads = []
    for k in range(PLANES // STEP):
        part = pl.ds(k * STEP, STEP)
        for t in range(2):
            loads.append(
                pltpu.make_async_copy(
                    dens.at[part, :, pl.ds(t * LANES, LANES)], box.at[t, part], load_sem.at[2 * k + t]
                )
            )
            loads[-1].start()
    for k, (src, dst) in enumerate(((sx_in, sx), (sy_in, sy))):
        loads.append(pltpu.make_async_copy(src, dst, load_sem.at[2 * PLANES // STEP + k]))
        loads[-1].start()
    barrier = pltpu.get_barrier_semaphore()
    for i in (up, p, down):
        for j in (left, r, right):
            if i is p and j is r:
                continue
            pl.semaphore_signal(barrier, inc=1, device_id=(i, j), device_id_type=MESH)

    right_rows, left_rows = FINE // 2, FINE // 4
    lane_r, lane_l = iota((right_rows, LANES), 1), iota((left_rows, LANES), 1)
    to_right[...] = jnp.zeros((right_rows, LANES), F32)
    to_left[...] = jnp.zeros((left_rows, LANES), F32)
    for k in range(PLANES // STEP):
        loads[2 * k].wait()
        loads[2 * k + 1].wait()
        acc_r, acc_l = to_right[...], to_left[...]
        for zi in range(STEP):
            z = k * STEP + zi
            for m in range(2):
                rows = slice(m * right_rows, (m + 1) * right_rows)
                at = 2 * m * PLANES + z
                acc_r = jnp.where(lane_r == at, box[1, z, rows, LANES - 2 : LANES - 1], acc_r)
                acc_r = jnp.where(lane_r == at + PLANES, box[1, z, rows, LANES - 1 : LANES], acc_r)
            for m in range(4):
                rows = slice(m * left_rows, (m + 1) * left_rows)
                acc_l = jnp.where(lane_l == m * PLANES + z, box[0, z, rows, 0:1], acc_l)
            for t in range(2):
                rsend[0, t, z : z + 1, :] = box[t, z, FINE - 2 : FINE - 1, :]
                rsend[1, t, z : z + 1, :] = box[t, z, FINE - 1 : FINE, :]
                rsend[2, t, z : z + 1, :] = box[t, z, 0:1, :]
        to_right[...] = acc_r
        to_left[...] = acc_l

    pl.semaphore_wait(barrier, 8)
    top = pl.ds(0, 8)
    end_r, end_l = pl.ds(right_rows - 8, 8), pl.ds(left_rows - 8, 8)
    plan = (
        (to_right, from_left, p, right),
        (to_left, from_right, p, left),
        (rsend.at[pl.ds(0, 2)], rrecv.at[pl.ds(0, 2)], down, r),
        (rsend.at[pl.ds(2, 1)], rrecv.at[pl.ds(2, 1)], up, r),
        (to_left.at[end_l], tiles.at[0], down, r),
        (to_left.at[top], tiles.at[1], up, r),
        (to_right.at[end_r], tiles.at[2], down, right),
        (to_left.at[end_l], tiles.at[3], down, left),
        (to_right.at[top], tiles.at[4], up, right),
        (to_left.at[top], tiles.at[5], up, left),
    )
    copies = []
    for k, (src, dst, i, j) in enumerate(plan):
        copies.append(
            pltpu.make_async_remote_copy(
                src_ref=src, dst_ref=dst, send_sem=send_sem.at[k], recv_sem=recv_sem.at[k],
                device_id=(i, j), device_id_type=MESH,
            )
        )
        copies[-1].start()

    for load in loads[2 * PLANES // STEP :]:
        load.wait()
    chain_tables(nx, ny, sx, sy, tab, rows_in)
    weights_between(tab[11], 0, nx, p, cf, cb)
    weights_between(tab[11], nx, ny, r, cf, cb)
    row_x, row_y = pl.ds(p, 1), pl.ds(nx + r, 1)
    ux, wx, uy, wy = tab[7, row_x, :], tab[8, row_x, :], tab[7, row_y, :], tab[8, row_y, :]
    stack[...] = jnp.zeros((LANES, LANES), F32)
    for k in range(7):
        stack[k : k + 1, :] = tab[k, row_x, :]
    stack[X_U : X_U + 1, :] = ux
    stack[X_PSI : X_PSI + 1, :] = wx * tab[11, row_x, :]
    stack[X_W : X_W + 1, :] = wx
    for k in range(5):
        stack[Y_K1 + k : Y_K1 + k + 1, :] = tab[2 + k, row_y, :]
    stack[Y_U : Y_U + 1, :] = uy
    stack[Y_W : Y_W + 1, :] = wy
    cols = stack[...].T
    colx[...] = cols
    scal[...] = jnp.zeros((8, LANES), F32)
    scal[S_FX : S_FX + 1, :] = tab[12, row_x, :]
    scal[S_BX : S_BX + 1, :] = tab[13, row_x, :]
    scal[S_FY : S_FY + 1, :] = tab[12, row_y, :]
    scal[S_BY : S_BY + 1, :] = tab[13, row_y, :]
    wl_x = tab[9, row_x, :][:, 0:1]
    wr_x = tab[10, row_x, :][:, 0:1]
    wl_y = tab[9, row_y, :][:, 0:1]
    wr_y = tab[10, row_y, :][:, 0:1]
    scal[S_WRM : S_WRM + 1, :] = jnp.broadcast_to(wr_x, (1, LANES))
    scal[S_UY : S_UY + 1, :] = uy
    scal[S_PSIY : S_PSIY + 1, :] = wy * tab[11, row_y, :]

    lane_z = iota((PLANES, LANES), 1)
    for k, index in enumerate((X_U, X_PSI)):
        packed[k] = sum(
            jnp.where(lane_z // PLANES == m, cols[m * PLANES : (m + 1) * PLANES, index : index + 1], 0.0)
            for m in range(LANES // PLANES)
        )

    odd_row = (iota((1, LANES), 1) & 1) == 1
    ycoef[...] = jnp.zeros((8, FINE), F32)
    for t in range(2):
        h = sy[pl.ds(2 * r + t, 1), :]
        hp = pltpu.roll(h, 1, 1)
        inv = 1.0 / (h + hp)
        ycoef[0:1, t * LANES : (t + 1) * LANES] = jnp.where(odd_row, h * inv, 0.0)
        ycoef[1:2, t * LANES : (t + 1) * LANES] = jnp.where(odd_row, hp * inv, 0.0)

    hi, lo = split(green_block(column(cols, X_U), column(cols, X_W), ux, wx))
    gxh[...] = hi
    gxl[...] = lo
    gy = green_block(column(cols, Y_U), column(cols, Y_W), uy, wy)
    g1, g2, g3, g4, g5 = (column(cols, Y_K1 + k) * gy for k in range(5))
    wfine[pl.ds(0, LANES, stride=2), :] = g3 + shift_down(g5, 0.0) + shift_up(g1, 0.0)
    wfine[pl.ds(1, LANES, stride=2), :] = g4 + shift_up(g2, 0.0)
    i = iota((LANES, LANES), 0)
    outer = jnp.where(
        i < PLANES, g1[0:1, :],
        jnp.where(i < 2 * PLANES, g2[0:1, :], jnp.where(i < 3 * PLANES, g5[LANES - 1 : LANES, :], 0.0)),
    )
    hi, lo = split(wfine[...])
    wcat[0:FINE, 0:LANES] = hi
    wcat[0:FINE, LANES:FINE] = lo
    hi, lo = split(outer)
    wcat[FINE : FINE + LANES, 0:LANES] = hi
    wcat[FINE : FINE + LANES, LANES:FINE] = lo

    for copy in copies:
        copy.wait()

    has_up = (p > 0).astype(F32)
    has_down = (p < nx - 1).astype(F32)
    has_left = (r > 0).astype(F32)
    has_right = (r < ny - 1).astype(F32)
    lane_8 = iota((8, LANES), 1)
    lane = iota((LANES, LANES), 1)

    def unpack(ref, start, shifts):
        values = ref[pl.ds(start, LANES // len(shifts), stride=2), :]
        return jnp.concatenate([pltpu.roll(values, n, 1) if n else values for n in shifts], axis=0)

    e_c, o_c = (
        jnp.where(
            lane < 2 * PLANES,
            unpack(from_left, start, (0, 64)) * has_left,
            unpack(from_right, start, (64, 32, 0, 96)) * has_right,
        )
        for start in range(2)
    )
    own = unpack(to_left, 0, (32, 0, 96, 64))
    own_n = pltpu.roll(tiles[0], 64, 1) * has_up
    own_s = pltpu.roll(tiles[1], 32, 1) * has_down
    north = (
        jnp.where(
            lane_8 < 2 * PLANES,
            pltpu.roll(tiles[2], 64, 1) * has_left,
            pltpu.roll(tiles[3], 96, 1) * has_right,
        )
        * has_up
    )
    south = (
        jnp.where(lane_8 < 2 * PLANES, tiles[4] * has_left, pltpu.roll(tiles[5], 64, 1) * has_right)
        * has_down
    )

    def along_y(values, own_values):
        at = iota(values.shape, 1)
        guess = wl_y * pltpu.roll(values, PLANES, 1) + wr_y * own_values
        return jnp.where((at >= PLANES) & (at < 2 * PLANES), guess, values)

    se = along_y(e_c, own)
    se_n = along_y(north, own_n)[6:7, :]
    se_s = along_y(south, own_s)[0:1, :]
    do = o_c - (column(cols, X_WL) * se + column(cols, X_WR) * shift_up(se, se_s))
    de = e_c - se
    de_n = north[6:7, :] - se_n
    do_n = north[7:8, :] - (wl_x * se_n + wr_x * se[0:1, :])
    de_s = south[0:1, :] - se_s
    loads_c = (
        column(cols, X_K1) * shift_down(de, de_n)
        + column(cols, X_K2) * shift_down(do, do_n)
        + column(cols, X_K3) * de
        + column(cols, X_K4) * do
        + column(cols, X_K5) * shift_up(de, de_s)
    )
    hi, lo = split(loads_c)
    lch[...] = hi
    lcl[...] = lo
    er[...] = e_c

    stack[0:8, :] = north
    stack[8:16, :] = south
    corner = stack[...].T
    corner_n = corner[2 * PLANES : 3 * PLANES, 6:7]
    corner_s = corner[2 * PLANES : 3 * PLANES, 8:9]
    odd = (lane_z & 1) == 1

    def row_along_y(layer, scale, corner_col):
        tiles_in = [layer[t] * scale for t in range(2)]
        next_in = [pltpu.roll(v, LANES - 1, 1) for v in tiles_in]
        after = [
            jnp.where(lane_z < LANES - 1, next_in[0], next_in[1]),
            jnp.where(lane_z < LANES - 1, next_in[1], corner_col),
        ]
        result = []
        for t in range(2):
            part = slice(t * LANES, (t + 1) * LANES)
            guess = ycoef[0:1, part] * pltpu.roll(tiles_in[t], 1, 1) + ycoef[1:2, part] * after[t]
            result.append(jnp.where(odd, guess, tiles_in[t]))
        return tiles_in, result

    e_n, s_n = row_along_y(rrecv[0], has_up, corner_n)
    e_s, s_s = row_along_y(rrecv[2], has_down, corner_s)
    for t in range(2):
        rh[0, t] = e_n[t] - s_n[t]
        rh[1, t] = rrecv[1, t] * has_up - wl_x * s_n[t]
        rh[2, t] = s_s[t]
        rh[3, t] = e_s[t] - s_s[t]


def main_kernel(
    box, colx, ycoef, scal, rh, er, lch, lcl, wcat, gxh, gxl,
    detail, local, coarse, wide, se_buf, de_buf, do_buf, woven, high, low, sem,
):
    for k in range(7):
        wide[k] = column(colx[...], k)
    lane = iota((LANES, LANES), 1)
    odd = (lane & 1) == 1
    inner = lane < LANES - 1
    pick = (2 * lane) & (LANES - 1)
    wrm = scal[S_WRM : S_WRM + 1, :]
    body, before, after = pl.ds(8, LANES), pl.ds(7, LANES), pl.ds(9, LANES)
    turns = PLANES // PER

    def stencil(z, k, slot):
        row = pl.ds(z, 1)
        e = [box[t, z, pl.ds(0, LANES, stride=2), :] for t in range(2)]
        o = [box[t, z, pl.ds(1, LANES, stride=2), :] for t in range(2)]
        nxt = [pltpu.roll(v, LANES - 1, 1) for v in e]
        beyond = pltpu.roll(er[...], lax.rem(3 * LANES - 1 - 2 * PLANES - z, LANES), 1)
        nxt = [jnp.where(inner, nxt[0], nxt[1]), jnp.where(inner, nxt[1], beyond)]
        for t in range(2):
            part = slice(t * LANES, (t + 1) * LANES)
            guess = ycoef[0:1, part] * pltpu.roll(e[t], 1, 1) + ycoef[1:2, part] * nxt[t]
            se = jnp.where(odd, guess, e[t])
            de = e[t] - se
            se_buf[k, t, body, :] = se
            se_buf[k, t, pl.ds(8 + LANES, 1), :] = rh[2, t, row, :]
            do = o[t] - (wide[X_WL] * se + wide[X_WR] * se_buf[k, t, after, :])
            woven[slot, k, t, pl.ds(0, LANES, stride=2), :] = de
            woven[slot, k, t, pl.ds(1, LANES, stride=2), :] = do
            de_buf[k, t, body, :] = de
            de_buf[k, t, pl.ds(7, 1), :] = rh[0, t, row, :]
            de_buf[k, t, pl.ds(8 + LANES, 1), :] = rh[3, t, row, :]
            do_buf[k, t, body, :] = do
            do_buf[k, t, pl.ds(7, 1), :] = rh[1, t, row, :] - wrm * se[0:1, :]
            load = (
                wide[X_K3] * de
                + wide[X_K4] * do
                + wide[X_K1] * de_buf[k, t, before, :]
                + wide[X_K2] * do_buf[k, t, before, :]
                + wide[X_K5] * de_buf[k, t, after, :]
            )
            hi, lo = split(load)
            high[slot, k, :, part] = hi
            low[slot, k, :, part] = lo
        coarse[z] = jnp.where(
            lane < LANES // 2,
            jnp.take_along_axis(e[0], pick, axis=1, mode="promise_in_bounds"),
            jnp.take_along_axis(e[1], pick, axis=1, mode="promise_in_bounds"),
        )
        mine = (lane & (PLANES - 1)) == z
        high[slot, k, :, FINE:] = jnp.where(mine, lch[...].astype(F32), 0.0).astype(BF16)
        low[slot, k, :, FINE:] = jnp.where(mine, lcl[...].astype(F32), 0.0).astype(BF16)

    def solve(z, slot):
        pairs = []
        for k in range(0, PER, 2):
            pair = []
            for n in (k, k + 1):
                both = mxu(high[slot, n], wcat[...])
                rest = mxu(low[slot, n], wcat[:, 0:LANES])
                pair.append(both[:, :LANES] + both[:, LANES:] + rest)
            pairs.append(jnp.concatenate(pair, axis=1))
        for k in range(0, PER, 2):
            hi, lo = split(pairs[k // 2])
            solved = mxu(gxh[...], hi) + (mxu(gxh[...], lo) + mxu(gxl[...], hi))
            local[z + k] = solved[:, :LANES]
            local[z + k + 1] = solved[:, LANES:]

    def writes(it, slot):
        return [
            pltpu.make_async_copy(
                woven.at[slot, :, t],
                detail.at[pl.ds(PER * it, PER), :, pl.ds(t * LANES, LANES)],
                sem.at[slot, t],
            )
            for t in range(2)
        ]

    def step(it, carry):
        slot = lax.rem(it, 2)

        @pl.when(it >= 2)
        def _():
            for write in writes(it - 2, slot):
                write.wait()

        solve(PER * it - PER, 1 - slot)
        for k in range(PER):
            stencil(PER * it + k, k, slot)
        for write in writes(it, slot):
            write.start()
        return carry

    for k in range(PER):
        stencil(k, k, 0)
    for write in writes(0, 0):
        write.start()
    lax.fori_loop(1, turns, step, 0)
    solve(PLANES - PER, (turns - 1) % 2)
    for it in (turns - 2, turns - 1):
        for write in writes(it, it % 2):
            write.wait()


def exchange_kernel(
    nx, ny, local, coarse, colx, scal, cf, cb, packed, mid, outer_l, outer_r,
    xs, xr, ys, yr, cs, cr, ks, kr, sums, uwide, pwide,
    sx_sem, rx_sem, sy_sem, ry_sem, sc_sem, rc_sem, sk_sem, rk_sem,
):
    p, r = lax.axis_index("gx"), lax.axis_index("gy")
    barrier = pltpu.get_barrier_semaphore()
    for k in range(1, nx):
        pl.semaphore_signal(barrier, inc=1, device_id=(lax.rem(p + k, nx), r), device_id_type=MESH)
    for k in range(1, ny):
        pl.semaphore_signal(barrier, inc=1, device_id=(p, lax.rem(r + k, ny)), device_id_type=MESH)
    tail, front = local[:, LANES - 1, :], local[:, 0, :]
    xs[0] = tail * scal[S_FX : S_FX + 1, :]
    xs[1] = front * scal[S_BX : S_BX + 1, :]
    ends = jnp.concatenate([tail, front, tail, front], axis=0).T
    lane_1 = iota((1, LANES), 1)

    def spread_planes(row):
        row = jnp.where(lane_1 < PLANES, row, 0.0)
        row = row + pltpu.roll(row, PLANES, 1)
        return row + pltpu.roll(row, 2 * PLANES, 1)

    ks[...] = jnp.zeros((2, 8, LANES), F32)
    for n, at in enumerate((LANES - 1, 0)):
        corner = ends[at : at + 1, :]
        ks[0, n : n + 1, :] = spread_planes(corner) * scal[S_FX : S_FX + 1, :]
        ks[1, n : n + 1, :] = spread_planes(pltpu.roll(corner, LANES - PLANES, 1)) * scal[S_BX : S_BX + 1, :]
    uwide[...] = column(colx[...], X_U)
    pwide[...] = column(colx[...], X_PSI)

    def start(sent, got, send_sem, recv_sem, own, count, target):
        copies = []
        for k in range(1, count):
            wraps = jnp.where(own + k >= count, 1, 0)
            copies.append(
                pltpu.make_async_remote_copy(
                    src_ref=sent.at[wraps], dst_ref=got.at[k - 1],
                    send_sem=send_sem.at[k - 1], recv_sem=recv_sem.at[k - 1],
                    device_id=target(lax.rem(own + k, count)), device_id_type=MESH,
                )
            )
            copies[-1].start()
        return copies

    def gather(copies, got, own, count, low):
        forward = backward = 0.0
        for k in range(1, count):
            copies[k - 1].wait_recv()
            row = pl.ds(low + lax.rem(own + count - k, count), 1)
            values = got[k - 1]
            forward = forward + cf[row, :] * values
            backward = backward + cb[row, :] * values
        return forward, backward


    lane = iota((PLANES, LANES), 1)
    blocks = LANES // PLANES

    def edges(z, carry):
        last, head = carry
        for m in range(blocks):
            block = local[z, pl.ds(m * PLANES, PLANES), :]
            here = lane == m * PLANES + z
            last = jnp.where(here, block[:, LANES - 1 : LANES], last)
            head = jnp.where(here, block[:, 0:1], head)
        return last, head

    zero = jnp.zeros((PLANES, LANES), F32)
    last, head = lax.fori_loop(0, PLANES, edges, (zero, zero), unroll=4)
    scale_f, scale_b = scal[S_FY : S_FY + 1, :], scal[S_BY : S_BY + 1, :]
    ys[0] = last * scale_f
    ys[1] = head * scale_b
    pl.semaphore_wait(barrier, nx + ny - 2)
    k_copies = start(ks, kr, sk_sem, rk_sem, p, nx, lambda i: (i, r))
    x_copies = start(xs, xr, sx_sem, rx_sem, p, nx, lambda i: (i, r))
    y_copies = start(ys, yr, sy_sem, ry_sem, r, ny, lambda j: (p, j))

    corner_f, corner_b = gather(k_copies, kr, p, nx, 0)
    cs[...] = jnp.zeros((2, 8, LANES), F32)
    cs[0, 0:1, :] = corner_f[0:1, :] * scale_f
    cs[0, 1:2, :] = corner_b[0:1, :] * scale_f
    cs[1, 0:1, :] = corner_f[1:2, :] * scale_b
    cs[1, 1:2, :] = corner_b[1:2, :] * scale_b
    c_copies = start(cs, cr, sc_sem, rc_sem, r, ny, lambda j: (p, j))
    forward, backward = gather(x_copies, xr, p, nx, 0)
    sums[0] = forward
    sums[1] = backward

    edge = jnp.where(
        (iota((LANES, LANES), 0) // PLANES) % 2 == 0,
        scal[S_UY : S_UY + 1, :], scal[S_PSIY : S_PSIY + 1, :],
    )
    edge_h = edge.astype(BF16).astype(F32)
    edge_l = edge - edge_h
    plane_of = iota((LANES, LANES), 0) % PLANES

    def x_part(z, carry):
        row = pl.ds(z, 1)
        mid[z] = local[z] + coarse[z] + uwide[...] * sums[0, row, :] + pwide[...] * sums[1, row, :]
        outer_r[z, 0:LANES, :] = jnp.where(plane_of == z, edge_h, 0.0).astype(BF16)
        outer_r[z, LANES:, :] = jnp.where(plane_of == z, edge_l, 0.0).astype(BF16)
        return carry

    lax.fori_loop(0, PLANES, x_part, 0, unroll=2)
    u_x, psi_x = packed[0], packed[1]
    forward, backward = gather(y_copies, yr, r, ny, nx)
    extra_f, extra_b = gather(c_copies, cr, r, ny, nx)
    forward = forward + u_x * extra_f[0:1, :] + psi_x * extra_f[1:2, :]
    backward = backward + u_x * extra_b[0:1, :] + psi_x * extra_b[1:2, :]
    lane = iota((LANES, LANES), 1)

    def spread(values):
        return jnp.concatenate(
            [pltpu.roll(values, (LANES - m * PLANES) % LANES, 1) if m else values for m in range(blocks)],
            axis=0,
        )

    both = jnp.where(lane < PLANES, spread(forward), pltpu.roll(spread(backward), PLANES, 1))
    high = both.astype(BF16).astype(F32)
    both = jnp.where(lane < 2 * PLANES, high, pltpu.roll(both - high, 2 * PLANES, 1))
    outer_l[:, 0:LANES] = both.astype(BF16)
    outer_l[:, LANES:] = both.astype(BF16)
    for copy in k_copies + x_copies + y_copies + c_copies:
        copy.wait_send()


def final_kernel(mid, outer_l, outer_r, out, total, sem):
    writes = []
    for g in range(PLANES // 8):
        planes = pl.ds(g * 8, 8)
        for k in range(g * 8, g * 8 + 8, 2):
            pair = jnp.concatenate([outer_r[k], outer_r[k + 1]], axis=1)
            update = mxu(outer_l[...], pair)
            total[k] = mid[k] + update[:, :LANES]
            total[k + 1] = mid[k + 1] + update[:, LANES:]
        writes.append(pltpu.make_async_copy(total.at[planes], out.at[planes], sem.at[g]))
        writes[-1].start()
    for write in writes:
        write.wait()


def per_device(nx, ny, density, spacing_x, spacing_y):
    blocks = nx + ny
    hbm = pl.BlockSpec(memory_space=pltpu.HBM)
    vmem = pl.BlockSpec(memory_space=pltpu.VMEM)
    f32 = lambda *shape: jax.ShapeDtypeStruct(shape, F32)
    bf16 = lambda *shape: jax.ShapeDtypeStruct(shape, BF16)
    sx = spacing_x.reshape(2 * nx, LANES)
    sy = spacing_y.reshape(2 * ny, LANES)
    colx, ycoef, scal, cf, cb, wcat, gxh, gxl, rh, er, lch, lcl, packed, box = pl.pallas_call(
        functools.partial(prepare_kernel, nx, ny),
        out_shape=(
            f32(LANES, LANES), f32(8, FINE), f32(8, LANES), f32(blocks, LANES), f32(blocks, LANES),
            bf16(FINE + LANES, FINE), bf16(LANES, LANES), bf16(LANES, LANES),
            f32(4, 2, PLANES, LANES), f32(LANES, LANES), bf16(LANES, LANES), bf16(LANES, LANES),
            f32(2, PLANES, LANES), f32(2, PLANES, FINE, LANES),
        ),
        in_specs=[hbm] * 3,
        out_specs=(vmem,) * 14,
        scratch_shapes=[
            pltpu.VMEM((2 * nx, LANES), F32),
            pltpu.VMEM((2 * ny, LANES), F32),
            pltpu.VMEM((3, 2, PLANES, LANES), F32),
            pltpu.VMEM((FINE // 2, LANES), F32),
            pltpu.VMEM((FINE // 4, LANES), F32),
            pltpu.VMEM((3, 2, PLANES, LANES), F32),
            pltpu.VMEM((FINE // 2, LANES), F32),
            pltpu.VMEM((FINE // 4, LANES), F32),
            pltpu.VMEM((6, 8, LANES), F32),
            pltpu.VMEM((14, blocks, LANES), F32),
            pltpu.VMEM((3, blocks, LANES), F32),
            pltpu.VMEM((LANES, LANES), F32),
            pltpu.VMEM((FINE, LANES), F32),
            pltpu.SemaphoreType.DMA((2 * PLANES // STEP + 2,)),
            pltpu.SemaphoreType.DMA((10,)),
            pltpu.SemaphoreType.DMA((10,)),
        ],
        compiler_params=pltpu.CompilerParams(
            collective_id=0, has_side_effects=True, vmem_limit_bytes=32 * MIB
        ),
        name="prepare",
    )(*(pltpu.with_memory_space_constraint(v, pltpu.HBM) for v in (density, sx, sy)))
    tables = (colx, ycoef, scal, rh, er, lch, lcl, wcat, gxh, gxl)
    detail, local, coarse = pl.pallas_call(
        main_kernel,
        out_shape=(f32(PLANES, FINE, FINE), f32(PLANES, LANES, LANES), f32(PLANES, LANES, LANES)),
        in_specs=[vmem] * (1 + len(tables)),
        out_specs=(hbm, vmem, vmem),
        scratch_shapes=[
            pltpu.VMEM((7, LANES, LANES), F32),
            pltpu.VMEM((PER, 2, LANES + 16, LANES), F32),
            pltpu.VMEM((PER, 2, LANES + 16, LANES), F32),
            pltpu.VMEM((PER, 2, LANES + 16, LANES), F32),
            pltpu.VMEM((2, PER, 2, FINE, LANES), F32),
            pltpu.VMEM((2, PER, LANES, FINE + LANES), BF16),
            pltpu.VMEM((2, PER, LANES, FINE + LANES), BF16),
            pltpu.SemaphoreType.DMA((2, 2)),
        ],
        compiler_params=pltpu.CompilerParams(vmem_limit_bytes=32 * MIB),
        name="main",
    )(box, *tables)
    mid, outer_l, outer_r = pl.pallas_call(
        functools.partial(exchange_kernel, nx, ny),
        out_shape=(f32(PLANES, LANES, LANES), bf16(LANES, FINE), bf16(PLANES, FINE, LANES)),
        in_specs=[vmem] * 7,
        out_specs=(vmem,) * 3,
        scratch_shapes=[
            pltpu.VMEM((2, PLANES, LANES), F32),
            pltpu.VMEM((nx - 1, PLANES, LANES), F32),
            pltpu.VMEM((2, PLANES, LANES), F32),
            pltpu.VMEM((ny - 1, PLANES, LANES), F32),
            pltpu.VMEM((2, 8, LANES), F32),
            pltpu.VMEM((ny - 1, 8, LANES), F32),
            pltpu.VMEM((2, 8, LANES), F32),
            pltpu.VMEM((nx - 1, 8, LANES), F32),
            pltpu.VMEM((2, PLANES, LANES), F32),
            pltpu.VMEM((LANES, LANES), F32),
            pltpu.VMEM((LANES, LANES), F32),
            pltpu.SemaphoreType.DMA((nx - 1,)),
            pltpu.SemaphoreType.DMA((nx - 1,)),
            pltpu.SemaphoreType.DMA((ny - 1,)),
            pltpu.SemaphoreType.DMA((ny - 1,)),
            pltpu.SemaphoreType.DMA((ny - 1,)),
            pltpu.SemaphoreType.DMA((ny - 1,)),
            pltpu.SemaphoreType.DMA((nx - 1,)),
            pltpu.SemaphoreType.DMA((nx - 1,)),
        ],
        compiler_params=pltpu.CompilerParams(
            collective_id=1, has_side_effects=True, vmem_limit_bytes=32 * MIB
        ),
        name="exchange",
    )(local, coarse, colx, scal, cf, cb, packed)
    coarse_new = pl.pallas_call(
        final_kernel,
        out_shape=f32(PLANES, LANES, LANES),
        in_specs=[vmem] * 3,
        out_specs=hbm,
        scratch_shapes=[pltpu.VMEM((PLANES, LANES, LANES), F32), pltpu.SemaphoreType.DMA((PLANES // 8,))],
        compiler_params=pltpu.CompilerParams(vmem_limit_bytes=16 * MIB),
        name="final",
    )(mid, outer_l, outer_r)
    return detail, coarse_new


def solution(mesh):
    placed = P(None, "gx", "gy")
    return jax.shard_map(
        functools.partial(per_device, mesh.shape["gx"], mesh.shape["gy"]),
        mesh=mesh,
        in_specs=(placed, P(), P()),
        out_specs=(placed, placed),
        check_vma=False,
    )
```

```python
import functools

import jax
import jax.numpy as jnp
from jax import lax
from jax.experimental import pallas as pl
from jax.experimental.pallas import tpu as pltpu
from jax.sharding import PartitionSpec as P

MESH = pl.DeviceIdType.MESH
F32 = jnp.float32
BF16 = jnp.bfloat16
HIGHEST = lax.Precision.HIGHEST
stiffness_weight = 4096.0
operator_divisor = 32.0
LANES = 128
FINE = 256
PLANES = 32
PER = 8
STEP = 4
MIB = 1 << 20
X_WL, X_WR, X_K1, X_K2, X_K3, X_K4, X_K5, X_U, X_PSI, X_W = range(10)
Y_K1, Y_K2, Y_K3, Y_K4, Y_K5, Y_U, Y_W = range(10, 17)
S_FX, S_BX, S_FY, S_BY, S_WRM, S_UY, S_PSIY = range(7)


def split(values):
    high = values.astype(BF16)
    return high, (values - high.astype(F32)).astype(BF16)


def mxu(a, b):
    return jnp.dot(a, b, preferred_element_type=F32)


def iota(shape, dim):
    return lax.broadcasted_iota(jnp.int32, shape, dim)


def column(table, index):
    return jnp.broadcast_to(table[:, index : index + 1], (LANES, LANES))


def shift_up(values, last):
    rolled = pltpu.roll(values, LANES - 1, 0)
    return jnp.where(iota(values.shape, 0) == LANES - 1, last, rolled)


def shift_down(values, first):
    return jnp.where(iota(values.shape, 0) == 0, first, pltpu.roll(values, 1, 0))


def chain_tables(blocks_x, blocks_y, sx, sy, tab, rows_in):
    count = blocks_x + blocks_y
    shape = (count, LANES)
    lane, row = iota(shape, 1), iota(shape, 0)
    first = (lane == 0) & ((row == 0) | (row == blocks_x))

    def prev(values, fill):
        rolled = pltpu.roll(values, 1, 1)
        return jnp.where(first, fill, jnp.where(lane == 0, pltpu.roll(rolled, 1, 0), rolled))

    def following(values):
        rolled = pltpu.roll(values, LANES - 1, 1)
        return jnp.where(lane == LANES - 1, pltpu.roll(rolled, count - 1, 0), rolled)

    def halves(start):
        return jnp.concatenate(
            [sx[pl.ds(start, blocks_x, stride=2), :], sy[pl.ds(start, blocks_y, stride=2), :]], axis=0
        )

    fine = jnp.concatenate([halves(0), halves(1)], axis=1)
    node, place = iota((FINE, FINE), 0), iota((FINE, FINE), 1)
    pick = jnp.where(place < LANES, 2 * place, 2 * (place - LANES) + 1)
    parts = jnp.dot((fine), (node == pick).astype(F32), precision=HIGHEST, preferred_element_type=F32)
    c, d = parts[:, :LANES], parts[:, LANES:]
    span = c + d
    a, b = prev(c, 0.0), prev(d, 0.0)
    span_before = prev(span, 1.0)
    inverse = 1.0 / span
    inverse_before = 1.0 / span_before
    tab[0] = d * inverse
    tab[1] = c * inverse
    tab[2] = a * a * inverse_before * (1.0 / 6.0)
    tab[3] = a * (1.0 / 3.0) + b * (1.0 / 6.0)
    tab[4] = (a * b * inverse_before + c * d * inverse) * (1.0 / 6.0) + (b + c) * (1.0 / 3.0)
    tab[5] = c * (1.0 / 6.0) + d * (1.0 / 3.0)
    tab[6] = d * d * inverse * (1.0 / 6.0)
    tab[9] = b * inverse_before
    tab[10] = a * inverse_before

    rho = 1.0 / (stiffness_weight * inverse - span * (1.0 / 6.0))
    rho_before = prev(rho, 0.0)
    mu = 0.5 * (a + b + span)
    mu_after = following(mu)
    one = jnp.ones(shape, F32)
    fwd = (one + mu * rho_before, mu, rho_before, one)
    bwd = (one, mu_after, rho, one + rho * mu_after)
    step = 1
    while step < LANES:
        def join(m, shift, outside):
            fill = (1.0, 0.0, 0.0, 1.0)
            a1, b1, c1, d1 = m
            a0, b0, c0, d0 = (
                jnp.where(outside, f, pltpu.roll(v, shift, 1)) for v, f in zip(m, fill)
            )
            return (a1 * a0 + b1 * c0, a1 * b0 + b1 * d0, c1 * a0 + d1 * c0, c1 * b0 + d1 * d0)

        fwd = join(fwd, step, lane < step)
        bwd = join(bwd, LANES - step, lane >= LANES - step)
        step *= 2
    ends = [jnp.broadcast_to(v[:, LANES - 1 : LANES], shape) for v in fwd]
    starts = [jnp.broadcast_to(v[:, 0:1], shape) for v in bwd]
    for low, size in ((0, blocks_x), (blocks_x, blocks_y)):
        y = jnp.zeros((1, LANES), F32)
        for q in range(low, low + size):
            rows_in[0, q : q + 1, :] = y
            at, bt, ct, dt = (v[q : q + 1, :] for v in ends)
            y = (at * y + bt) / (ct * y + dt)
        z = None
        for q in reversed(range(low, low + size)):
            at, bt, ct, dt = (v[q : q + 1, :] for v in starts)
            if z is None:
                rows_in[1, q : q + 1, :] = jnp.ones((1, LANES), F32)
                rows_in[2, q : q + 1, :] = jnp.zeros((1, LANES), F32)
                z = at / ct
            else:
                rows_in[1, q : q + 1, :] = z
                rows_in[2, q : q + 1, :] = jnp.ones((1, LANES), F32)
                z = (at * z + bt) / (ct * z + dt)
    y_in, z_num, z_den = rows_in[0], rows_in[1], rows_in[2]
    den = fwd[2] * y_in + fwd[3]
    left = (fwd[0] * y_in + fwd[1]) / den
    right = (bwd[0] * z_num + bwd[1] * z_den) / (bwd[2] * z_num + bwd[3] * z_den)
    green = operator_divisor / (left + right)
    tab[7] = green / den
    tab[8] = den
    tab[11] = 1.0 / jnp.broadcast_to(den[:, LANES - 1 : LANES], shape)
    tab[12] = 1.0 / jnp.broadcast_to(green[:, LANES - 1 : LANES], shape)
    tab[13] = 1.0 / jnp.broadcast_to(den[:, 0:1], shape)


def weights_between(gain, low, size, own, forward, backward):
    q = iota((size, LANES), 0)
    ahead = jnp.ones((size, LANES), F32)
    behind = jnp.ones((size, LANES), F32)
    for m in range(size):
        g = gain[low + m : low + m + 1, :]
        ahead = ahead * jnp.where((m > q) & (m < own), g, 1.0)
        behind = behind * jnp.where((m < q) & (m > own), g, 1.0)
    forward[low : low + size, :] = jnp.where(q < own, ahead, 0.0)
    backward[low : low + size, :] = jnp.where(q > own, behind, 0.0)


def green_block(u_col, w_col, u_row, w_row):
    i, j = iota((LANES, LANES), 0), iota((LANES, LANES), 1)
    return jnp.where(i >= j, u_col * w_row, w_col * u_row)


def prepare_kernel(
    nx, ny, dens, sx_in, sy_in,
    colx, ycoef, scal, cf, cb, wcat, gxh, gxl, rh, er, lch, lcl, packed, box,
    sx, sy, rsend, to_right, to_left, rrecv, from_left, from_right, tiles,
    tab, rows_in, stack, wfine, load_sem, send_sem, recv_sem,
):
    p, r = lax.axis_index("gx"), lax.axis_index("gy")
    up, down = lax.rem(p + nx - 1, nx), lax.rem(p + 1, nx)
    left, right = lax.rem(r + ny - 1, ny), lax.rem(r + 1, ny)
    loads = []
    for k in range(PLANES // STEP):
        part = pl.ds(k * STEP, STEP)
        for t in range(2):
            loads.append(
                pltpu.make_async_copy(
                    dens.at[part, :, pl.ds(t * LANES, LANES)], box.at[t, part], load_sem.at[2 * k + t]
                )
            )
            loads[-1].start()
    for k, (src, dst) in enumerate(((sx_in, sx), (sy_in, sy))):
        loads.append(pltpu.make_async_copy(src, dst, load_sem.at[2 * PLANES // STEP + k]))
        loads[-1].start()
    barrier = pltpu.get_barrier_semaphore()
    for i in (up, p, down):
        for j in (left, r, right):
            if i is p and j is r:
                continue
            pl.semaphore_signal(barrier, inc=1, device_id=(i, j), device_id_type=MESH)

    right_rows, left_rows = FINE // 2, FINE // 4
    lane_r, lane_l = iota((right_rows, LANES), 1), iota((left_rows, LANES), 1)
    to_right[...] = jnp.zeros((right_rows, LANES), F32)
    to_left[...] = jnp.zeros((left_rows, LANES), F32)
    for k in range(PLANES // STEP):
        loads[2 * k].wait()
        loads[2 * k + 1].wait()
        acc_r, acc_l = to_right[...], to_left[...]
        for zi in range(STEP):
            z = k * STEP + zi
            for m in range(2):
                rows = slice(m * right_rows, (m + 1) * right_rows)
                at = 2 * m * PLANES + z
                acc_r = jnp.where(lane_r == at, box[1, z, rows, LANES - 2 : LANES - 1], acc_r)
                acc_r = jnp.where(lane_r == at + PLANES, box[1, z, rows, LANES - 1 : LANES], acc_r)
            for m in range(4):
                rows = slice(m * left_rows, (m + 1) * left_rows)
                acc_l = jnp.where(lane_l == m * PLANES + z, box[0, z, rows, 0:1], acc_l)
            for t in range(2):
                rsend[0, t, z : z + 1, :] = box[t, z, FINE - 2 : FINE - 1, :]
                rsend[1, t, z : z + 1, :] = box[t, z, FINE - 1 : FINE, :]
                rsend[2, t, z : z + 1, :] = box[t, z, 0:1, :]
        to_right[...] = acc_r
        to_left[...] = acc_l

    pl.semaphore_wait(barrier, 8)
    top = pl.ds(0, 8)
    end_r, end_l = pl.ds(right_rows - 8, 8), pl.ds(left_rows - 8, 8)
    plan = (
        (to_right, from_left, p, right),
        (to_left, from_right, p, left),
        (rsend.at[pl.ds(0, 2)], rrecv.at[pl.ds(0, 2)], down, r),
        (rsend.at[pl.ds(2, 1)], rrecv.at[pl.ds(2, 1)], up, r),
        (to_left.at[end_l], tiles.at[0], down, r),
        (to_left.at[top], tiles.at[1], up, r),
        (to_right.at[end_r], tiles.at[2], down, right),
        (to_left.at[end_l], tiles.at[3], down, left),
        (to_right.at[top], tiles.at[4], up, right),
        (to_left.at[top], tiles.at[5], up, left),
    )
    copies = []
    for k, (src, dst, i, j) in enumerate(plan):
        copies.append(
            pltpu.make_async_remote_copy(
                src_ref=src, dst_ref=dst, send_sem=send_sem.at[k], recv_sem=recv_sem.at[k],
                device_id=(i, j), device_id_type=MESH,
            )
        )
        copies[-1].start()

    for load in loads[2 * PLANES // STEP :]:
        load.wait()
    chain_tables(nx, ny, sx, sy, tab, rows_in)
    weights_between(tab[11], 0, nx, p, cf, cb)
    weights_between(tab[11], nx, ny, r, cf, cb)
    row_x, row_y = pl.ds(p, 1), pl.ds(nx + r, 1)
    ux, wx, uy, wy = tab[7, row_x, :], tab[8, row_x, :], tab[7, row_y, :], tab[8, row_y, :]
    stack[...] = jnp.zeros((LANES, LANES), F32)
    for k in range(7):
        stack[k : k + 1, :] = tab[k, row_x, :]
    stack[X_U : X_U + 1, :] = ux
    stack[X_PSI : X_PSI + 1, :] = wx * tab[11, row_x, :]
    stack[X_W : X_W + 1, :] = wx
    for k in range(5):
        stack[Y_K1 + k : Y_K1 + k + 1, :] = tab[2 + k, row_y, :]
    stack[Y_U : Y_U + 1, :] = uy
    stack[Y_W : Y_W + 1, :] = wy
    cols = stack[...].T
    colx[...] = cols
    scal[...] = jnp.zeros((8, LANES), F32)
    scal[S_FX : S_FX + 1, :] = tab[12, row_x, :]
    scal[S_BX : S_BX + 1, :] = tab[13, row_x, :]
    scal[S_FY : S_FY + 1, :] = tab[12, row_y, :]
    scal[S_BY : S_BY + 1, :] = tab[13, row_y, :]
    wl_x = tab[9, row_x, :][:, 0:1]
    wr_x = tab[10, row_x, :][:, 0:1]
    wl_y = tab[9, row_y, :][:, 0:1]
    wr_y = tab[10, row_y, :][:, 0:1]
    scal[S_WRM : S_WRM + 1, :] = jnp.broadcast_to(wr_x, (1, LANES))
    scal[S_UY : S_UY + 1, :] = uy
    scal[S_PSIY : S_PSIY + 1, :] = wy * tab[11, row_y, :]

    lane_z = iota((PLANES, LANES), 1)
    for k, index in enumerate((X_U, X_PSI)):
        packed[k] = sum(
            jnp.where(lane_z // PLANES == m, cols[m * PLANES : (m + 1) * PLANES, index : index + 1], 0.0)
            for m in range(LANES // PLANES)
        )

    odd_row = (iota((1, LANES), 1) & 1) == 1
    ycoef[...] = jnp.zeros((8, FINE), F32)
    for t in range(2):
        h = sy[pl.ds(2 * r + t, 1), :]
        hp = pltpu.roll(h, 1, 1)
        inv = 1.0 / (h + hp)
        ycoef[0:1, t * LANES : (t + 1) * LANES] = jnp.where(odd_row, h * inv, 0.0)
        ycoef[1:2, t * LANES : (t + 1) * LANES] = jnp.where(odd_row, hp * inv, 0.0)

    hi, lo = split(green_block(column(cols, X_U), column(cols, X_W), ux, wx))
    gxh[...] = hi
    gxl[...] = lo
    gy = green_block(column(cols, Y_U), column(cols, Y_W), uy, wy)
    g1, g2, g3, g4, g5 = (column(cols, Y_K1 + k) * gy for k in range(5))
    wfine[pl.ds(0, LANES, stride=2), :] = g3 + shift_down(g5, 0.0) + shift_up(g1, 0.0)
    wfine[pl.ds(1, LANES, stride=2), :] = g4 + shift_up(g2, 0.0)
    i = iota((LANES, LANES), 0)
    outer = jnp.where(
        i < PLANES, g1[0:1, :],
        jnp.where(i < 2 * PLANES, g2[0:1, :], jnp.where(i < 3 * PLANES, g5[LANES - 1 : LANES, :], 0.0)),
    )
    hi, lo = split(wfine[...])
    wcat[0:FINE, 0:LANES] = hi
    wcat[0:FINE, LANES:FINE] = lo
    hi, lo = split(outer)
    wcat[FINE : FINE + LANES, 0:LANES] = hi
    wcat[FINE : FINE + LANES, LANES:FINE] = lo

    for copy in copies:
        copy.wait()

    has_up = (p > 0).astype(F32)
    has_down = (p < nx - 1).astype(F32)
    has_left = (r > 0).astype(F32)
    has_right = (r < ny - 1).astype(F32)
    lane_8 = iota((8, LANES), 1)
    lane = iota((LANES, LANES), 1)

    def unpack(ref, start, shifts):
        values = ref[pl.ds(start, LANES // len(shifts), stride=2), :]
        return jnp.concatenate([pltpu.roll(values, n, 1) if n else values for n in shifts], axis=0)

    e_c, o_c = (
        jnp.where(
            lane < 2 * PLANES,
            unpack(from_left, start, (0, 64)) * has_left,
            unpack(from_right, start, (64, 32, 0, 96)) * has_right,
        )
        for start in range(2)
    )
    own = unpack(to_left, 0, (32, 0, 96, 64))
    own_n = pltpu.roll(tiles[0], 64, 1) * has_up
    own_s = pltpu.roll(tiles[1], 32, 1) * has_down
    north = (
        jnp.where(
            lane_8 < 2 * PLANES,
            pltpu.roll(tiles[2], 64, 1) * has_left,
            pltpu.roll(tiles[3], 96, 1) * has_right,
        )
        * has_up
    )
    south = (
        jnp.where(lane_8 < 2 * PLANES, tiles[4] * has_left, pltpu.roll(tiles[5], 64, 1) * has_right)
        * has_down
    )

    def along_y(values, own_values):
        at = iota(values.shape, 1)
        guess = wl_y * pltpu.roll(values, PLANES, 1) + wr_y * own_values
        return jnp.where((at >= PLANES) & (at < 2 * PLANES), guess, values)

    se = along_y(e_c, own)
    se_n = along_y(north, own_n)[6:7, :]
    se_s = along_y(south, own_s)[0:1, :]
    do = o_c - (column(cols, X_WL) * se + column(cols, X_WR) * shift_up(se, se_s))
    de = e_c - se
    de_n = north[6:7, :] - se_n
    do_n = north[7:8, :] - (wl_x * se_n + wr_x * se[0:1, :])
    de_s = south[0:1, :] - se_s
    loads_c = (
        column(cols, X_K1) * shift_down(de, de_n)
        + column(cols, X_K2) * shift_down(do, do_n)
        + column(cols, X_K3) * de
        + column(cols, X_K4) * do
        + column(cols, X_K5) * shift_up(de, de_s)
    )
    hi, lo = split(loads_c)
    lch[...] = hi
    lcl[...] = lo
    er[...] = e_c

    stack[0:8, :] = north
    stack[8:16, :] = south
    corner = stack[...].T
    corner_n = corner[2 * PLANES : 3 * PLANES, 6:7]
    corner_s = corner[2 * PLANES : 3 * PLANES, 8:9]
    odd = (lane_z & 1) == 1

    def row_along_y(layer, scale, corner_col):
        tiles_in = [layer[t] * scale for t in range(2)]
        next_in = [pltpu.roll(v, LANES - 1, 1) for v in tiles_in]
        after = [
            jnp.where(lane_z < LANES - 1, next_in[0], next_in[1]),
            jnp.where(lane_z < LANES - 1, next_in[1], corner_col),
        ]
        result = []
        for t in range(2):
            part = slice(t * LANES, (t + 1) * LANES)
            guess = ycoef[0:1, part] * pltpu.roll(tiles_in[t], 1, 1) + ycoef[1:2, part] * after[t]
            result.append(jnp.where(odd, guess, tiles_in[t]))
        return tiles_in, result

    e_n, s_n = row_along_y(rrecv[0], has_up, corner_n)
    e_s, s_s = row_along_y(rrecv[2], has_down, corner_s)
    for t in range(2):
        rh[0, t] = e_n[t] - s_n[t]
        rh[1, t] = rrecv[1, t] * has_up - wl_x * s_n[t]
        rh[2, t] = s_s[t]
        rh[3, t] = e_s[t] - s_s[t]


def main_kernel(
    box, colx, ycoef, scal, rh, er, lch, lcl, wcat, gxh, gxl,
    detail, local, wide, se_buf, de_buf, do_buf, woven, high, low, sem,
):
    for k in range(7):
        wide[k] = column(colx[...], k)
    lane = iota((LANES, LANES), 1)
    odd = (lane & 1) == 1
    inner = lane < LANES - 1
    wrm = scal[S_WRM : S_WRM + 1, :]
    body, before, after = pl.ds(8, LANES), pl.ds(7, LANES), pl.ds(9, LANES)
    turns = PLANES // PER

    def stencil(z, k, slot):
        row = pl.ds(z, 1)
        e = [box[t, z, pl.ds(0, LANES, stride=2), :] for t in range(2)]
        o = [box[t, z, pl.ds(1, LANES, stride=2), :] for t in range(2)]
        nxt = [pltpu.roll(v, LANES - 1, 1) for v in e]
        beyond = pltpu.roll(er[...], lax.rem(3 * LANES - 1 - 2 * PLANES - z, LANES), 1)
        nxt = [jnp.where(inner, nxt[0], nxt[1]), jnp.where(inner, nxt[1], beyond)]
        for t in range(2):
            part = slice(t * LANES, (t + 1) * LANES)
            guess = ycoef[0:1, part] * pltpu.roll(e[t], 1, 1) + ycoef[1:2, part] * nxt[t]
            se = jnp.where(odd, guess, e[t])
            de = e[t] - se
            se_buf[k, t, body, :] = se
            se_buf[k, t, pl.ds(8 + LANES, 1), :] = rh[2, t, row, :]
            do = o[t] - (wide[X_WL] * se + wide[X_WR] * se_buf[k, t, after, :])
            woven[slot, k, t, pl.ds(0, LANES, stride=2), :] = de
            woven[slot, k, t, pl.ds(1, LANES, stride=2), :] = do
            de_buf[k, t, body, :] = de
            de_buf[k, t, pl.ds(7, 1), :] = rh[0, t, row, :]
            de_buf[k, t, pl.ds(8 + LANES, 1), :] = rh[3, t, row, :]
            do_buf[k, t, body, :] = do
            do_buf[k, t, pl.ds(7, 1), :] = rh[1, t, row, :] - wrm * se[0:1, :]
            load = (
                wide[X_K3] * de
                + wide[X_K4] * do
                + wide[X_K1] * de_buf[k, t, before, :]
                + wide[X_K2] * do_buf[k, t, before, :]
                + wide[X_K5] * de_buf[k, t, after, :]
            )
            hi, lo = split(load)
            high[slot, k, :, part] = hi
            low[slot, k, :, part] = lo
        mine = (lane & (PLANES - 1)) == z
        high[slot, k, :, FINE:] = jnp.where(mine, lch[...].astype(F32), 0.0).astype(BF16)
        low[slot, k, :, FINE:] = jnp.where(mine, lcl[...].astype(F32), 0.0).astype(BF16)

    def solve(z, slot):
        pairs = []
        for k in range(0, PER, 2):
            pair = []
            for n in (k, k + 1):
                both = mxu(high[slot, n], wcat[...])
                rest = mxu(low[slot, n], wcat[:, 0:LANES])
                pair.append(both[:, :LANES] + both[:, LANES:] + rest)
            pairs.append(jnp.concatenate(pair, axis=1))
        for k in range(0, PER, 2):
            hi, lo = split(pairs[k // 2])
            solved = mxu(gxh[...], hi) + (mxu(gxh[...], lo) + mxu(gxl[...], hi))
            local[z + k] = solved[:, :LANES]
            local[z + k + 1] = solved[:, LANES:]

    def writes(it, slot):
        return [
            pltpu.make_async_copy(
                woven.at[slot, :, t],
                detail.at[pl.ds(PER * it, PER), :, pl.ds(t * LANES, LANES)],
                sem.at[slot, t],
            )
            for t in range(2)
        ]

    def step(it, carry):
        slot = lax.rem(it, 2)

        @pl.when(it >= 2)
        def _():
            for write in writes(it - 2, slot):
                write.wait()

        solve(PER * it - PER, 1 - slot)
        for k in range(PER):
            stencil(PER * it + k, k, slot)
        for write in writes(it, slot):
            write.start()
        return carry

    for k in range(PER):
        stencil(k, k, 0)
    for write in writes(0, 0):
        write.start()
    lax.fori_loop(1, turns, step, 0)
    solve(PLANES - PER, (turns - 1) % 2)
    for it in (turns - 2, turns - 1):
        for write in writes(it, it % 2):
            write.wait()


def exchange_kernel(
    nx, ny, local, box, colx, scal, cf, cb, packed, mid, outer_l, outer_r,
    xs, xr, ys, yr, cs, cr, ks, kr, sums, uwide, pwide,
    sx_sem, rx_sem, sy_sem, ry_sem, sc_sem, rc_sem, sk_sem, rk_sem,
):
    p, r = lax.axis_index("gx"), lax.axis_index("gy")
    barrier = pltpu.get_barrier_semaphore()
    for k in range(1, nx):
        pl.semaphore_signal(barrier, inc=1, device_id=(lax.rem(p + k, nx), r), device_id_type=MESH)
    for k in range(1, ny):
        pl.semaphore_signal(barrier, inc=1, device_id=(p, lax.rem(r + k, ny)), device_id_type=MESH)
    tail, front = local[:, LANES - 1, :], local[:, 0, :]
    xs[0] = tail * scal[S_FX : S_FX + 1, :]
    xs[1] = front * scal[S_BX : S_BX + 1, :]
    ends = jnp.concatenate([tail, front, tail, front], axis=0).T
    lane_1 = iota((1, LANES), 1)

    def spread_planes(row):
        row = jnp.where(lane_1 < PLANES, row, 0.0)
        row = row + pltpu.roll(row, PLANES, 1)
        return row + pltpu.roll(row, 2 * PLANES, 1)

    ks[...] = jnp.zeros((2, 8, LANES), F32)
    for n, at in enumerate((LANES - 1, 0)):
        corner = ends[at : at + 1, :]
        ks[0, n : n + 1, :] = spread_planes(corner) * scal[S_FX : S_FX + 1, :]
        ks[1, n : n + 1, :] = spread_planes(pltpu.roll(corner, LANES - PLANES, 1)) * scal[S_BX : S_BX + 1, :]
    uwide[...] = column(colx[...], X_U)
    pwide[...] = column(colx[...], X_PSI)

    def start(sent, got, send_sem, recv_sem, own, count, target):
        copies = []
        for k in range(1, count):
            wraps = jnp.where(own + k >= count, 1, 0)
            copies.append(
                pltpu.make_async_remote_copy(
                    src_ref=sent.at[wraps], dst_ref=got.at[k - 1],
                    send_sem=send_sem.at[k - 1], recv_sem=recv_sem.at[k - 1],
                    device_id=target(lax.rem(own + k, count)), device_id_type=MESH,
                )
            )
            copies[-1].start()
        return copies

    def gather(copies, got, own, count, low):
        forward = backward = 0.0
        for k in range(1, count):
            copies[k - 1].wait_recv()
            row = pl.ds(low + lax.rem(own + count - k, count), 1)
            values = got[k - 1]
            forward = forward + cf[row, :] * values
            backward = backward + cb[row, :] * values
        return forward, backward


    lane = iota((PLANES, LANES), 1)
    blocks = LANES // PLANES

    def edges(z, carry):
        last, head = carry
        for m in range(blocks):
            block = local[z, pl.ds(m * PLANES, PLANES), :]
            here = lane == m * PLANES + z
            last = jnp.where(here, block[:, LANES - 1 : LANES], last)
            head = jnp.where(here, block[:, 0:1], head)
        return last, head

    zero = jnp.zeros((PLANES, LANES), F32)
    last, head = lax.fori_loop(0, PLANES, edges, (zero, zero), unroll=4)
    scale_f, scale_b = scal[S_FY : S_FY + 1, :], scal[S_BY : S_BY + 1, :]
    ys[0] = last * scale_f
    ys[1] = head * scale_b
    pl.semaphore_wait(barrier, nx + ny - 2)
    k_copies = start(ks, kr, sk_sem, rk_sem, p, nx, lambda i: (i, r))
    x_copies = start(xs, xr, sx_sem, rx_sem, p, nx, lambda i: (i, r))
    y_copies = start(ys, yr, sy_sem, ry_sem, r, ny, lambda j: (p, j))

    corner_f, corner_b = gather(k_copies, kr, p, nx, 0)
    cs[...] = jnp.zeros((2, 8, LANES), F32)
    cs[0, 0:1, :] = corner_f[0:1, :] * scale_f
    cs[0, 1:2, :] = corner_b[0:1, :] * scale_f
    cs[1, 0:1, :] = corner_f[1:2, :] * scale_b
    cs[1, 1:2, :] = corner_b[1:2, :] * scale_b
    c_copies = start(cs, cr, sc_sem, rc_sem, r, ny, lambda j: (p, j))
    forward, backward = gather(x_copies, xr, p, nx, 0)
    sums[0] = forward
    sums[1] = backward

    edge = jnp.where(
        (iota((LANES, LANES), 0) // PLANES) % 2 == 0,
        scal[S_UY : S_UY + 1, :], scal[S_PSIY : S_PSIY + 1, :],
    )
    edge_h = edge.astype(BF16).astype(F32)
    edge_l = edge - edge_h
    plane_of = iota((LANES, LANES), 0) % PLANES

    lane_w = iota((LANES, LANES), 1)
    pick = (2 * lane_w) & (LANES - 1)

    def x_part(z, carry):
        row = pl.ds(z, 1)
        left, right = (
            jnp.take_along_axis(
                box[t, z, pl.ds(0, LANES, stride=2), :], pick, axis=1, mode="promise_in_bounds"
            )
            for t in range(2)
        )
        coarse = jnp.where(lane_w < LANES // 2, left, right)
        mid[z] = local[z] + coarse + uwide[...] * sums[0, row, :] + pwide[...] * sums[1, row, :]
        outer_r[z, 0:LANES, :] = jnp.where(plane_of == z, edge_h, 0.0).astype(BF16)
        outer_r[z, LANES:, :] = jnp.where(plane_of == z, edge_l, 0.0).astype(BF16)
        return carry

    lax.fori_loop(0, PLANES, x_part, 0, unroll=2)
    u_x, psi_x = packed[0], packed[1]
    forward, backward = gather(y_copies, yr, r, ny, nx)
    extra_f, extra_b = gather(c_copies, cr, r, ny, nx)
    forward = forward + u_x * extra_f[0:1, :] + psi_x * extra_f[1:2, :]
    backward = backward + u_x * extra_b[0:1, :] + psi_x * extra_b[1:2, :]
    lane = iota((LANES, LANES), 1)

    def spread(values):
        return jnp.concatenate(
            [pltpu.roll(values, (LANES - m * PLANES) % LANES, 1) if m else values for m in range(blocks)],
            axis=0,
        )

    both = jnp.where(lane < PLANES, spread(forward), pltpu.roll(spread(backward), PLANES, 1))
    high = both.astype(BF16).astype(F32)
    both = jnp.where(lane < 2 * PLANES, high, pltpu.roll(both - high, 2 * PLANES, 1))
    outer_l[:, 0:LANES] = both.astype(BF16)
    outer_l[:, LANES:] = both.astype(BF16)
    for copy in k_copies + x_copies + y_copies + c_copies:
        copy.wait_send()


def final_kernel(mid, outer_l, outer_r, out, total, sem):
    writes = []
    for g in range(PLANES // 8):
        planes = pl.ds(g * 8, 8)
        for k in range(g * 8, g * 8 + 8, 2):
            pair = jnp.concatenate([outer_r[k], outer_r[k + 1]], axis=1)
            update = mxu(outer_l[...], pair)
            total[k] = mid[k] + update[:, :LANES]
            total[k + 1] = mid[k + 1] + update[:, LANES:]
        writes.append(pltpu.make_async_copy(total.at[planes], out.at[planes], sem.at[g]))
        writes[-1].start()
    for write in writes:
        write.wait()


def per_device(nx, ny, density, spacing_x, spacing_y):
    blocks = nx + ny
    hbm = pl.BlockSpec(memory_space=pltpu.HBM)
    vmem = pl.BlockSpec(memory_space=pltpu.VMEM)
    f32 = lambda *shape: jax.ShapeDtypeStruct(shape, F32)
    bf16 = lambda *shape: jax.ShapeDtypeStruct(shape, BF16)
    sx = spacing_x.reshape(2 * nx, LANES)
    sy = spacing_y.reshape(2 * ny, LANES)
    colx, ycoef, scal, cf, cb, wcat, gxh, gxl, rh, er, lch, lcl, packed, box = pl.pallas_call(
        functools.partial(prepare_kernel, nx, ny),
        out_shape=(
            f32(LANES, LANES), f32(8, FINE), f32(8, LANES), f32(blocks, LANES), f32(blocks, LANES),
            bf16(FINE + LANES, FINE), bf16(LANES, LANES), bf16(LANES, LANES),
            f32(4, 2, PLANES, LANES), f32(LANES, LANES), bf16(LANES, LANES), bf16(LANES, LANES),
            f32(2, PLANES, LANES), f32(2, PLANES, FINE, LANES),
        ),
        in_specs=[hbm] * 3,
        out_specs=(vmem,) * 14,
        scratch_shapes=[
            pltpu.VMEM((2 * nx, LANES), F32),
            pltpu.VMEM((2 * ny, LANES), F32),
            pltpu.VMEM((3, 2, PLANES, LANES), F32),
            pltpu.VMEM((FINE // 2, LANES), F32),
            pltpu.VMEM((FINE // 4, LANES), F32),
            pltpu.VMEM((3, 2, PLANES, LANES), F32),
            pltpu.VMEM((FINE // 2, LANES), F32),
            pltpu.VMEM((FINE // 4, LANES), F32),
            pltpu.VMEM((6, 8, LANES), F32),
            pltpu.VMEM((14, blocks, LANES), F32),
            pltpu.VMEM((3, blocks, LANES), F32),
            pltpu.VMEM((LANES, LANES), F32),
            pltpu.VMEM((FINE, LANES), F32),
            pltpu.SemaphoreType.DMA((2 * PLANES // STEP + 2,)),
            pltpu.SemaphoreType.DMA((10,)),
            pltpu.SemaphoreType.DMA((10,)),
        ],
        compiler_params=pltpu.CompilerParams(
            collective_id=0, has_side_effects=True, vmem_limit_bytes=32 * MIB
        ),
        name="prepare",
    )(*(pltpu.with_memory_space_constraint(v, pltpu.HBM) for v in (density, sx, sy)))
    tables = (colx, ycoef, scal, rh, er, lch, lcl, wcat, gxh, gxl)
    detail, local = pl.pallas_call(
        main_kernel,
        out_shape=(f32(PLANES, FINE, FINE), f32(PLANES, LANES, LANES)),
        in_specs=[vmem] * (1 + len(tables)),
        out_specs=(hbm, vmem),
        scratch_shapes=[
            pltpu.VMEM((7, LANES, LANES), F32),
            pltpu.VMEM((PER, 2, LANES + 16, LANES), F32),
            pltpu.VMEM((PER, 2, LANES + 16, LANES), F32),
            pltpu.VMEM((PER, 2, LANES + 16, LANES), F32),
            pltpu.VMEM((2, PER, 2, FINE, LANES), F32),
            pltpu.VMEM((2, PER, LANES, FINE + LANES), BF16),
            pltpu.VMEM((2, PER, LANES, FINE + LANES), BF16),
            pltpu.SemaphoreType.DMA((2, 2)),
        ],
        compiler_params=pltpu.CompilerParams(vmem_limit_bytes=32 * MIB),
        name="main",
    )(box, *tables)
    mid, outer_l, outer_r = pl.pallas_call(
        functools.partial(exchange_kernel, nx, ny),
        out_shape=(f32(PLANES, LANES, LANES), bf16(LANES, FINE), bf16(PLANES, FINE, LANES)),
        in_specs=[vmem] * 7,
        out_specs=(vmem,) * 3,
        scratch_shapes=[
            pltpu.VMEM((2, PLANES, LANES), F32),
            pltpu.VMEM((nx - 1, PLANES, LANES), F32),
            pltpu.VMEM((2, PLANES, LANES), F32),
            pltpu.VMEM((ny - 1, PLANES, LANES), F32),
            pltpu.VMEM((2, 8, LANES), F32),
            pltpu.VMEM((ny - 1, 8, LANES), F32),
            pltpu.VMEM((2, 8, LANES), F32),
            pltpu.VMEM((nx - 1, 8, LANES), F32),
            pltpu.VMEM((2, PLANES, LANES), F32),
            pltpu.VMEM((LANES, LANES), F32),
            pltpu.VMEM((LANES, LANES), F32),
            pltpu.SemaphoreType.DMA((nx - 1,)),
            pltpu.SemaphoreType.DMA((nx - 1,)),
            pltpu.SemaphoreType.DMA((ny - 1,)),
            pltpu.SemaphoreType.DMA((ny - 1,)),
            pltpu.SemaphoreType.DMA((ny - 1,)),
            pltpu.SemaphoreType.DMA((ny - 1,)),
            pltpu.SemaphoreType.DMA((nx - 1,)),
            pltpu.SemaphoreType.DMA((nx - 1,)),
        ],
        compiler_params=pltpu.CompilerParams(
            collective_id=1, has_side_effects=True, vmem_limit_bytes=32 * MIB
        ),
        name="exchange",
    )(local, box, colx, scal, cf, cb, packed)
    coarse_new = pl.pallas_call(
        final_kernel,
        out_shape=f32(PLANES, LANES, LANES),
        in_specs=[vmem] * 3,
        out_specs=hbm,
        scratch_shapes=[pltpu.VMEM((PLANES, LANES, LANES), F32), pltpu.SemaphoreType.DMA((PLANES // 8,))],
        compiler_params=pltpu.CompilerParams(vmem_limit_bytes=16 * MIB),
        name="final",
    )(mid, outer_l, outer_r)
    return detail, coarse_new


def solution(mesh):
    placed = P(None, "gx", "gy")
    return jax.shard_map(
        functools.partial(per_device, mesh.shape["gx"], mesh.shape["gy"]),
        mesh=mesh,
        in_specs=(placed, P(), P()),
        out_specs=(placed, placed),
        check_vma=False,
    )
```

```python
import functools

import jax
import jax.numpy as jnp
from jax import lax
from jax.experimental import pallas as pl
from jax.experimental.pallas import tpu as pltpu
from jax.sharding import PartitionSpec as P

MESH = pl.DeviceIdType.MESH
F32 = jnp.float32
BF16 = jnp.bfloat16
HIGHEST = lax.Precision.HIGHEST
stiffness_weight = 4096.0
operator_divisor = 32.0
LANES = 128
FINE = 256
PLANES = 32
PER = 8
STEP = 4
MIB = 1 << 20
X_WL, X_WR, X_K1, X_K2, X_K3, X_K4, X_K5, X_U, X_PSI, X_W = range(10)
Y_K1, Y_K2, Y_K3, Y_K4, Y_K5, Y_U, Y_W = range(10, 17)
S_FX, S_BX, S_FY, S_BY, S_WRM, S_UY, S_PSIY = range(7)


def split(values):
    high = values.astype(BF16)
    return high, (values - high.astype(F32)).astype(BF16)


def mxu(a, b):
    return jnp.dot(a, b, preferred_element_type=F32)


def iota(shape, dim):
    return lax.broadcasted_iota(jnp.int32, shape, dim)


def column(table, index):
    return jnp.broadcast_to(table[:, index : index + 1], (LANES, LANES))


def shift_up(values, last):
    rolled = pltpu.roll(values, LANES - 1, 0)
    return jnp.where(iota(values.shape, 0) == LANES - 1, last, rolled)


def shift_down(values, first):
    return jnp.where(iota(values.shape, 0) == 0, first, pltpu.roll(values, 1, 0))


def chain_tables(blocks_x, blocks_y, sx, sy, tab, rows_in):
    count = blocks_x + blocks_y
    shape = (count, LANES)
    lane, row = iota(shape, 1), iota(shape, 0)
    first = (lane == 0) & ((row == 0) | (row == blocks_x))

    def prev(values, fill):
        rolled = pltpu.roll(values, 1, 1)
        return jnp.where(first, fill, jnp.where(lane == 0, pltpu.roll(rolled, 1, 0), rolled))

    def following(values):
        rolled = pltpu.roll(values, LANES - 1, 1)
        return jnp.where(lane == LANES - 1, pltpu.roll(rolled, count - 1, 0), rolled)

    def halves(start):
        return jnp.concatenate(
            [sx[pl.ds(start, blocks_x, stride=2), :], sy[pl.ds(start, blocks_y, stride=2), :]], axis=0
        )

    fine = jnp.concatenate([halves(0), halves(1)], axis=1)
    node, place = iota((FINE, FINE), 0), iota((FINE, FINE), 1)
    pick = jnp.where(place < LANES, 2 * place, 2 * (place - LANES) + 1)
    parts = jnp.dot((fine), (node == pick).astype(F32), precision=HIGHEST, preferred_element_type=F32)
    c, d = parts[:, :LANES], parts[:, LANES:]
    span = c + d
    a, b = prev(c, 0.0), prev(d, 0.0)
    span_before = prev(span, 1.0)
    inverse = 1.0 / span
    inverse_before = 1.0 / span_before
    tab[0] = d * inverse
    tab[1] = c * inverse
    tab[2] = a * a * inverse_before * (1.0 / 6.0)
    tab[3] = a * (1.0 / 3.0) + b * (1.0 / 6.0)
    tab[4] = (a * b * inverse_before + c * d * inverse) * (1.0 / 6.0) + (b + c) * (1.0 / 3.0)
    tab[5] = c * (1.0 / 6.0) + d * (1.0 / 3.0)
    tab[6] = d * d * inverse * (1.0 / 6.0)
    tab[9] = b * inverse_before
    tab[10] = a * inverse_before

    rho = 1.0 / (stiffness_weight * inverse - span * (1.0 / 6.0))
    rho_before = prev(rho, 0.0)
    mu = 0.5 * (a + b + span)
    mu_after = following(mu)
    one = jnp.ones(shape, F32)
    fwd = (one + mu * rho_before, mu, rho_before, one)
    bwd = (one, mu_after, rho, one + rho * mu_after)
    step = 1
    while step < LANES:
        def join(m, shift, outside):
            fill = (1.0, 0.0, 0.0, 1.0)
            a1, b1, c1, d1 = m
            a0, b0, c0, d0 = (
                jnp.where(outside, f, pltpu.roll(v, shift, 1)) for v, f in zip(m, fill)
            )
            return (a1 * a0 + b1 * c0, a1 * b0 + b1 * d0, c1 * a0 + d1 * c0, c1 * b0 + d1 * d0)

        fwd = join(fwd, step, lane < step)
        bwd = join(bwd, LANES - step, lane >= LANES - step)
        step *= 2
    ends = [jnp.broadcast_to(v[:, LANES - 1 : LANES], shape) for v in fwd]
    starts = [jnp.broadcast_to(v[:, 0:1], shape) for v in bwd]
    for low, size in ((0, blocks_x), (blocks_x, blocks_y)):
        y = jnp.zeros((1, LANES), F32)
        for q in range(low, low + size):
            rows_in[0, q : q + 1, :] = y
            at, bt, ct, dt = (v[q : q + 1, :] for v in ends)
            y = (at * y + bt) / (ct * y + dt)
        z = None
        for q in reversed(range(low, low + size)):
            at, bt, ct, dt = (v[q : q + 1, :] for v in starts)
            if z is None:
                rows_in[1, q : q + 1, :] = jnp.ones((1, LANES), F32)
                rows_in[2, q : q + 1, :] = jnp.zeros((1, LANES), F32)
                z = at / ct
            else:
                rows_in[1, q : q + 1, :] = z
                rows_in[2, q : q + 1, :] = jnp.ones((1, LANES), F32)
                z = (at * z + bt) / (ct * z + dt)
    y_in, z_num, z_den = rows_in[0], rows_in[1], rows_in[2]
    den = fwd[2] * y_in + fwd[3]
    left = (fwd[0] * y_in + fwd[1]) / den
    right = (bwd[0] * z_num + bwd[1] * z_den) / (bwd[2] * z_num + bwd[3] * z_den)
    green = operator_divisor / (left + right)
    tab[7] = green / den
    tab[8] = den
    tab[11] = 1.0 / jnp.broadcast_to(den[:, LANES - 1 : LANES], shape)
    tab[12] = 1.0 / jnp.broadcast_to(green[:, LANES - 1 : LANES], shape)
    tab[13] = 1.0 / jnp.broadcast_to(den[:, 0:1], shape)


def weights_between(gain, low, size, own, forward, backward):
    q = iota((size, LANES), 0)
    ahead = jnp.ones((size, LANES), F32)
    behind = jnp.ones((size, LANES), F32)
    for m in range(size):
        g = gain[low + m : low + m + 1, :]
        ahead = ahead * jnp.where((m > q) & (m < own), g, 1.0)
        behind = behind * jnp.where((m < q) & (m > own), g, 1.0)
    forward[low : low + size, :] = jnp.where(q < own, ahead, 0.0)
    backward[low : low + size, :] = jnp.where(q > own, behind, 0.0)


def green_block(u_col, w_col, u_row, w_row):
    i, j = iota((LANES, LANES), 0), iota((LANES, LANES), 1)
    return jnp.where(i >= j, u_col * w_row, w_col * u_row)


def prepare_kernel(
    nx, ny, dens, sx_in, sy_in,
    colx, ycoef, scal, cf, cb, wcat, gxh, gxl, rh, er, lch, lcl, packed, box,
    sx, sy, rsend, to_right, to_left, rrecv, from_left, from_right, tiles,
    tab, rows_in, stack, wfine, load_sem, send_sem, recv_sem,
):
    p, r = lax.axis_index("gx"), lax.axis_index("gy")
    up, down = lax.rem(p + nx - 1, nx), lax.rem(p + 1, nx)
    left, right = lax.rem(r + ny - 1, ny), lax.rem(r + 1, ny)
    loads = []
    for k in range(PLANES // STEP):
        part = pl.ds(k * STEP, STEP)
        for t in range(2):
            loads.append(
                pltpu.make_async_copy(
                    dens.at[part, :, pl.ds(t * LANES, LANES)], box.at[t, part], load_sem.at[2 * k + t]
                )
            )
            loads[-1].start()
    for k, (src, dst) in enumerate(((sx_in, sx), (sy_in, sy))):
        loads.append(pltpu.make_async_copy(src, dst, load_sem.at[2 * PLANES // STEP + k]))
        loads[-1].start()
    barrier = pltpu.get_barrier_semaphore()
    for i in (up, p, down):
        for j in (left, r, right):
            if i is p and j is r:
                continue
            pl.semaphore_signal(barrier, inc=1, device_id=(i, j), device_id_type=MESH)

    right_rows, left_rows = FINE // 2, FINE // 4
    lane_r, lane_l = iota((right_rows, LANES), 1), iota((left_rows, LANES), 1)
    to_right[...] = jnp.zeros((right_rows, LANES), F32)
    to_left[...] = jnp.zeros((left_rows, LANES), F32)
    for k in range(PLANES // STEP):
        loads[2 * k].wait()
        loads[2 * k + 1].wait()
        acc_r, acc_l = to_right[...], to_left[...]
        for zi in range(STEP):
            z = k * STEP + zi
            for m in range(2):
                rows = slice(m * right_rows, (m + 1) * right_rows)
                at = 2 * m * PLANES + z
                acc_r = jnp.where(lane_r == at, box[1, z, rows, LANES - 2 : LANES - 1], acc_r)
                acc_r = jnp.where(lane_r == at + PLANES, box[1, z, rows, LANES - 1 : LANES], acc_r)
            for m in range(4):
                rows = slice(m * left_rows, (m + 1) * left_rows)
                acc_l = jnp.where(lane_l == m * PLANES + z, box[0, z, rows, 0:1], acc_l)
            for t in range(2):
                rsend[0, t, z : z + 1, :] = box[t, z, FINE - 2 : FINE - 1, :]
                rsend[1, t, z : z + 1, :] = box[t, z, FINE - 1 : FINE, :]
                rsend[2, t, z : z + 1, :] = box[t, z, 0:1, :]
        to_right[...] = acc_r
        to_left[...] = acc_l

    pl.semaphore_wait(barrier, 8)
    top = pl.ds(0, 8)
    end_r, end_l = pl.ds(right_rows - 8, 8), pl.ds(left_rows - 8, 8)
    plan = (
        (to_right, from_left, p, right),
        (to_left, from_right, p, left),
        (rsend.at[pl.ds(0, 2)], rrecv.at[pl.ds(0, 2)], down, r),
        (rsend.at[pl.ds(2, 1)], rrecv.at[pl.ds(2, 1)], up, r),
        (to_left.at[end_l], tiles.at[0], down, r),
        (to_left.at[top], tiles.at[1], up, r),
        (to_right.at[end_r], tiles.at[2], down, right),
        (to_left.at[end_l], tiles.at[3], down, left),
        (to_right.at[top], tiles.at[4], up, right),
        (to_left.at[top], tiles.at[5], up, left),
    )
    copies = []
    for k, (src, dst, i, j) in enumerate(plan):
        copies.append(
            pltpu.make_async_remote_copy(
                src_ref=src, dst_ref=dst, send_sem=send_sem.at[k], recv_sem=recv_sem.at[k],
                device_id=(i, j), device_id_type=MESH,
            )
        )
        copies[-1].start()

    for load in loads[2 * PLANES // STEP :]:
        load.wait()
    chain_tables(nx, ny, sx, sy, tab, rows_in)
    weights_between(tab[11], 0, nx, p, cf, cb)
    weights_between(tab[11], nx, ny, r, cf, cb)
    row_x, row_y = pl.ds(p, 1), pl.ds(nx + r, 1)
    ux, wx, uy, wy = tab[7, row_x, :], tab[8, row_x, :], tab[7, row_y, :], tab[8, row_y, :]
    stack[...] = jnp.zeros((LANES, LANES), F32)
    for k in range(7):
        stack[k : k + 1, :] = tab[k, row_x, :]
    stack[X_U : X_U + 1, :] = ux
    stack[X_PSI : X_PSI + 1, :] = wx * tab[11, row_x, :]
    stack[X_W : X_W + 1, :] = wx
    for k in range(5):
        stack[Y_K1 + k : Y_K1 + k + 1, :] = tab[2 + k, row_y, :]
    stack[Y_U : Y_U + 1, :] = uy
    stack[Y_W : Y_W + 1, :] = wy
    cols = stack[...].T
    colx[...] = cols
    scal[...] = jnp.zeros((8, LANES), F32)
    scal[S_FX : S_FX + 1, :] = tab[12, row_x, :]
    scal[S_BX : S_BX + 1, :] = tab[13, row_x, :]
    scal[S_FY : S_FY + 1, :] = tab[12, row_y, :]
    scal[S_BY : S_BY + 1, :] = tab[13, row_y, :]
    wl_x = tab[9, row_x, :][:, 0:1]
    wr_x = tab[10, row_x, :][:, 0:1]
    wl_y = tab[9, row_y, :][:, 0:1]
    wr_y = tab[10, row_y, :][:, 0:1]
    scal[S_WRM : S_WRM + 1, :] = jnp.broadcast_to(wr_x, (1, LANES))
    scal[S_UY : S_UY + 1, :] = uy
    scal[S_PSIY : S_PSIY + 1, :] = wy * tab[11, row_y, :]

    lane_z = iota((PLANES, LANES), 1)
    for k, index in enumerate((X_U, X_PSI)):
        packed[k] = sum(
            jnp.where(lane_z // PLANES == m, cols[m * PLANES : (m + 1) * PLANES, index : index + 1], 0.0)
            for m in range(LANES // PLANES)
        )

    odd_row = (iota((1, LANES), 1) & 1) == 1
    ycoef[...] = jnp.zeros((8, FINE), F32)
    for t in range(2):
        h = sy[pl.ds(2 * r + t, 1), :]
        hp = pltpu.roll(h, 1, 1)
        inv = 1.0 / (h + hp)
        ycoef[0:1, t * LANES : (t + 1) * LANES] = jnp.where(odd_row, h * inv, 0.0)
        ycoef[1:2, t * LANES : (t + 1) * LANES] = jnp.where(odd_row, hp * inv, 0.0)

    hi, lo = split(green_block(column(cols, X_U), column(cols, X_W), ux, wx))
    gxh[...] = hi
    gxl[...] = lo
    gy = green_block(column(cols, Y_U), column(cols, Y_W), uy, wy)
    g1, g2, g3, g4, g5 = (column(cols, Y_K1 + k) * gy for k in range(5))
    wfine[pl.ds(0, LANES, stride=2), :] = g3 + shift_down(g5, 0.0) + shift_up(g1, 0.0)
    wfine[pl.ds(1, LANES, stride=2), :] = g4 + shift_up(g2, 0.0)
    i = iota((LANES, LANES), 0)
    outer = jnp.where(
        i < PLANES, g1[0:1, :],
        jnp.where(i < 2 * PLANES, g2[0:1, :], jnp.where(i < 3 * PLANES, g5[LANES - 1 : LANES, :], 0.0)),
    )
    hi, lo = split(wfine[...])
    wcat[0:FINE, 0:LANES] = hi
    wcat[0:FINE, LANES:FINE] = lo
    hi, lo = split(outer)
    wcat[FINE : FINE + LANES, 0:LANES] = hi
    wcat[FINE : FINE + LANES, LANES:FINE] = lo

    for copy in copies:
        copy.wait()

    has_up = (p > 0).astype(F32)
    has_down = (p < nx - 1).astype(F32)
    has_left = (r > 0).astype(F32)
    has_right = (r < ny - 1).astype(F32)
    lane_8 = iota((8, LANES), 1)
    lane = iota((LANES, LANES), 1)

    def unpack(ref, start, shifts):
        values = ref[pl.ds(start, LANES // len(shifts), stride=2), :]
        return jnp.concatenate([pltpu.roll(values, n, 1) if n else values for n in shifts], axis=0)

    e_c, o_c = (
        jnp.where(
            lane < 2 * PLANES,
            unpack(from_left, start, (0, 64)) * has_left,
            unpack(from_right, start, (64, 32, 0, 96)) * has_right,
        )
        for start in range(2)
    )
    own = unpack(to_left, 0, (32, 0, 96, 64))
    own_n = pltpu.roll(tiles[0], 64, 1) * has_up
    own_s = pltpu.roll(tiles[1], 32, 1) * has_down
    north = (
        jnp.where(
            lane_8 < 2 * PLANES,
            pltpu.roll(tiles[2], 64, 1) * has_left,
            pltpu.roll(tiles[3], 96, 1) * has_right,
        )
        * has_up
    )
    south = (
        jnp.where(lane_8 < 2 * PLANES, tiles[4] * has_left, pltpu.roll(tiles[5], 64, 1) * has_right)
        * has_down
    )

    def along_y(values, own_values):
        at = iota(values.shape, 1)
        guess = wl_y * pltpu.roll(values, PLANES, 1) + wr_y * own_values
        return jnp.where((at >= PLANES) & (at < 2 * PLANES), guess, values)

    se = along_y(e_c, own)
    se_n = along_y(north, own_n)[6:7, :]
    se_s = along_y(south, own_s)[0:1, :]
    do = o_c - (column(cols, X_WL) * se + column(cols, X_WR) * shift_up(se, se_s))
    de = e_c - se
    de_n = north[6:7, :] - se_n
    do_n = north[7:8, :] - (wl_x * se_n + wr_x * se[0:1, :])
    de_s = south[0:1, :] - se_s
    loads_c = (
        column(cols, X_K1) * shift_down(de, de_n)
        + column(cols, X_K2) * shift_down(do, do_n)
        + column(cols, X_K3) * de
        + column(cols, X_K4) * do
        + column(cols, X_K5) * shift_up(de, de_s)
    )
    hi, lo = split(loads_c)
    lch[...] = hi
    lcl[...] = lo
    er[...] = e_c

    stack[0:8, :] = north
    stack[8:16, :] = south
    corner = stack[...].T
    corner_n = corner[2 * PLANES : 3 * PLANES, 6:7]
    corner_s = corner[2 * PLANES : 3 * PLANES, 8:9]
    odd = (lane_z & 1) == 1

    def row_along_y(layer, scale, corner_col):
        tiles_in = [layer[t] * scale for t in range(2)]
        next_in = [pltpu.roll(v, LANES - 1, 1) for v in tiles_in]
        after = [
            jnp.where(lane_z < LANES - 1, next_in[0], next_in[1]),
            jnp.where(lane_z < LANES - 1, next_in[1], corner_col),
        ]
        result = []
        for t in range(2):
            part = slice(t * LANES, (t + 1) * LANES)
            guess = ycoef[0:1, part] * pltpu.roll(tiles_in[t], 1, 1) + ycoef[1:2, part] * after[t]
            result.append(jnp.where(odd, guess, tiles_in[t]))
        return tiles_in, result

    e_n, s_n = row_along_y(rrecv[0], has_up, corner_n)
    e_s, s_s = row_along_y(rrecv[2], has_down, corner_s)
    for t in range(2):
        rh[0, t] = e_n[t] - s_n[t]
        rh[1, t] = rrecv[1, t] * has_up - wl_x * s_n[t]
        rh[2, t] = s_s[t]
        rh[3, t] = e_s[t] - s_s[t]


def main_kernel(
    box, colx, ycoef, scal, rh, er, lch, lcl, wcat, gxh, gxl,
    detail, local, wide, se_buf, de_buf, do_buf, woven, high, low, sem,
):
    for k in range(7):
        wide[k] = column(colx[...], k)
    lane = iota((LANES, LANES), 1)
    odd = (lane & 1) == 1
    inner = lane < LANES - 1
    wrm = scal[S_WRM : S_WRM + 1, :]
    body, before, after = pl.ds(8, LANES), pl.ds(7, LANES), pl.ds(9, LANES)
    turns = PLANES // PER

    def stencil(z, k, slot):
        row = pl.ds(z, 1)
        e = [box[t, z, pl.ds(0, LANES, stride=2), :] for t in range(2)]
        o = [box[t, z, pl.ds(1, LANES, stride=2), :] for t in range(2)]
        nxt = [pltpu.roll(v, LANES - 1, 1) for v in e]
        beyond = pltpu.roll(er[...], lax.rem(3 * LANES - 1 - 2 * PLANES - z, LANES), 1)
        nxt = [jnp.where(inner, nxt[0], nxt[1]), jnp.where(inner, nxt[1], beyond)]
        for t in range(2):
            part = slice(t * LANES, (t + 1) * LANES)
            guess = ycoef[0:1, part] * pltpu.roll(e[t], 1, 1) + ycoef[1:2, part] * nxt[t]
            se = jnp.where(odd, guess, e[t])
            de = e[t] - se
            se_buf[k, t, body, :] = se
            se_buf[k, t, pl.ds(8 + LANES, 1), :] = rh[2, t, row, :]
            do = o[t] - (wide[X_WL] * se + wide[X_WR] * se_buf[k, t, after, :])
            woven[slot, k, t, pl.ds(0, LANES, stride=2), :] = de
            woven[slot, k, t, pl.ds(1, LANES, stride=2), :] = do
            de_buf[k, t, body, :] = de
            de_buf[k, t, pl.ds(7, 1), :] = rh[0, t, row, :]
            de_buf[k, t, pl.ds(8 + LANES, 1), :] = rh[3, t, row, :]
            do_buf[k, t, body, :] = do
            do_buf[k, t, pl.ds(7, 1), :] = rh[1, t, row, :] - wrm * se[0:1, :]
            load = (
                wide[X_K3] * de
                + wide[X_K4] * do
                + wide[X_K1] * de_buf[k, t, before, :]
                + wide[X_K2] * do_buf[k, t, before, :]
                + wide[X_K5] * de_buf[k, t, after, :]
            )
            hi, lo = split(load)
            high[slot, k, :, part] = hi
            low[slot, k, :, part] = lo
        mine = (lane & (PLANES - 1)) == z
        high[slot, k, :, FINE:] = jnp.where(mine, lch[...].astype(F32), 0.0).astype(BF16)
        low[slot, k, :, FINE:] = jnp.where(mine, lcl[...].astype(F32), 0.0).astype(BF16)

    def solve(z, slot):
        pairs = []
        for k in range(0, PER, 2):
            pair = []
            for n in (k, k + 1):
                both = mxu(high[slot, n], wcat[...])
                rest = mxu(low[slot, n], wcat[:, 0:LANES])
                pair.append(both[:, :LANES] + both[:, LANES:] + rest)
            pairs.append(jnp.concatenate(pair, axis=1))
        for k in range(0, PER, 2):
            hi, lo = split(pairs[k // 2])
            solved = mxu(gxh[...], hi) + (mxu(gxh[...], lo) + mxu(gxl[...], hi))
            local[z + k] = solved[:, :LANES]
            local[z + k + 1] = solved[:, LANES:]

    def writes(it, slot):
        return [
            pltpu.make_async_copy(
                woven.at[slot, :, t],
                detail.at[pl.ds(PER * it, PER), :, pl.ds(t * LANES, LANES)],
                sem.at[slot, t],
            )
            for t in range(2)
        ]

    def step(it, carry):
        slot = lax.rem(it, 2)

        @pl.when(it >= 2)
        def _():
            for write in writes(it - 2, slot):
                write.wait()

        solve(PER * it - PER, 1 - slot)
        for k in range(PER):
            stencil(PER * it + k, k, slot)
        for write in writes(it, slot):
            write.start()
        return carry

    for k in range(PER):
        stencil(k, k, 0)
    for write in writes(0, 0):
        write.start()
    lax.fori_loop(1, turns, step, 0)
    solve(PLANES - PER, (turns - 1) % 2)
    for it in (turns - 2, turns - 1):
        for write in writes(it, it % 2):
            write.wait()


def exchange_kernel(
    nx, ny, local, box, colx, scal, cf, cb, packed, mid, outer_l, outer_r,
    xs, xr, ys, yr, cs, cr, ks, kr, sums, uwide, pwide,
    sx_sem, rx_sem, sy_sem, ry_sem, sc_sem, rc_sem, sk_sem, rk_sem,
):
    p, r = lax.axis_index("gx"), lax.axis_index("gy")
    barrier = pltpu.get_barrier_semaphore()
    for k in range(1, nx):
        pl.semaphore_signal(barrier, inc=1, device_id=(lax.rem(p + k, nx), r), device_id_type=MESH)
    for k in range(1, ny):
        pl.semaphore_signal(barrier, inc=1, device_id=(p, lax.rem(r + k, ny)), device_id_type=MESH)
    tail, front = local[:, LANES - 1, :], local[:, 0, :]
    xs[0] = tail * scal[S_FX : S_FX + 1, :]
    xs[1] = front * scal[S_BX : S_BX + 1, :]
    ends = jnp.concatenate([tail, front, tail, front], axis=0).T
    lane_1 = iota((1, LANES), 1)

    def spread_planes(row):
        row = jnp.where(lane_1 < PLANES, row, 0.0)
        row = row + pltpu.roll(row, PLANES, 1)
        return row + pltpu.roll(row, 2 * PLANES, 1)

    ks[...] = jnp.zeros((2, 8, LANES), F32)
    for n, at in enumerate((LANES - 1, 0)):
        corner = ends[at : at + 1, :]
        ks[0, n : n + 1, :] = spread_planes(corner) * scal[S_FX : S_FX + 1, :]
        ks[1, n : n + 1, :] = spread_planes(pltpu.roll(corner, LANES - PLANES, 1)) * scal[S_BX : S_BX + 1, :]

    def start(sent, got, send_sem, recv_sem, own, count, target):
        copies = [None] * (count - 1)
        for k in sorted(range(1, count), key=lambda k: abs(count - 2 * k)):
            wraps = jnp.where(own + k >= count, 1, 0)
            copies[k - 1] = pltpu.make_async_remote_copy(
                src_ref=sent.at[wraps], dst_ref=got.at[k - 1],
                send_sem=send_sem.at[k - 1], recv_sem=recv_sem.at[k - 1],
                device_id=target(lax.rem(own + k, count)), device_id_type=MESH,
            )
            copies[k - 1].start()
        return copies

    def gather(copies, got, own, count, low):
        forward = backward = 0.0
        for k in range(1, count):
            copies[k - 1].wait_recv()
            row = pl.ds(low + lax.rem(own + count - k, count), 1)
            values = got[k - 1]
            forward = forward + cf[row, :] * values
            backward = backward + cb[row, :] * values
        return forward, backward


    lane = iota((PLANES, LANES), 1)
    blocks = LANES // PLANES

    def edges(z, carry):
        last, head = carry
        for m in range(blocks):
            block = local[z, pl.ds(m * PLANES, PLANES), :]
            here = lane == m * PLANES + z
            last = jnp.where(here, block[:, LANES - 1 : LANES], last)
            head = jnp.where(here, block[:, 0:1], head)
        return last, head

    zero = jnp.zeros((PLANES, LANES), F32)
    last, head = lax.fori_loop(0, PLANES, edges, (zero, zero), unroll=4)
    scale_f, scale_b = scal[S_FY : S_FY + 1, :], scal[S_BY : S_BY + 1, :]
    ys[0] = last * scale_f
    ys[1] = head * scale_b
    pl.semaphore_wait(barrier, nx + ny - 2)
    k_copies = start(ks, kr, sk_sem, rk_sem, p, nx, lambda i: (i, r))
    x_copies = start(xs, xr, sx_sem, rx_sem, p, nx, lambda i: (i, r))
    y_copies = start(ys, yr, sy_sem, ry_sem, r, ny, lambda j: (p, j))

    corner_f, corner_b = gather(k_copies, kr, p, nx, 0)
    cs[...] = jnp.zeros((2, 8, LANES), F32)
    cs[0, 0:1, :] = corner_f[0:1, :] * scale_f
    cs[0, 1:2, :] = corner_b[0:1, :] * scale_f
    cs[1, 0:1, :] = corner_f[1:2, :] * scale_b
    cs[1, 1:2, :] = corner_b[1:2, :] * scale_b
    c_copies = start(cs, cr, sc_sem, rc_sem, r, ny, lambda j: (p, j))
    uwide[...] = column(colx[...], X_U)
    pwide[...] = column(colx[...], X_PSI)
    forward, backward = gather(x_copies, xr, p, nx, 0)
    sums[0] = forward
    sums[1] = backward

    edge = jnp.where(
        (iota((LANES, LANES), 0) // PLANES) % 2 == 0,
        scal[S_UY : S_UY + 1, :], scal[S_PSIY : S_PSIY + 1, :],
    )
    edge_h = edge.astype(BF16).astype(F32)
    edge_l = edge - edge_h
    plane_of = iota((LANES, LANES), 0) % PLANES

    lane_w = iota((LANES, LANES), 1)
    pick = (2 * lane_w) & (LANES - 1)

    def x_part(z, carry):
        row = pl.ds(z, 1)
        left, right = (
            jnp.take_along_axis(
                box[t, z, pl.ds(0, LANES, stride=2), :], pick, axis=1, mode="promise_in_bounds"
            )
            for t in range(2)
        )
        coarse = jnp.where(lane_w < LANES // 2, left, right)
        mid[z] = local[z] + coarse + uwide[...] * sums[0, row, :] + pwide[...] * sums[1, row, :]
        outer_r[z, 0:LANES, :] = jnp.where(plane_of == z, edge_h, 0.0).astype(BF16)
        outer_r[z, LANES:, :] = jnp.where(plane_of == z, edge_l, 0.0).astype(BF16)
        return carry

    lax.fori_loop(0, PLANES, x_part, 0, unroll=2)
    for copy in k_copies + x_copies + y_copies + c_copies:
        copy.wait_send()
    u_x, psi_x = packed[0], packed[1]
    forward, backward = gather(y_copies, yr, r, ny, nx)
    extra_f, extra_b = gather(c_copies, cr, r, ny, nx)
    forward = forward + u_x * extra_f[0:1, :] + psi_x * extra_f[1:2, :]
    backward = backward + u_x * extra_b[0:1, :] + psi_x * extra_b[1:2, :]
    lane = iota((LANES, LANES), 1)

    def spread(values):
        return jnp.concatenate(
            [pltpu.roll(values, (LANES - m * PLANES) % LANES, 1) if m else values for m in range(blocks)],
            axis=0,
        )

    both = jnp.where(lane < PLANES, spread(forward), pltpu.roll(spread(backward), PLANES, 1))
    high = both.astype(BF16).astype(F32)
    both = jnp.where(lane < 2 * PLANES, high, pltpu.roll(both - high, 2 * PLANES, 1))
    outer_l[:, 0:LANES] = both.astype(BF16)
    outer_l[:, LANES:] = both.astype(BF16)


def final_kernel(mid, outer_l, outer_r, out, total, sem):
    writes = []
    for g in range(PLANES // 8):
        planes = pl.ds(g * 8, 8)
        for k in range(g * 8, g * 8 + 8, 2):
            pair = jnp.concatenate([outer_r[k], outer_r[k + 1]], axis=1)
            update = mxu(outer_l[...], pair)
            total[k] = mid[k] + update[:, :LANES]
            total[k + 1] = mid[k + 1] + update[:, LANES:]
        writes.append(pltpu.make_async_copy(total.at[planes], out.at[planes], sem.at[g]))
        writes[-1].start()
    for write in writes:
        write.wait()


def per_device(nx, ny, density, spacing_x, spacing_y):
    blocks = nx + ny
    hbm = pl.BlockSpec(memory_space=pltpu.HBM)
    vmem = pl.BlockSpec(memory_space=pltpu.VMEM)
    f32 = lambda *shape: jax.ShapeDtypeStruct(shape, F32)
    bf16 = lambda *shape: jax.ShapeDtypeStruct(shape, BF16)
    sx = spacing_x.reshape(2 * nx, LANES)
    sy = spacing_y.reshape(2 * ny, LANES)
    colx, ycoef, scal, cf, cb, wcat, gxh, gxl, rh, er, lch, lcl, packed, box = pl.pallas_call(
        functools.partial(prepare_kernel, nx, ny),
        out_shape=(
            f32(LANES, LANES), f32(8, FINE), f32(8, LANES), f32(blocks, LANES), f32(blocks, LANES),
            bf16(FINE + LANES, FINE), bf16(LANES, LANES), bf16(LANES, LANES),
            f32(4, 2, PLANES, LANES), f32(LANES, LANES), bf16(LANES, LANES), bf16(LANES, LANES),
            f32(2, PLANES, LANES), f32(2, PLANES, FINE, LANES),
        ),
        in_specs=[hbm] * 3,
        out_specs=(vmem,) * 14,
        scratch_shapes=[
            pltpu.VMEM((2 * nx, LANES), F32),
            pltpu.VMEM((2 * ny, LANES), F32),
            pltpu.VMEM((3, 2, PLANES, LANES), F32),
            pltpu.VMEM((FINE // 2, LANES), F32),
            pltpu.VMEM((FINE // 4, LANES), F32),
            pltpu.VMEM((3, 2, PLANES, LANES), F32),
            pltpu.VMEM((FINE // 2, LANES), F32),
            pltpu.VMEM((FINE // 4, LANES), F32),
            pltpu.VMEM((6, 8, LANES), F32),
            pltpu.VMEM((14, blocks, LANES), F32),
            pltpu.VMEM((3, blocks, LANES), F32),
            pltpu.VMEM((LANES, LANES), F32),
            pltpu.VMEM((FINE, LANES), F32),
            pltpu.SemaphoreType.DMA((2 * PLANES // STEP + 2,)),
            pltpu.SemaphoreType.DMA((10,)),
            pltpu.SemaphoreType.DMA((10,)),
        ],
        compiler_params=pltpu.CompilerParams(
            collective_id=0, has_side_effects=True, vmem_limit_bytes=32 * MIB
        ),
        name="prepare",
    )(*(pltpu.with_memory_space_constraint(v, pltpu.HBM) for v in (density, sx, sy)))
    tables = (colx, ycoef, scal, rh, er, lch, lcl, wcat, gxh, gxl)
    detail, local = pl.pallas_call(
        main_kernel,
        out_shape=(f32(PLANES, FINE, FINE), f32(PLANES, LANES, LANES)),
        in_specs=[vmem] * (1 + len(tables)),
        out_specs=(hbm, vmem),
        scratch_shapes=[
            pltpu.VMEM((7, LANES, LANES), F32),
            pltpu.VMEM((PER, 2, LANES + 16, LANES), F32),
            pltpu.VMEM((PER, 2, LANES + 16, LANES), F32),
            pltpu.VMEM((PER, 2, LANES + 16, LANES), F32),
            pltpu.VMEM((2, PER, 2, FINE, LANES), F32),
            pltpu.VMEM((2, PER, LANES, FINE + LANES), BF16),
            pltpu.VMEM((2, PER, LANES, FINE + LANES), BF16),
            pltpu.SemaphoreType.DMA((2, 2)),
        ],
        compiler_params=pltpu.CompilerParams(vmem_limit_bytes=32 * MIB),
        name="main",
    )(box, *tables)
    mid, outer_l, outer_r = pl.pallas_call(
        functools.partial(exchange_kernel, nx, ny),
        out_shape=(f32(PLANES, LANES, LANES), bf16(LANES, FINE), bf16(PLANES, FINE, LANES)),
        in_specs=[vmem] * 7,
        out_specs=(vmem,) * 3,
        scratch_shapes=[
            pltpu.VMEM((2, PLANES, LANES), F32),
            pltpu.VMEM((nx - 1, PLANES, LANES), F32),
            pltpu.VMEM((2, PLANES, LANES), F32),
            pltpu.VMEM((ny - 1, PLANES, LANES), F32),
            pltpu.VMEM((2, 8, LANES), F32),
            pltpu.VMEM((ny - 1, 8, LANES), F32),
            pltpu.VMEM((2, 8, LANES), F32),
            pltpu.VMEM((nx - 1, 8, LANES), F32),
            pltpu.VMEM((2, PLANES, LANES), F32),
            pltpu.VMEM((LANES, LANES), F32),
            pltpu.VMEM((LANES, LANES), F32),
            pltpu.SemaphoreType.DMA((nx - 1,)),
            pltpu.SemaphoreType.DMA((nx - 1,)),
            pltpu.SemaphoreType.DMA((ny - 1,)),
            pltpu.SemaphoreType.DMA((ny - 1,)),
            pltpu.SemaphoreType.DMA((ny - 1,)),
            pltpu.SemaphoreType.DMA((ny - 1,)),
            pltpu.SemaphoreType.DMA((nx - 1,)),
            pltpu.SemaphoreType.DMA((nx - 1,)),
        ],
        compiler_params=pltpu.CompilerParams(
            collective_id=1, has_side_effects=True, vmem_limit_bytes=32 * MIB
        ),
        name="exchange",
    )(local, box, colx, scal, cf, cb, packed)
    coarse_new = pl.pallas_call(
        final_kernel,
        out_shape=f32(PLANES, LANES, LANES),
        in_specs=[vmem] * 3,
        out_specs=hbm,
        scratch_shapes=[pltpu.VMEM((PLANES, LANES, LANES), F32), pltpu.SemaphoreType.DMA((PLANES // 8,))],
        compiler_params=pltpu.CompilerParams(vmem_limit_bytes=16 * MIB),
        name="final",
    )(mid, outer_l, outer_r)
    return detail, coarse_new


def solution(mesh):
    placed = P(None, "gx", "gy")
    return jax.shard_map(
        functools.partial(per_device, mesh.shape["gx"], mesh.shape["gy"]),
        mesh=mesh,
        in_specs=(placed, P(), P()),
        out_specs=(placed, placed),
        check_vma=False,
    )
```
